32 devices in a mesh: gx: 8 (over z, y), pb: 4 (over x, core).
Axes of the slice: x: 2, y: 2, z: 4, core: 2. Of those that a mesh axis runs over, the one named last changes fastest.
Arguments:
- density: float32 [16, 128, 128], P('gx', 'pb'), may hold values from 0.5 to 2
- velocity: float32 [3, 16, 128, 128], P(None, 'gx', 'pb'), may hold values from -3 to 3
- magnetic: float32 [3, 16, 128, 128], P(None, 'gx', 'pb'), may hold values from -4 to 4
- pressure: float32 [16, 128, 128], P('gx', 'pb'), may hold values from 0.2 to 2
- line_owner: int32 [8, 4, 64, 1], P('gx', 'pb'), may hold values from 0 to 7; in each aligned block of 64 rows (0 to 63, 64 to 127, ..., all dimensions but the last counted through in order) at most 16 rows name the same one
- line_row: int32 [8, 4, 64], P('gx', 'pb'), may hold values from 0 to 7
- pedersen: float32 [256, 128], P(('gx', 'pb')), may hold values from 0.5 to 8
- hall: float32 [256, 128], P(('gx', 'pb')), may hold values from 0.3 to 5
- mirror_shift: int32 [256], P(('gx', 'pb')), may hold values from 0 to 127, as said below
Outputs:
- conserved: float32 [8, 16, 128, 128], P(None, 'gx', 'pb')
- potential: float32 [256, 128], P(('gx', 'pb'))
The draws below stay inside these ranges and needn't reach their ends.
Inputs may be any that keep to these rules, and one draw needn't show every extreme that they name: `line_owner`: among the rows of one device no owner index is named more than 16 times. `mirror_shift`: entry r + 128 equals (128 - entry r) mod 128 for every row r below 128.
All inputs are finite; a program needn't handle non-finite values.
Results may differ from the reference program's by a relative error of at most 0.0003.
Values sent between devices are 32-bit elements; how exact they have to be, the bound alone decides.
A program may use at most 64 MiB of HBM per device.

```python
import math
import jax
import jax.numpy as jnp
import numpy as np
from jax import lax

CX = 2
CY = 32
NZ = 128
RI = 8
SWEEPS = 8
NX = 16
NY = 128
ROWS_DEV = 64
CAP = 16
NLAT = 256
ILAT = 128
ILON = 128
N_GX = 8
N_PB = 4


def draw_mirror_shift(key, part):
    northern = jax.random.randint(key, (ILAT,), 0, ILON, dtype=jnp.int32)
    southern = (ILON - northern) % ILON
    return jnp.concatenate([northern, southern])


def with_ends(values, own_key, low, top_value):
    extent = values.shape
    place = [jax.random.randint(jax.random.fold_in(own_key, axis), (), 0, extent[axis]) for axis in range(len(extent))]
    values = values.at[tuple(place)].set(low)
    longest = extent.index(max(extent))
    place[longest] = (place[longest] + 1) % extent[longest]
    return values.at[tuple(place)].set(top_value)


def levels(stream_key, dims, shards, least, high):
    factor_of = 1.0
    for axis_at, shards_of in shards:
        heights = jax.random.uniform(jax.random.fold_in(jax.random.fold_in(stream_key, 6), axis_at), (shards_of,), jnp.float32, least / len(shards), high / len(shards))
        factor_of = factor_of * jnp.repeat(jnp.exp(heights), dims[axis_at] // shards_of).reshape((-1,) + (1,) * (len(dims) - 1 - axis_at))
    return factor_of


def routed_block(key, own, number, rows, count, top, limit, slope):
    ranking = jax.random.permutation(key, count)
    heavy_load, usual = load_shares(count, rows * top, limit, slope, True), load_shares(count, rows * top, limit, slope, False)
    places = jnp.arange(count)

    def named(sizes, turn):
        used = int((sizes > 0).sum())
        fixed = max(1, used // 4)
        shifted = fixed + (places - fixed + turn * (used - fixed)) % max(1, count - fixed)
        return jnp.zeros((count,), jnp.int32).at[ranking[jnp.where(places < fixed, places, shifted)]].set(jnp.asarray(sizes, jnp.int32))

    sizes = jnp.where(number % 4 == 0, named(heavy_load, number // 4), named(usual, number - number // 4 - 1))
    mixed = jax.random.permutation(jax.random.fold_in(own, 3), count)
    donor, sink = mixed[0:count // 2 * 2:2], mixed[1:count // 2 * 2:2]
    room = jnp.minimum(sizes[donor] - 1, limit - sizes[sink]) // 2
    room = jnp.where((donor == ranking[0]) | (sink == ranking[0]) | (sizes[sink] == 0), 0, jnp.maximum(room, 0))
    shifted = jax.random.randint(jax.random.fold_in(own, 4), (count // 2,), 0, 1 << 20) % (room + 1)
    sizes = sizes.at[donor].add(-shifted).at[sink].add(shifted)
    members = jnp.searchsorted(jnp.cumsum(sizes), jnp.arange(rows * top), side="right").astype(jnp.int32)
    table = members.reshape(top, rows).T
    table = table[jax.random.permutation(jax.random.fold_in(own, 1), rows)]
    turn = jax.random.randint(jax.random.fold_in(own, 2), (rows, 1), 0, top)
    return jnp.take_along_axis(table, (jnp.arange(top)[None, :] + turn) % top, axis=1)


def load_shares(count, total, limit, lean, full):
    weights = [(1 << 20) // math.isqrt(standing ** lean) + 1 for standing in range(1, count + 1)]
    largest = limit if full else min(limit, max(-(-total // count), total * weights[0] // sum(weights)))
    least = 1 if total - largest >= count - 1 else 0
    holding, surplus = [largest] + [least] * (count - 1), total - largest - least * (count - 1)
    while surplus > 0:
        movable = [i for i in range(1, count) if holding[i] < largest] or [i for i in range(1, count) if holding[i] < limit]
        mass, left = sum([weights[i] for i in movable]), surplus
        for i in movable:
            addition = min(limit - holding[i], max(1, left * weights[i] // mass), surplus)
            holding[i] = holding[i] + addition
            surplus = surplus - addition
    return np.array(holding)


def noise(key, extent, width, most, cuts=(), kind=jnp.bfloat16):
    array = jax.random.normal(key, extent, jnp.float32) * width
    if len(cuts) > 0:
        array = levels(key, extent, cuts, -0.22, 0.18) * array
    return jnp.clip(array, min=-most, max=most).astype(kind)


def setup_inputs(seed: int = 0) -> dict:
    key_list = jax.random.split(jax.random.key(seed), 10)
    density = jnp.clip(0.5 + 1.5 * jax.random.uniform(key_list[0], (NX, NY, NZ), jnp.float32) ** levels(key_list[0], (NX, NY, NZ), ((0, 8), (1, 4)), -0.2, 0.2), 0.5, 2.0)
    velocity = noise(key_list[1], (3, NX, NY, NZ), 0.5, 3.0, ((1, 8), (2, 4)), jnp.float32)
    magnetic = noise(key_list[2], (3, NX, NY, NZ), 0.7, 4.0, ((1, 8), (2, 4)), jnp.float32)
    pressure = jnp.clip(jnp.exp(math.log(2.0) - 2.3025851 * jax.random.uniform(key_list[3], (NX, NY, NZ), jnp.float32) ** levels(key_list[3], (NX, NY, NZ), ((0, 8), (1, 4)), -0.2, 0.2)), 0.2, 2.0)
    line_owner_keys = jax.random.split(jax.random.fold_in(key_list[4], 1), N_GX * N_PB * ROWS_DEV // ROWS_DEV)
    line_owner_turns = jax.random.permutation(jax.random.fold_in(key_list[4], 3), N_GX * N_PB * ROWS_DEV // ROWS_DEV)
    line_owner = jax.vmap(lambda own, number: routed_block(jax.random.fold_in(key_list[4], 2), own, number, ROWS_DEV, N_GX, 1, CAP, 2))(line_owner_keys, line_owner_turns).reshape((N_GX, N_PB, ROWS_DEV, 1))
    line_row = with_ends(jax.random.randint(key_list[5], (N_GX, N_PB, ROWS_DEV), 0, RI), jax.random.fold_in(key_list[5], 1), 0, RI - 1).astype(jnp.int32)
    pedersen = jnp.clip(jnp.exp(math.log(8.0) - 2.7725887 * jax.random.uniform(key_list[6], (NLAT, ILON), jnp.float32) ** levels(key_list[6], (NLAT, ILON), ((0, 32),), -0.2, 0.2)), 0.5, 8.0)
    hall = jnp.clip(jnp.exp(math.log(5.0) - 2.8134107 * jax.random.uniform(key_list[7], (NLAT, ILON), jnp.float32) ** levels(key_list[7], (NLAT, ILON), ((0, 32),), -0.2, 0.2)), 0.3, 5.0)
    mirror_shift = draw_mirror_shift(jax.random.fold_in(key_list[9], 71), 0)
    return dict(density=density, velocity=velocity, magnetic=magnetic, pressure=pressure, line_owner=line_owner, line_row=line_row, pedersen=pedersen, hall=hall, mirror_shift=mirror_shift)


GAMMA = 5.0 / 3.0
COURANT = 0.08

def spatial_slice(values, axis, start, stop):
    return lax.slice_in_dim(values, start, stop, axis=values.ndim - 3 + axis)

def conserved_of(density, velocity, magnetic, pressure):
    field_sq = lax.optimization_barrier(jnp.sum(magnetic * magnetic, axis=0))
    energy = pressure / (GAMMA - 1.0) + 0.5 * density * lax.optimization_barrier(jnp.sum(velocity * velocity, axis=0)) + 0.5 * field_sq
    return jnp.concatenate([density[None], density * velocity, magnetic, energy[None]], axis=0)

def direction_flux(density, velocity, magnetic, pressure, d):
    normal_v = velocity[d]
    normal_b = magnetic[d]
    field_sq = lax.optimization_barrier(jnp.sum(magnetic * magnetic, axis=0))
    total_p = pressure + 0.5 * field_sq
    energy = pressure / (GAMMA - 1.0) + 0.5 * density * lax.optimization_barrier(jnp.sum(velocity * velocity, axis=0)) + 0.5 * field_sq
    normal_unit = (jnp.arange(3) == d).astype(jnp.float32)[:, None, None, None]
    momentum = density * velocity * normal_v - magnetic * normal_b + normal_unit * total_p
    induced = magnetic * normal_v - normal_b * velocity
    v_dot_b = lax.optimization_barrier(jnp.sum(velocity * magnetic, axis=0))
    fluxes = jnp.concatenate([(density * normal_v)[None], momentum, induced, ((energy + total_p) * normal_v - normal_b * v_dot_b)[None]], axis=0)
    sound_sq = GAMMA * pressure / density
    alfven = field_sq / density
    spread = (sound_sq + alfven) ** 2 - 4.0 * sound_sq * normal_b * normal_b / density
    fast_speed = jnp.sqrt(0.5 * (sound_sq + alfven + jnp.sqrt(jnp.maximum(spread, 0.0))))
    return (fluxes, jnp.abs(normal_v) + fast_speed)

def advance(density, velocity, magnetic, pressure):
    conserved_state = conserved_of(density, velocity, magnetic, pressure)
    change = jnp.zeros_like(conserved_state[:, 1:-1, 1:-1, 1:-1])
    for d in range(3):
        fluxes, speeds = direction_flux(density, velocity, magnetic, pressure, d)
        n = density.shape[d]
        lower_flux = spatial_slice(fluxes, d, 0, n - 1)
        upper_flux = spatial_slice(fluxes, d, 1, n)
        lower_state = spatial_slice(conserved_state, d, 0, n - 1)
        upper_state = spatial_slice(conserved_state, d, 1, n)
        largest = jnp.maximum(spatial_slice(speeds, d, 0, n - 1), spatial_slice(speeds, d, 1, n))
        interface = 0.5 * (lower_flux + upper_flux) - 0.5 * largest * (upper_state - lower_state)
        divergence = spatial_slice(interface, d, 1, n - 1) - spatial_slice(interface, d, 0, n - 2)
        for e in range(3):
            if e != d:
                divergence = spatial_slice(divergence, e, 1, density.shape[e] - 1)
        change = change + divergence
    interior = conserved_state[:, 1:-1, 1:-1, 1:-1]
    return interior - COURANT * change

def derivative(values, axis):
    n = values.shape[axis]
    result = (lax.slice_in_dim(values, 2, n, axis=axis) - lax.slice_in_dim(values, 0, n - 2, axis=axis)) * 0.5
    for e in range(3):
        if e != axis:
            result = lax.slice_in_dim(result, 1, result.shape[e] - 1, axis=e)
    return result

def aligned_current(field_pad):
    field_x, field_y, field_z = (field_pad[0], field_pad[1], field_pad[2])
    current_x = derivative(field_z, 1) - derivative(field_y, 2)
    current_y = derivative(field_x, 2) - derivative(field_z, 0)
    current_z = derivative(field_y, 0) - derivative(field_x, 1)
    interior = field_pad[:, 1:-1, 1:-1, 1:-1]
    field_size = jnp.sqrt(lax.optimization_barrier(jnp.sum(interior * interior, axis=0)))
    along = current_x * interior[0] + current_y * interior[1] + current_z * interior[2]
    return along / jnp.maximum(field_size, 1.0)

def weights(pedersen_pad, hall_pad):
    pedersen = pedersen_pad[..., 1:-1, :]
    hall = hall_pad[..., 1:-1, :]
    up_ped = pedersen_pad[..., :-2, :]
    down_ped = pedersen_pad[..., 2:, :]
    up_hall = hall_pad[..., :-2, :]
    down_hall = hall_pad[..., 2:, :]
    up_weight = 0.5 * (pedersen + up_ped)
    down_weight = 0.5 * (pedersen + down_ped)
    east_weight = 0.5 * (pedersen + jnp.roll(pedersen, -1, axis=-1))
    west_weight = 0.5 * (pedersen + jnp.roll(pedersen, 1, axis=-1))
    up_east = 0.125 * (hall + jnp.roll(up_hall, -1, axis=-1))
    up_west = 0.125 * (hall + jnp.roll(up_hall, 1, axis=-1))
    down_east = 0.125 * (hall + jnp.roll(down_hall, -1, axis=-1))
    down_west = 0.125 * (hall + jnp.roll(down_hall, 1, axis=-1))
    center = up_weight + down_weight + east_weight + west_weight + up_east + up_west + down_east + down_west
    return (up_weight, down_weight, east_weight, west_weight, up_east, -up_west, -down_east, down_west, center)

def sweep(potential_pad, stencil, sources):
    up_weight, down_weight, east_weight, west_weight, up_east, up_west, down_east, down_west, center = stencil
    middle = potential_pad[..., 1:-1, :]
    upper = potential_pad[..., :-2, :]
    lower = potential_pad[..., 2:, :]
    summed = up_weight * upper + down_weight * lower
    summed = summed + east_weight * jnp.roll(middle, -1, axis=-1) + west_weight * jnp.roll(middle, 1, axis=-1)
    summed = summed + up_east * jnp.roll(upper, -1, axis=-1) + up_west * jnp.roll(upper, 1, axis=-1)
    summed = summed + down_east * jnp.roll(lower, -1, axis=-1) + down_west * jnp.roll(lower, 1, axis=-1)
    return (summed + sources) / center

def couple(local_phi, partner_phi, local_ped, partner_ped, shifts):
    n = local_phi.shape[-1]
    columns = (jnp.arange(n, dtype=jnp.int32)[None, :] + shifts[:, None]) % n
    mirrored = jnp.take_along_axis(partner_phi, columns, axis=-1)
    mirrored_ped = jnp.take_along_axis(partner_ped, columns, axis=-1)
    return (local_ped * local_phi + mirrored_ped * mirrored) / (local_ped + mirrored_ped)

def pad_edge(values):
    widths = [(0, 0)] * (values.ndim - 3) + [(1, 1)] * 3
    return jnp.pad(values, widths, mode='edge')

def reference(density, velocity, magnetic, pressure, line_owner, line_row, pedersen, hall, mirror_shift):
    density_pad = pad_edge(density)
    velocity_pad = pad_edge(velocity)
    magnetic_pad = pad_edge(magnetic)
    pressure_pad = pad_edge(pressure)

    def advance_plane(i):

        def window(values):
            return lax.dynamic_slice_in_dim(values, i, 3, axis=values.ndim - 3)
        return advance(window(density_pad), window(velocity_pad), window(magnetic_pad), window(pressure_pad))[:, 0]
    planes = lax.map(advance_plane, jnp.arange(NX, dtype=jnp.int32))
    updated = jnp.transpose(planes, (1, 0, 2, 3))
    current = aligned_current(pad_edge(updated[4:7]))
    current_rows = current.reshape(N_GX, CX, N_PB, CY, NZ).transpose(0, 2, 1, 3, 4).reshape(N_GX, N_PB, CX * CY, NZ)
    band_index = jnp.arange(N_PB, dtype=jnp.int32)[None, :, None]
    target = (line_owner[..., 0] * N_PB + band_index) * RI + line_row
    sources = jax.ops.segment_sum(current_rows.reshape(-1, NZ), target.reshape(-1), num_segments=NLAT)
    quarter = ILAT // 2

    def split_halves(values):
        return jnp.roll(values, quarter, axis=0).reshape((2, ILAT) + values.shape[1:])

    def zero_pad(values):
        return jnp.pad(values, ((0, 0), (1, 1), (0, 0)))
    pedersen_two = split_halves(pedersen)
    stencil = weights(zero_pad(pedersen_two), zero_pad(split_halves(hall)))
    sources_two = split_halves(sources)
    shifts = split_halves(mirror_shift)
    potential = jnp.zeros((2, ILAT, ILON), jnp.float32)
    for repeat in range(SWEEPS):
        potential = sweep(zero_pad(potential), stencil, sources_two)
        northern = couple(potential[0], potential[1], pedersen_two[0], pedersen_two[1], shifts[0])
        southern = couple(potential[1], potential[0], pedersen_two[1], pedersen_two[0], shifts[1])
        potential = jnp.stack([northern, southern])
    return (updated, jnp.roll(potential.reshape(NLAT, ILON), -quarter, axis=0))
```

```python
import functools

import jax
import jax.numpy as jnp
from jax import lax
from jax.experimental import pallas as pl
from jax.experimental.pallas import tpu as pltpu
from jax.sharding import PartitionSpec as P

SWEEPS = 8
GAMMA = 5.0 / 3.0
COURANT = 0.08
PAD = 8
COEFS = 11
F32 = jnp.float32
BF16 = jnp.bfloat16
MESH = pl.DeviceIdType.MESH
ORDER = (0, 2, 3, 4, 5, 6, 7, 1)


def cell_terms(prim):
    rho, vel, mag, pres = prim[0], prim[1:4], prim[4:7], prim[7]
    field_sq = mag[0] * mag[0] + mag[1] * mag[1] + mag[2] * mag[2]
    vel_sq = vel[0] * vel[0] + vel[1] * vel[1] + vel[2] * vel[2]
    half_sq = 0.5 * field_sq
    energy = pres * (1.0 / (GAMMA - 1.0)) + 0.5 * rho * vel_sq + half_sq
    total_p = pres + half_sq
    v_dot_b = vel[0] * mag[0] + vel[1] * mag[1] + vel[2] * mag[2]
    inv = 1.0 / rho
    sound_sq = GAMMA * pres * inv
    both = sound_sq + field_sq * inv
    momentum = [rho * v for v in vel]
    state = [rho] + momentum + list(mag) + [energy]
    return state, total_p, v_dot_b, sound_sq * inv, both


def flux_of(prim, terms, d):
    state, total_p, v_dot_b = terms[:3]
    vel, mag = prim[1:4], prim[4:7]
    vn, bn = vel[d], mag[d]
    flux = [state[1 + d]]
    for e in range(3):
        m = state[1 + e] * vn - mag[e] * bn
        flux.append(m + total_p if e == d else m)
    for e in range(3):
        flux.append(None if e == d else mag[e] * vn - bn * vel[e])
    flux.append((state[7] + total_p) * vn - bn * v_dot_b)
    return flux


def speed_of(prim, terms, d):
    sound_over, both = terms[3:]
    vn, bn = prim[1 + d], prim[4 + d]
    spread = both * both - 4.0 * sound_over * bn * bn
    fast = jnp.sqrt(0.5 * (both + jnp.sqrt(jnp.maximum(spread, 0.0))))
    return jnp.abs(vn) + fast


def face(f_lo, f_hi, u_lo, u_hi, largest):
    jump = largest * (u_hi - u_lo)
    return -0.5 * jump if f_lo is None else 0.5 * ((f_lo + f_hi) - jump)


def roll(values, shift, axis):
    return pltpu.roll(values, shift % values.shape[axis], axis)


def east(a):
    return roll(a, -1, 1)


def west(a):
    return roll(a, 1, 1)


def up(a):
    return roll(a, 1, 0)


def down(a):
    return roll(a, -1, 0)


def swap_by(cols, a):
    h = a.shape[0] // 2
    other = jnp.concatenate([a[h:], a[:h]], axis=0)
    return jnp.take_along_axis(other, cols, axis=1)


def flux_kernel(sizes, rho, vel, mag, pres, owner, line_row, ped, hall, shift,
                out, src_out, coef_out, cols_out,
                win, fwin, pstage, pin, part, part_in, cwin, own_v, row_v, shift_s,
                loc_sem, xs, xr, ls, lr, ys, yr, ds, dr, ps, pr, cs, cr, as_, ar):
    nx, ny = sizes
    cx, cy, nz = rho.shape
    ri = ped.shape[0]
    g, p = lax.axis_index("gx"), lax.axis_index("pb")
    n = nx * ny
    half = n // 2
    pairs = nx // 2
    b = g * ny + p
    wide = cy + 2 * PAD

    def dev(flat):
        return (flat // ny, flat % ny)

    barrier = pltpu.get_barrier_semaphore()

    def greet_columns(k, carry):
        for o in (-1, 0, 1):
            def signal(k=k, o=o):
                pl.semaphore_signal(
                    barrier, inc=1, device_id=((g + k) % nx, (p + o) % ny), device_id_type=MESH)
            if o:
                signal()
            else:
                pl.when(k > 0)(signal)
        return carry

    lax.fori_loop(0, nx, greet_columns, 0)

    rows = pl.ds(PAD, cy)
    mid = pl.ds(1, cx)
    loads = [
        (rho, win.at[0, mid, rows]), (vel, win.at[pl.ds(2, 3), mid, rows]),
        (mag, win.at[pl.ds(5, 3), mid, rows]), (pres, win.at[1, mid, rows]),
        (ped, cwin.at[1, 0]), (hall, cwin.at[1, 1]), (shift, shift_s),
        (owner, own_v), (line_row, row_v)]
    loads = [pltpu.make_async_copy(s, d, loc_sem.at[i]) for i, (s, d) in enumerate(loads)]
    for c in loads:
        c.start()
    for c in loads:
        c.wait()

    row8 = lax.broadcasted_iota(jnp.int32, (ri, nz), 0)
    sh = jnp.zeros((ri, nz), F32)
    for i in range(ri):
        sh = jnp.where(row8 == i, shift_s[i].astype(F32), sh)
    cwin[1, 2] = sh

    lane = lax.broadcasted_iota(jnp.int32, (cx, cy, nz), 2)
    first, last = lane == 0, lane == nz - 1

    def z_dn(a):
        return jnp.where(first[:, :a.shape[1]], a, roll(a, 1, 2))

    def z_change(u, f, largest):
        low = face(None if f is None else z_dn(f), f, z_dn(u), u, largest)
        top = jnp.zeros_like(u) if f is None else f
        high = jnp.where(last[:, :u.shape[1]], top, roll(low, -1, 2))
        return high - low

    prim = [win[v, 1:1 + cx, PAD:PAD + cy, :] for v in ORDER]
    terms = cell_terms(prim)
    win[8, 1:1 + cx, PAD:PAD + cy, :] = speed_of(prim, terms, 0)
    flux, speed = flux_of(prim, terms, 2), speed_of(prim, terms, 2)
    largest = jnp.maximum(speed, z_dn(speed))
    for v in range(8):
        out[v] = terms[0][v] - COURANT * z_change(terms[0][v], flux[v], largest)

    pl.semaphore_wait(barrier, 3 * nx - 1)

    def remote(src, dst, send, recv, where):
        return pltpu.make_async_remote_copy(
            src_ref=src, dst_ref=dst, send_sem=send, recv_sem=recv,
            device_id=where, device_id_type=MESH)

    g_up, g_dn = jnp.minimum(g + 1, nx - 1), jnp.maximum(g - 1, 0)
    p_up, p_dn = jnp.minimum(p + 1, ny - 1), jnp.maximum(p - 1, 0)
    has_xu, has_xd, has_yu, has_yd = g < nx - 1, g > 0, p < ny - 1, p > 0

    def each(cond, copies, act):
        @pl.when(cond)
        def _():
            for c in copies:
                getattr(c, act)()

    def x_pair(at, count, send, recv):
        return [
            remote(win.at[pl.ds(at, count), s, rows], win.at[pl.ds(at, count), d, rows],
                   send.at[way], recv.at[way], (where, p))
            for way, (s, d, where) in enumerate(((cx, 0, g_up), (1, cx + 1, g_dn)))]

    xc = x_pair(2, 7, xs, xr)
    xlate = x_pair(0, 2, ls, lr)
    yc = [
        remote(win.at[pl.ds(0, 8), mid, pl.ds(s, PAD)], win.at[pl.ds(0, 8), mid, pl.ds(d, PAD)],
               ys.at[way], yr.at[way], (g, where))
        for way, (s, d, where) in enumerate(((cy, 0, p_up), (PAD, PAD + cy, p_dn)))]
    diag = []
    for i, (xu, yu) in enumerate(((1, 1), (1, 0), (0, 1), (0, 0))):
        s_x, d_x, to_g = (cx, 0, g_up) if xu else (1, cx + 1, g_dn)
        s_y, d_y, to_p = (PAD + cy - 1, PAD - 1, p_up) if yu else (PAD, PAD + cy, p_dn)
        c = remote(win.at[pl.ds(0, 8), s_x, pl.ds(s_y, 1)], win.at[pl.ds(0, 8), d_x, pl.ds(d_y, 1)],
                   ds.at[i], dr.at[i], (to_g, to_p))
        to = (has_xu if xu else has_xd) & (has_yu if yu else has_yd)
        come = (has_xd if xu else has_xu) & (has_yd if yu else has_yu)
        diag.append((c, to, come))
    ion = [
        ((b + 1) % n, 0),
        ((b + n - 1) % n, 2),
        ((b + half + 1) % n, 3),
        ((b + half) % n, 4),
        ((b + half + n - 1) % n, 5),
    ]
    cond_copies = [
        remote(cwin.at[1], cwin.at[slot], cs.at[slot], cr.at[slot], dev(flat)) for flat, slot in ion]

    each(has_yu, yc[:1], "start")
    each(has_yd, yc[1:], "start")
    for c, to, _ in diag:
        each(to, [c], "start")
    each(has_xu, xc[:1], "start")
    each(has_xd, xc[1:], "start")
    for c in cond_copies:
        c.start()

    each(has_yd, yc[:1], "wait_recv")
    each(has_yu, yc[1:], "wait_recv")

    @pl.when(p == 0)
    def _():
        for v in range(8):
            win[v, 1:1 + cx, PAD - 1:PAD, :] = win[v, 1:1 + cx, PAD:PAD + 1, :]

    @pl.when(p == ny - 1)
    def _():
        for v in range(8):
            win[v, 1:1 + cx, PAD + cy:PAD + cy + 1, :] = win[v, 1:1 + cx, PAD + cy - 1:PAD + cy, :]

    def x_inner(values, u, f):
        if cx == 1:
            return values
        speed = win[8, 1:1 + cx, PAD:PAD + cy, :]
        lows = face(None if f is None else f[:-1], None if f is None else f[1:], u[:-1], u[1:],
                    jnp.maximum(speed[:-1], speed[1:]))
        none = jnp.zeros_like(lows[:1])
        return values - COURANT * (jnp.concatenate([lows, none], 0) - jnp.concatenate([none, lows], 0))

    prim = [win[v, 1:1 + cx] for v in ORDER]
    terms = cell_terms(prim)
    flux, speed = flux_of(prim, terms, 1), speed_of(prim, terms, 1)
    largest = jnp.maximum(speed, roll(speed, 1, 1))

    def y_change(v):
        u, f = terms[0][v], flux[v]
        low = face(None if f is None else roll(f, 1, 1), f, roll(u, 1, 1), u, largest)
        return roll(low, -1, 1) - low

    def ends(a):
        return jnp.concatenate([a[:, :PAD], a[:, PAD + cy:]], axis=1)

    side = {}
    for v in (5, 6, 4):
        diff = y_change(v)
        if v != 5:
            side[v] = ends(diff)
        u = win[v + 1, 1:1 + cx, PAD:PAD + cy, :]
        f = None
        if v != 4:
            f = u * win[2, 1:1 + cx, PAD:PAD + cy, :] - (
                win[5, 1:1 + cx, PAD:PAD + cy, :] * win[v - 2, 1:1 + cx, PAD:PAD + cy, :])
        done = x_inner(out[v] - COURANT * diff[:, PAD:PAD + cy, :], u, f)
        if v == 4:
            out[v] = done
        else:
            pstage[v - 5] = done
        if v == 6:
            pc = [
                remote(pstage.at[:, s], pin.at[way], ps.at[way], pr.at[way], (where, p))
                for way, (s, where) in enumerate(((cx - 1, g_up), (0, g_dn)))]
            each(has_xu, pc[:1], "start")
            each(has_xd, pc[1:], "start")
    for v in (0, 1, 2, 3, 7):
        out[v] = out[v] - COURANT * y_change(v)[:, PAD:PAD + cy, :]

    for c, _, come in diag:
        each(come, [c], "wait_recv")

    def edge_planes(which, at, count):
        at = pl.ds(at, count)

        @pl.when(g == 0)
        def _():
            for v in which:
                win[v, 0, at, :] = win[v, 1, at, :]

        @pl.when(g == nx - 1)
        def _():
            for v in which:
                win[v, cx + 1, at, :] = win[v, cx, at, :]

    edge_planes(range(8), 0, PAD)
    edge_planes(range(8), PAD + cy, PAD)
    prim = [jnp.concatenate([win[v, :, :PAD, :], win[v, :, PAD + cy:, :]], axis=1) for v in ORDER]
    terms = cell_terms(prim)
    own = [a[1:1 + cx] for a in prim]
    speed_z = speed_of(own, (None, None, None, terms[3][1:1 + cx], terms[4][1:1 + cx]), 2)
    largest_z = jnp.maximum(speed_z, z_dn(speed_z))
    speed_x = speed_of(prim, terms, 0)
    largest_x = jnp.maximum(speed_x[:-1], speed_x[1:])
    for v in (4, 6):
        u = prim[v]
        fz = None if v == 6 else own[v] * own[3] - own[6] * own[v - 3]
        fx = None if v == 4 else u * prim[1] - prim[4] * prim[v - 3]
        lows = face(None if fx is None else fx[:-1], None if fx is None else fx[1:], u[:-1], u[1:], largest_x)
        new = own[v] - COURANT * (z_change(own[v], fz, largest_z) + side[v] + (lows[1:] - lows[:-1]))
        fwin[v // 6, :, 0:PAD, :] = new[:, :PAD]
        fwin[v // 6, :, PAD + cy:, :] = new[:, PAD:]

    each(has_xd, xc[:1], "wait_recv")
    each(has_xu, xc[1:], "wait_recv")
    edge_planes(range(2, 9), PAD, cy)

    def outer_faces(v, f_of):
        faces = []
        for lo in (0, cx):
            u = [win[v + 1, lo + i, PAD:PAD + cy, :] for i in range(2)]
            f = [f_of(v, lo + i) for i in range(2)]
            most = jnp.maximum(win[8, lo, PAD:PAD + cy, :], win[8, lo + 1, PAD:PAD + cy, :])
            faces.append(COURANT * face(f[0], f[1], u[0], u[1], most))
        return faces

    def b_flux(v, at):
        if v == 4:
            return None
        q = [win[i, at, PAD:PAD + cy, :] for i in (v + 1, 2, 5, v - 2)]
        return q[0] * q[1] - q[2] * q[3]

    def close(values, faces):
        planes = [values[i] for i in range(cx)]
        planes[0] = planes[0] + faces[0]
        planes[-1] = planes[-1] - faces[1]
        return planes

    field, outer = {}, {}
    for v in (4, 6, 5):
        outer[v] = outer_faces(v, b_flux)
        field[v] = close(out[v] if v == 4 else pstage[v - 5], outer[v])
        for i in range(cx):
            out[v, i] = field[v][i]
            if v != 5:
                fwin[v // 6, i, PAD:PAD + cy, :] = field[v][i]

    @pl.when(p == 0)
    def _():
        fwin[:, :, PAD - 1:PAD, :] = fwin[:, :, PAD:PAD + 1, :]

    @pl.when(p == ny - 1)
    def _():
        fwin[:, :, PAD + cy:PAD + cy + 1, :] = fwin[:, :, PAD + cy - 1:PAD + cy, :]

    def d_y(v):
        a = fwin[v // 6]
        return 0.5 * (roll(a, -1, 1) - roll(a, 1, 1))[:, PAD:PAD + cy, :]

    def d_z(a):
        return 0.5 * (jnp.where(last, a, roll(a, -1, 2)) - z_dn(a))

    bx, by, bz = [jnp.stack(field[v]) for v in (4, 5, 6)]
    jx = d_y(6) - d_z(by)
    size = jnp.sqrt(bx * bx + by * by + bz * bz)
    dzx, dyx = d_z(bx), d_y(4)

    each(has_xd, pc[:1], "wait_recv")
    each(has_xu, pc[1:], "wait_recv")

    def d_x(v):
        lo = jnp.where(g == 0, field[v][0], pin[0, v - 5] - outer[v][0])
        hi = jnp.where(g == nx - 1, field[v][-1], pin[1, v - 5] + outer[v][1])
        a = jnp.stack([lo] + field[v] + [hi])
        return 0.5 * (a[2:] - a[:-2])

    jy = dzx - d_x(6)
    jz = d_x(5) - dyx
    current = (jx * bx + jy * by + jz * bz) / jnp.maximum(size, 1.0)
    current = current.reshape(cx * cy, nz)

    key = own_v[0] * ri + row_v[...]
    at = lax.broadcasted_iota(jnp.int32, (nx * ri, cx * cy), 0)
    pair, rest = at // (2 * ri), at % (2 * ri)
    hot = (key == (pair + (rest // ri) * pairs) * ri + rest % ri).astype(BF16)
    head = current.astype(BF16)
    tail = current - head.astype(F32)
    body_ = tail.astype(BF16)
    tail = (tail - body_.astype(F32)).astype(BF16)
    sums = jnp.dot(jnp.concatenate([hot, hot, hot], axis=1), jnp.concatenate([head, body_, tail], axis=0),
                   preferred_element_type=F32)
    part[...] = sums.reshape(pairs, 2, ri, nz)

    def part_copy(o, to):
        return remote(part.at[to % pairs], part_in.at[o + 1, g], as_.at[o + 1], ar.at[o + 1],
                      dev((to * ny + p - o + n) % n))

    def send(k, carry):
        to = (g + k) % nx
        for o in (-1, 0, 1):
            if o:
                part_copy(o, to).start()
            else:
                pl.when(k > 0)(lambda: part_copy(0, to).start())
        return carry

    lax.fori_loop(0, nx, send, 0, unroll=nx <= 8)
    each(has_xu, xlate[:1], "start")
    each(has_xd, xlate[1:], "start")

    for c in cond_copies:
        c.wait_recv()
    lines = 6 * ri
    row = lax.broadcasted_iota(jnp.int32, (lines, nz), 0)
    row = jnp.where(row >= 3 * ri, row - 3 * ri, row)
    place = b % half
    low_row = jnp.where(place == half // 2, ri, 0)
    high_row = jnp.where(place == half // 2 - 1, 2 * ri, 3 * ri)
    valid = (row >= low_row) & (row < high_row)
    pw = jnp.where(valid, cwin[:, 0].reshape(lines, nz), 0.0)
    hw = jnp.where(valid, cwin[:, 1].reshape(lines, nz), 0.0)
    own_shift = cwin[0:3, 2].reshape(3 * ri, nz).astype(jnp.int32)
    col = lax.broadcasted_iota(jnp.int32, (3 * ri, nz), 1)
    cols = jnp.concatenate(
        [(col + own_shift) % nz, (col + (nz - own_shift)) % nz], axis=0)
    he, hwst = east(hw), west(hw)
    coef = [
        0.5 * (pw + up(pw)), 0.5 * (pw + down(pw)),
        0.5 * (pw + east(pw)), 0.5 * (pw + west(pw)),
        0.125 * (hw + up(he)), 0.125 * (hw + up(hwst)),
        0.125 * (hw + down(he)), 0.125 * (hw + down(hwst)),
    ]
    center = coef[0]
    for c in coef[1:]:
        center = center + c
    inv = jnp.where(valid, 1.0 / jnp.where(valid, center, 1.0), 0.0)
    pm = swap_by(cols, pw)
    both = jnp.where(valid, pw + pm, 1.0)
    for i, c in enumerate(coef):
        coef_out[i] = c * inv
    coef_out[8] = inv
    coef_out[9] = jnp.where(valid, pw / both, 0.0)
    coef_out[10] = jnp.where(valid, pm / both, 0.0)
    cols_out[...] = cols

    def planes(v):
        return win[v, :, PAD:PAD + cy, :]

    each(has_xd, xlate[:1], "wait_recv")
    each(has_xu, xlate[1:], "wait_recv")
    edge_planes((0, 1), PAD, cy)
    prim = [planes(v) for v in ORDER]
    terms = cell_terms(prim)
    flux = flux_of(prim, terms, 0)
    speed = planes(8)
    largest = jnp.maximum(speed[:-1], speed[1:])
    for v in (0, 1, 2, 3, 7):
        u, f = terms[0][v], flux[v]
        lows = face(f[:-1], f[1:], u[:-1], u[1:], largest)
        out[v] = out[v] - COURANT * (lows[1:] - lows[:-1])

    for o in (-1, 0, 1):
        some = pl.ds(0, nx if o else nx - 1)
        pltpu.make_async_copy(part_in.at[o + 1, some], part_in.at[o + 1, some], ar.at[o + 1]).wait()
    part_in[1, g] = part[g % pairs]
    for o in (-1, 0, 1):
        def add(s, total, o=o):
            return total + part_in[o + 1, s]
        total = lax.fori_loop(1, nx, add, part_in[o + 1, 0], unroll=nx <= 8)
        northern = (b + o + n) % n < half
        src_out[0, o + 1] = jnp.where(northern, total[0], total[1])
        src_out[1, o + 1] = jnp.where(northern, total[1], total[0])

    each(has_xu, [xc[0], xlate[0], pc[0]], "wait_send")
    each(has_xd, [xc[1], xlate[1], pc[1]], "wait_send")
    each(has_yu, yc[:1], "wait_send")
    each(has_yd, yc[1:], "wait_send")
    for c, to, _ in diag:
        each(to, [c], "wait_send")
    for c in cond_copies:
        c.wait_send()
    for o in (-1, 0, 1):
        some = pl.ds(0, nx if o else nx - 1)
        pltpu.make_async_copy(part_in.at[o + 1, some], part_in.at[o + 1, some], as_.at[o + 1]).wait()


def sweep_kernel(con, src, coef, cols_ref, out, phi_out, phi_v, sems):
    write = pltpu.make_async_copy(con, out, sems.at[0])
    write.start()
    cu, cd, ce, cw, cue, cuw, cde, cdw, inv, wa, wb = [coef[i] for i in range(COEFS)]
    cols = cols_ref[...]
    ri = phi_v.shape[0]
    source = src[...].reshape(inv.shape) * inv

    def couple(phi):
        return wa * phi + wb * swap_by(cols, phi)

    phi = couple(source)
    for _ in range(SWEEPS - 1):
        e, w = east(phi), west(phi)
        acc = source + ce * e + cw * w
        acc = acc + up_terms(phi, e, w, cu, cue, cuw, up)
        acc = acc + up_terms(phi, e, w, cd, -cde, -cdw, down)
        phi = couple(acc)
    phi_v[...] = phi[ri:2 * ri]
    last = pltpu.make_async_copy(phi_v, phi_out, sems.at[1])
    last.start()
    write.wait()
    last.wait()


def up_terms(phi, e, w, straight, plus, minus, move):
    return straight * move(phi) + plus * move(e) - minus * move(w)


def body(sizes, density, velocity, magnetic, pressure, line_owner, line_row, pedersen, hall, mirror_shift):
    cx, cy, nz = density.shape
    ri = pedersen.shape[0]
    nx = sizes[0]
    any_ = pl.BlockSpec(memory_space=pl.ANY)
    vmem = pl.BlockSpec(memory_space=pltpu.VMEM)
    dma = pltpu.SemaphoreType.DMA
    con, src, coef, cols = pl.pallas_call(
        functools.partial(flux_kernel, sizes),
        out_shape=(
            pltpu.VMEM((8, cx, cy, nz), F32),
            pltpu.VMEM((2, 3, ri, nz), F32),
            pltpu.VMEM((COEFS, 6 * ri, nz), F32),
            pltpu.VMEM((6 * ri, nz), jnp.int32),
        ),
        in_specs=[any_] * 9,
        out_specs=(vmem,) * 4,
        scratch_shapes=[
            pltpu.VMEM((9, cx + 2, cy + 2 * PAD, nz), F32),
            pltpu.VMEM((2, cx, cy + 2 * PAD, nz), F32),
            pltpu.VMEM((2, cx, cy, nz), F32),
            pltpu.VMEM((2, 2, cy, nz), F32),
            pltpu.VMEM((nx // 2, 2, ri, nz), F32),
            pltpu.VMEM((3, nx, 2, ri, nz), F32),
            pltpu.VMEM((6, 3, ri, nz), F32),
            pltpu.VMEM((1, 1, cx * cy), jnp.int32),
            pltpu.VMEM((1, cx * cy), jnp.int32),
            pltpu.SMEM((ri,), jnp.int32),
            dma((9,)),
            dma((2,)), dma((2,)), dma((2,)), dma((2,)), dma((2,)), dma((2,)),
            dma((4,)), dma((4,)), dma((2,)), dma((2,)), dma((6,)), dma((6,)),
            dma((3,)), dma((3,)),
        ],
        compiler_params=pltpu.CompilerParams(collective_id=0, has_side_effects=True),
        name="flux_and_sources",
    )(density, velocity, magnetic, pressure, line_owner.reshape(1, 1, cx * cy), line_row.reshape(1, cx * cy),
      pedersen, hall, mirror_shift)
    return pl.pallas_call(
        sweep_kernel,
        out_shape=(
            jax.ShapeDtypeStruct((8, cx, cy, nz), F32),
            jax.ShapeDtypeStruct((ri, nz), F32),
        ),
        in_specs=[vmem] * 4,
        out_specs=(any_, any_),
        scratch_shapes=[pltpu.VMEM((ri, nz), F32), dma((2,))],
        name="sweeps",
    )(*[pltpu.with_memory_space_constraint(a, pltpu.VMEM) for a in (con, src, coef, cols)])


def solution(mesh):
    sizes = (mesh.shape["gx"], mesh.shape["pb"])
    in_specs = (
        P("gx", "pb", None),
        P(None, "gx", "pb", None),
        P(None, "gx", "pb", None),
        P("gx", "pb", None),
        P("gx", "pb", None, None),
        P("gx", "pb", None),
        P(("gx", "pb"), None),
        P(("gx", "pb"), None),
        P(("gx", "pb")),
    )
    out_specs = (P(None, "gx", "pb", None), P(("gx", "pb"), None))
    return jax.shard_map(
        functools.partial(body, sizes), mesh=mesh, in_specs=in_specs, out_specs=out_specs,
        check_vma=False)
```

```python
import functools

import jax
import jax.numpy as jnp
from jax import lax
from jax.experimental import pallas as pl
from jax.experimental.pallas import tpu as pltpu
from jax.sharding import PartitionSpec as P

SWEEPS = 8
GAMMA = 5.0 / 3.0
COURANT = 0.08
PAD = 8
COEFS = 11
F32 = jnp.float32
BF16 = jnp.bfloat16
MESH = pl.DeviceIdType.MESH
ORDER = (0, 2, 3, 4, 5, 6, 7, 1)


def cell_terms(prim):
    rho, vel, mag, pres = prim[0], prim[1:4], prim[4:7], prim[7]
    field_sq = mag[0] * mag[0] + mag[1] * mag[1] + mag[2] * mag[2]
    vel_sq = vel[0] * vel[0] + vel[1] * vel[1] + vel[2] * vel[2]
    half_sq = 0.5 * field_sq
    energy = pres * (1.0 / (GAMMA - 1.0)) + 0.5 * rho * vel_sq + half_sq
    total_p = pres + half_sq
    v_dot_b = vel[0] * mag[0] + vel[1] * mag[1] + vel[2] * mag[2]
    inv = 1.0 / rho
    sound_sq = GAMMA * pres * inv
    both = sound_sq + field_sq * inv
    momentum = [rho * v for v in vel]
    state = [rho] + momentum + list(mag) + [energy]
    return state, total_p, v_dot_b, sound_sq * inv, both


def flux_of(prim, terms, d):
    state, total_p, v_dot_b = terms[:3]
    vel, mag = prim[1:4], prim[4:7]
    vn, bn = vel[d], mag[d]
    flux = [state[1 + d]]
    for e in range(3):
        m = state[1 + e] * vn - mag[e] * bn
        flux.append(m + total_p if e == d else m)
    for e in range(3):
        flux.append(None if e == d else mag[e] * vn - bn * vel[e])
    flux.append((state[7] + total_p) * vn - bn * v_dot_b)
    return flux


def speed_of(prim, terms, d):
    sound_over, both = terms[3:]
    vn, bn = prim[1 + d], prim[4 + d]
    spread = both * both - 4.0 * sound_over * bn * bn
    fast = jnp.sqrt(0.5 * (both + jnp.sqrt(jnp.maximum(spread, 0.0))))
    return jnp.abs(vn) + fast


def face(f_lo, f_hi, u_lo, u_hi, largest):
    jump = largest * (u_hi - u_lo)
    return -0.5 * jump if f_lo is None else 0.5 * ((f_lo + f_hi) - jump)


def roll(values, shift, axis):
    return pltpu.roll(values, shift % values.shape[axis], axis)


def east(a):
    return roll(a, -1, 1)


def west(a):
    return roll(a, 1, 1)


def up(a):
    return roll(a, 1, 0)


def down(a):
    return roll(a, -1, 0)


def swap_by(cols, a):
    h = a.shape[0] // 2
    other = jnp.concatenate([a[h:], a[:h]], axis=0)
    return jnp.take_along_axis(other, cols, axis=1)


def flux_kernel(sizes, rho, vel, mag, pres, owner, line_row, ped, hall, shift,
                out, src_out, coef_out, cols_out,
                win, fwin, pstage, pin, part, part_in, cwin, own_v, row_v, shift_s,
                loc_sem, xs, xr, ls, lr, ys, yr, ds, dr, ps, pr, cs, cr, as_, ar, far):
    nx, ny = sizes
    cx, cy, nz = rho.shape
    ri = ped.shape[0]
    g, p = lax.axis_index("gx"), lax.axis_index("pb")
    n = nx * ny
    half = n // 2
    pairs = nx // 2
    b = g * ny + p
    wide = cy + 2 * PAD

    def dev(flat):
        return (flat // ny, flat % ny)

    barrier = pltpu.get_barrier_semaphore()

    for dg in (1, -1, 0, 2, -2):
        inside = (g + dg >= 0) & (g + dg < nx)

        @pl.when(inside)
        def _(to=jnp.clip(g + dg, 0, nx - 1), same=dg == 0):
            for o in (0, 1, -1):
                if o or not same:
                    pl.semaphore_signal(
                        barrier, inc=1, device_id=(to, (p + o) % ny), device_id_type=MESH)

    for o in (0, 1, -1):
        pl.semaphore_signal(barrier, inc=1, device_id=dev((b + half + o) % n), device_id_type=MESH)
    at_end = (b == 0) | (b == n - 1)

    @pl.when(at_end)
    def _():
        pl.semaphore_signal(barrier, inc=1, device_id=dev(n - 1 - b), device_id_type=MESH)

    doubling = [1 << i for i in range(1, 32) if 1 << i < nx]

    def pass_on(r):
        for to in (g + r, g - r):
            @pl.when((to >= 0) & (to < nx))
            def _(to=jnp.clip(to, 0, nx - 1), at=doubling.index(r)):
                pl.semaphore_signal(far.at[at], inc=1, device_id=(to, p), device_id_type=MESH)

    def hear(r):
        count = (g + r < nx).astype(jnp.int32) + (g - r >= 0).astype(jnp.int32)
        pl.semaphore_wait(far.at[doubling.index(r)], count)

    rows = pl.ds(PAD, cy)
    mid = pl.ds(1, cx)
    loads = [
        (rho, win.at[0, mid, rows]), (vel, win.at[pl.ds(2, 3), mid, rows]),
        (mag, win.at[pl.ds(5, 3), mid, rows]), (pres, win.at[1, mid, rows]),
        (ped, cwin.at[1, 0]), (hall, cwin.at[1, 1]), (shift, shift_s),
        (owner, own_v), (line_row, row_v)]
    loads = [pltpu.make_async_copy(s, d, loc_sem.at[i]) for i, (s, d) in enumerate(loads)]
    for c in loads:
        c.start()
    for c in loads:
        c.wait()

    row8 = lax.broadcasted_iota(jnp.int32, (ri, nz), 0)
    sh = jnp.zeros((ri, nz), F32)
    for i in range(ri):
        sh = jnp.where(row8 == i, shift_s[i].astype(F32), sh)
    cwin[1, 2] = sh

    lane = lax.broadcasted_iota(jnp.int32, (cx, cy, nz), 2)
    first, last = lane == 0, lane == nz - 1

    def z_dn(a):
        return jnp.where(first[:, :a.shape[1]], a, roll(a, 1, 2))

    def z_change(u, f, largest):
        low = face(None if f is None else z_dn(f), f, z_dn(u), u, largest)
        top = jnp.zeros_like(u) if f is None else f
        high = jnp.where(last[:, :u.shape[1]], top, roll(low, -1, 2))
        return high - low

    prim = [win[v, 1:1 + cx, PAD:PAD + cy, :] for v in ORDER]
    terms = cell_terms(prim)
    win[8, 1:1 + cx, PAD:PAD + cy, :] = speed_of(prim, terms, 0)
    flux, speed = flux_of(prim, terms, 2), speed_of(prim, terms, 2)
    largest = jnp.maximum(speed, z_dn(speed))
    for v in range(8):
        out[v] = terms[0][v] - COURANT * z_change(terms[0][v], flux[v], largest)

    pl.semaphore_wait(barrier, 3 * (jnp.minimum(g + 2, nx - 1) - jnp.maximum(g - 2, 0) + 1) + 2 + at_end.astype(jnp.int32))
    for r in doubling[:1]:
        pass_on(r)

    def remote(src, dst, send, recv, where):
        return pltpu.make_async_remote_copy(
            src_ref=src, dst_ref=dst, send_sem=send, recv_sem=recv,
            device_id=where, device_id_type=MESH)

    g_up, g_dn = jnp.minimum(g + 1, nx - 1), jnp.maximum(g - 1, 0)
    p_up, p_dn = jnp.minimum(p + 1, ny - 1), jnp.maximum(p - 1, 0)
    has_xu, has_xd, has_yu, has_yd = g < nx - 1, g > 0, p < ny - 1, p > 0

    def each(cond, copies, act):
        @pl.when(cond)
        def _():
            for c in copies:
                getattr(c, act)()

    def x_pair(at, count, send, recv):
        return [
            remote(win.at[pl.ds(at, count), s, rows], win.at[pl.ds(at, count), d, rows],
                   send.at[way], recv.at[way], (where, p))
            for way, (s, d, where) in enumerate(((cx, 0, g_up), (1, cx + 1, g_dn)))]

    xc = x_pair(2, 7, xs, xr)
    xlate = x_pair(0, 2, ls, lr)
    yc = [
        remote(win.at[pl.ds(0, 8), mid, pl.ds(s, PAD)], win.at[pl.ds(0, 8), mid, pl.ds(d, PAD)],
               ys.at[way], yr.at[way], (g, where))
        for way, (s, d, where) in enumerate(((cy, 0, p_up), (PAD, PAD + cy, p_dn)))]
    diag = []
    for i, (xu, yu) in enumerate(((1, 1), (1, 0), (0, 1), (0, 0))):
        s_x, d_x, to_g = (cx, 0, g_up) if xu else (1, cx + 1, g_dn)
        s_y, d_y, to_p = (PAD + cy - 1, PAD - 1, p_up) if yu else (PAD, PAD + cy, p_dn)
        c = remote(win.at[pl.ds(0, 8), s_x, pl.ds(s_y, 1)], win.at[pl.ds(0, 8), d_x, pl.ds(d_y, 1)],
                   ds.at[i], dr.at[i], (to_g, to_p))
        to = (has_xu if xu else has_xd) & (has_yu if yu else has_yd)
        come = (has_xd if xu else has_xu) & (has_yd if yu else has_yu)
        diag.append((c, to, come))
    ion = [
        ((b + 1) % n, 0),
        ((b + n - 1) % n, 2),
        ((b + half + 1) % n, 3),
        ((b + half) % n, 4),
        ((b + half + n - 1) % n, 5),
    ]
    cond_copies = [
        remote(cwin.at[1], cwin.at[slot], cs.at[slot], cr.at[slot], dev(flat)) for flat, slot in ion]

    each(has_yu, yc[:1], "start")
    each(has_yd, yc[1:], "start")
    for c, to, _ in diag:
        each(to, [c], "start")
    each(has_xu, xc[:1], "start")
    each(has_xd, xc[1:], "start")
    for c in cond_copies:
        c.start()

    each(has_yd, yc[:1], "wait_recv")
    each(has_yu, yc[1:], "wait_recv")

    @pl.when(p == 0)
    def _():
        for v in range(8):
            win[v, 1:1 + cx, PAD - 1:PAD, :] = win[v, 1:1 + cx, PAD:PAD + 1, :]

    @pl.when(p == ny - 1)
    def _():
        for v in range(8):
            win[v, 1:1 + cx, PAD + cy:PAD + cy + 1, :] = win[v, 1:1 + cx, PAD + cy - 1:PAD + cy, :]

    def x_inner(values, u, f):
        if cx == 1:
            return values
        speed = win[8, 1:1 + cx, PAD:PAD + cy, :]
        lows = face(None if f is None else f[:-1], None if f is None else f[1:], u[:-1], u[1:],
                    jnp.maximum(speed[:-1], speed[1:]))
        none = jnp.zeros_like(lows[:1])
        return values - COURANT * (jnp.concatenate([lows, none], 0) - jnp.concatenate([none, lows], 0))

    prim = [win[v, 1:1 + cx] for v in ORDER]
    terms = cell_terms(prim)
    flux, speed = flux_of(prim, terms, 1), speed_of(prim, terms, 1)
    largest = jnp.maximum(speed, roll(speed, 1, 1))

    def y_change(v):
        u, f = terms[0][v], flux[v]
        low = face(None if f is None else roll(f, 1, 1), f, roll(u, 1, 1), u, largest)
        return roll(low, -1, 1) - low

    def ends(a):
        return jnp.concatenate([a[:, :PAD], a[:, PAD + cy:]], axis=1)

    side = {}
    for v in (5, 6, 4):
        diff = y_change(v)
        if v != 5:
            side[v] = ends(diff)
        u = win[v + 1, 1:1 + cx, PAD:PAD + cy, :]
        f = None
        if v != 4:
            f = u * win[2, 1:1 + cx, PAD:PAD + cy, :] - (
                win[5, 1:1 + cx, PAD:PAD + cy, :] * win[v - 2, 1:1 + cx, PAD:PAD + cy, :])
        done = x_inner(out[v] - COURANT * diff[:, PAD:PAD + cy, :], u, f)
        if v == 4:
            out[v] = done
        else:
            pstage[v - 5] = done
        if v == 6:
            pc = [
                remote(pstage.at[:, s], pin.at[way], ps.at[way], pr.at[way], (where, p))
                for way, (s, where) in enumerate(((cx - 1, g_up), (0, g_dn)))]
            each(has_xu, pc[:1], "start")
            each(has_xd, pc[1:], "start")
    for at, r in enumerate(doubling[:-1]):
        hear(r)
        pass_on(doubling[at + 1])
    for v in (0, 1, 2, 3, 7):
        out[v] = out[v] - COURANT * y_change(v)[:, PAD:PAD + cy, :]

    for c, _, come in diag:
        each(come, [c], "wait_recv")

    def edge_planes(which, at, count):
        at = pl.ds(at, count)

        @pl.when(g == 0)
        def _():
            for v in which:
                win[v, 0, at, :] = win[v, 1, at, :]

        @pl.when(g == nx - 1)
        def _():
            for v in which:
                win[v, cx + 1, at, :] = win[v, cx, at, :]

    edge_planes(range(8), 0, PAD)
    edge_planes(range(8), PAD + cy, PAD)
    prim = [jnp.concatenate([win[v, :, :PAD, :], win[v, :, PAD + cy:, :]], axis=1) for v in ORDER]
    terms = cell_terms(prim)
    own = [a[1:1 + cx] for a in prim]
    speed_z = speed_of(own, (None, None, None, terms[3][1:1 + cx], terms[4][1:1 + cx]), 2)
    largest_z = jnp.maximum(speed_z, z_dn(speed_z))
    speed_x = speed_of(prim, terms, 0)
    largest_x = jnp.maximum(speed_x[:-1], speed_x[1:])
    for v in (4, 6):
        u = prim[v]
        fz = None if v == 6 else own[v] * own[3] - own[6] * own[v - 3]
        fx = None if v == 4 else u * prim[1] - prim[4] * prim[v - 3]
        lows = face(None if fx is None else fx[:-1], None if fx is None else fx[1:], u[:-1], u[1:], largest_x)
        new = own[v] - COURANT * (z_change(own[v], fz, largest_z) + side[v] + (lows[1:] - lows[:-1]))
        fwin[v // 6, :, 0:PAD, :] = new[:, :PAD]
        fwin[v // 6, :, PAD + cy:, :] = new[:, PAD:]

    each(has_xd, xc[:1], "wait_recv")
    each(has_xu, xc[1:], "wait_recv")
    for r in doubling[-1:]:
        hear(r)
    edge_planes(range(2, 9), PAD, cy)

    def outer_faces(v, f_of):
        faces = []
        for lo in (0, cx):
            u = [win[v + 1, lo + i, PAD:PAD + cy, :] for i in range(2)]
            f = [f_of(v, lo + i) for i in range(2)]
            most = jnp.maximum(win[8, lo, PAD:PAD + cy, :], win[8, lo + 1, PAD:PAD + cy, :])
            faces.append(COURANT * face(f[0], f[1], u[0], u[1], most))
        return faces

    def b_flux(v, at):
        if v == 4:
            return None
        q = [win[i, at, PAD:PAD + cy, :] for i in (v + 1, 2, 5, v - 2)]
        return q[0] * q[1] - q[2] * q[3]

    def close(values, faces):
        planes = [values[i] for i in range(cx)]
        planes[0] = planes[0] + faces[0]
        planes[-1] = planes[-1] - faces[1]
        return planes

    field, outer = {}, {}
    for v in (4, 6, 5):
        outer[v] = outer_faces(v, b_flux)
        field[v] = close(out[v] if v == 4 else pstage[v - 5], outer[v])
        for i in range(cx):
            out[v, i] = field[v][i]
            if v != 5:
                fwin[v // 6, i, PAD:PAD + cy, :] = field[v][i]

    @pl.when(p == 0)
    def _():
        fwin[:, :, PAD - 1:PAD, :] = fwin[:, :, PAD:PAD + 1, :]

    @pl.when(p == ny - 1)
    def _():
        fwin[:, :, PAD + cy:PAD + cy + 1, :] = fwin[:, :, PAD + cy - 1:PAD + cy, :]

    def d_y(v):
        a = fwin[v // 6]
        return 0.5 * (roll(a, -1, 1) - roll(a, 1, 1))[:, PAD:PAD + cy, :]

    def d_z(a):
        return 0.5 * (jnp.where(last, a, roll(a, -1, 2)) - z_dn(a))

    bx, by, bz = [jnp.stack(field[v]) for v in (4, 5, 6)]
    jx = d_y(6) - d_z(by)
    size = jnp.sqrt(bx * bx + by * by + bz * bz)
    dzx, dyx = d_z(bx), d_y(4)

    each(has_xd, pc[:1], "wait_recv")
    each(has_xu, pc[1:], "wait_recv")

    def d_x(v):
        lo = jnp.where(g == 0, field[v][0], pin[0, v - 5] - outer[v][0])
        hi = jnp.where(g == nx - 1, field[v][-1], pin[1, v - 5] + outer[v][1])
        a = jnp.stack([lo] + field[v] + [hi])
        return 0.5 * (a[2:] - a[:-2])

    jy = dzx - d_x(6)
    jz = d_x(5) - dyx
    current = (jx * bx + jy * by + jz * bz) / jnp.maximum(size, 1.0)
    current = current.reshape(cx * cy, nz)

    key = own_v[0] * ri + row_v[...]
    at = lax.broadcasted_iota(jnp.int32, (nx * ri, cx * cy), 0)
    pair, rest = at // (2 * ri), at % (2 * ri)
    hot = (key == (pair + (rest // ri) * pairs) * ri + rest % ri).astype(BF16)
    head = current.astype(BF16)
    tail = current - head.astype(F32)
    body_ = tail.astype(BF16)
    tail = (tail - body_.astype(F32)).astype(BF16)
    sums = jnp.dot(jnp.concatenate([hot, hot, hot], axis=1), jnp.concatenate([head, body_, tail], axis=0),
                   preferred_element_type=F32)
    part[...] = sums.reshape(pairs, 2, ri, nz)

    def part_copy(o, to):
        return remote(part.at[to % pairs], part_in.at[o + 1, g], as_.at[o + 1], ar.at[o + 1],
                      dev((to * ny + p - o + n) % n))

    def send(k, carry):
        to = (g + k) % nx
        for o in (-1, 0, 1):
            if o:
                part_copy(o, to).start()
            else:
                pl.when(k > 0)(lambda: part_copy(0, to).start())
        return carry

    lax.fori_loop(0, nx, send, 0, unroll=nx <= 8)
    each(has_xu, xlate[:1], "start")
    each(has_xd, xlate[1:], "start")

    for c in cond_copies:
        c.wait_recv()
    lines = 6 * ri
    row = lax.broadcasted_iota(jnp.int32, (lines, nz), 0)
    row = jnp.where(row >= 3 * ri, row - 3 * ri, row)
    place = b % half
    low_row = jnp.where(place == half // 2, ri, 0)
    high_row = jnp.where(place == half // 2 - 1, 2 * ri, 3 * ri)
    valid = (row >= low_row) & (row < high_row)
    pw = jnp.where(valid, cwin[:, 0].reshape(lines, nz), 0.0)
    hw = jnp.where(valid, cwin[:, 1].reshape(lines, nz), 0.0)
    own_shift = cwin[0:3, 2].reshape(3 * ri, nz).astype(jnp.int32)
    col = lax.broadcasted_iota(jnp.int32, (3 * ri, nz), 1)
    cols = jnp.concatenate(
        [(col + own_shift) % nz, (col + (nz - own_shift)) % nz], axis=0)
    he, hwst = east(hw), west(hw)
    coef = [
        0.5 * (pw + up(pw)), 0.5 * (pw + down(pw)),
        0.5 * (pw + east(pw)), 0.5 * (pw + west(pw)),
        0.125 * (hw + up(he)), 0.125 * (hw + up(hwst)),
        0.125 * (hw + down(he)), 0.125 * (hw + down(hwst)),
    ]
    center = coef[0]
    for c in coef[1:]:
        center = center + c
    inv = jnp.where(valid, 1.0 / jnp.where(valid, center, 1.0), 0.0)
    pm = swap_by(cols, pw)
    both = jnp.where(valid, pw + pm, 1.0)
    for i, c in enumerate(coef):
        coef_out[i] = c * inv
    coef_out[8] = inv
    coef_out[9] = jnp.where(valid, pw / both, 0.0)
    coef_out[10] = jnp.where(valid, pm / both, 0.0)
    cols_out[...] = cols

    def planes(v):
        return win[v, :, PAD:PAD + cy, :]

    each(has_xd, xlate[:1], "wait_recv")
    each(has_xu, xlate[1:], "wait_recv")
    edge_planes((0, 1), PAD, cy)
    prim = [planes(v) for v in ORDER]
    terms = cell_terms(prim)
    flux = flux_of(prim, terms, 0)
    speed = planes(8)
    largest = jnp.maximum(speed[:-1], speed[1:])
    for v in (0, 1, 2, 3, 7):
        u, f = terms[0][v], flux[v]
        lows = face(f[:-1], f[1:], u[:-1], u[1:], largest)
        out[v] = out[v] - COURANT * (lows[1:] - lows[:-1])

    for o in (-1, 0, 1):
        some = pl.ds(0, nx if o else nx - 1)
        pltpu.make_async_copy(part_in.at[o + 1, some], part_in.at[o + 1, some], ar.at[o + 1]).wait()
    part_in[1, g] = part[g % pairs]
    for o in (-1, 0, 1):
        def add(s, total, o=o):
            return total + part_in[o + 1, s]
        total = lax.fori_loop(1, nx, add, part_in[o + 1, 0], unroll=nx <= 8)
        northern = (b + o + n) % n < half
        src_out[0, o + 1] = jnp.where(northern, total[0], total[1])
        src_out[1, o + 1] = jnp.where(northern, total[1], total[0])

    each(has_xu, [xc[0], xlate[0], pc[0]], "wait_send")
    each(has_xd, [xc[1], xlate[1], pc[1]], "wait_send")
    each(has_yu, yc[:1], "wait_send")
    each(has_yd, yc[1:], "wait_send")
    for c, to, _ in diag:
        each(to, [c], "wait_send")
    for c in cond_copies:
        c.wait_send()
    for o in (-1, 0, 1):
        some = pl.ds(0, nx if o else nx - 1)
        pltpu.make_async_copy(part_in.at[o + 1, some], part_in.at[o + 1, some], as_.at[o + 1]).wait()


def sweep_kernel(con, src, coef, cols_ref, out, phi_out, phi_v, sems):
    write = pltpu.make_async_copy(con, out, sems.at[0])
    write.start()
    cu, cd, ce, cw, cue, cuw, cde, cdw, inv, wa, wb = [coef[i] for i in range(COEFS)]
    cols = cols_ref[...]
    ri = phi_v.shape[0]
    source = src[...].reshape(inv.shape) * inv

    def couple(phi):
        return wa * phi + wb * swap_by(cols, phi)

    phi = couple(source)
    for _ in range(SWEEPS - 1):
        e, w = east(phi), west(phi)
        acc = source + ce * e + cw * w
        acc = acc + up_terms(phi, e, w, cu, cue, cuw, up)
        acc = acc + up_terms(phi, e, w, cd, -cde, -cdw, down)
        phi = couple(acc)
    phi_v[...] = phi[ri:2 * ri]
    last = pltpu.make_async_copy(phi_v, phi_out, sems.at[1])
    last.start()
    write.wait()
    last.wait()


def up_terms(phi, e, w, straight, plus, minus, move):
    return straight * move(phi) + plus * move(e) - minus * move(w)


def body(sizes, density, velocity, magnetic, pressure, line_owner, line_row, pedersen, hall, mirror_shift):
    cx, cy, nz = density.shape
    ri = pedersen.shape[0]
    nx = sizes[0]
    any_ = pl.BlockSpec(memory_space=pl.ANY)
    vmem = pl.BlockSpec(memory_space=pltpu.VMEM)
    dma = pltpu.SemaphoreType.DMA
    con, src, coef, cols = pl.pallas_call(
        functools.partial(flux_kernel, sizes),
        out_shape=(
            pltpu.VMEM((8, cx, cy, nz), F32),
            pltpu.VMEM((2, 3, ri, nz), F32),
            pltpu.VMEM((COEFS, 6 * ri, nz), F32),
            pltpu.VMEM((6 * ri, nz), jnp.int32),
        ),
        in_specs=[any_] * 9,
        out_specs=(vmem,) * 4,
        scratch_shapes=[
            pltpu.VMEM((9, cx + 2, cy + 2 * PAD, nz), F32),
            pltpu.VMEM((2, cx, cy + 2 * PAD, nz), F32),
            pltpu.VMEM((2, cx, cy, nz), F32),
            pltpu.VMEM((2, 2, cy, nz), F32),
            pltpu.VMEM((nx // 2, 2, ri, nz), F32),
            pltpu.VMEM((3, nx, 2, ri, nz), F32),
            pltpu.VMEM((6, 3, ri, nz), F32),
            pltpu.VMEM((1, 1, cx * cy), jnp.int32),
            pltpu.VMEM((1, cx * cy), jnp.int32),
            pltpu.SMEM((ri,), jnp.int32),
            dma((9,)),
            dma((2,)), dma((2,)), dma((2,)), dma((2,)), dma((2,)), dma((2,)),
            dma((4,)), dma((4,)), dma((2,)), dma((2,)), dma((6,)), dma((6,)),
            dma((3,)), dma((3,)),
            pltpu.SemaphoreType.REGULAR((8,)),
        ],
        compiler_params=pltpu.CompilerParams(collective_id=0, has_side_effects=True),
        name="flux_and_sources",
    )(density, velocity, magnetic, pressure, line_owner.reshape(1, 1, cx * cy), line_row.reshape(1, cx * cy),
      pedersen, hall, mirror_shift)
    return pl.pallas_call(
        sweep_kernel,
        out_shape=(
            jax.ShapeDtypeStruct((8, cx, cy, nz), F32),
            jax.ShapeDtypeStruct((ri, nz), F32),
        ),
        in_specs=[vmem] * 4,
        out_specs=(any_, any_),
        scratch_shapes=[pltpu.VMEM((ri, nz), F32), dma((2,))],
        name="sweeps",
    )(*[pltpu.with_memory_space_constraint(a, pltpu.VMEM) for a in (con, src, coef, cols)])


def solution(mesh):
    sizes = (mesh.shape["gx"], mesh.shape["pb"])
    in_specs = (
        P("gx", "pb", None),
        P(None, "gx", "pb", None),
        P(None, "gx", "pb", None),
        P("gx", "pb", None),
        P("gx", "pb", None, None),
        P("gx", "pb", None),
        P(("gx", "pb"), None),
        P(("gx", "pb"), None),
        P(("gx", "pb")),
    )
    out_specs = (P(None, "gx", "pb", None), P(("gx", "pb"), None))
    return jax.shard_map(
        functools.partial(body, sizes), mesh=mesh, in_specs=in_specs, out_specs=out_specs,
        check_vma=False)
```

```python
import functools

import jax
import jax.numpy as jnp
from jax import lax
from jax.experimental import pallas as pl
from jax.experimental.pallas import tpu as pltpu
from jax.sharding import PartitionSpec as P

SWEEPS = 8
GAMMA = 5.0 / 3.0
COURANT = 0.08
PAD = 8
COEFS = 11
F32 = jnp.float32
BF16 = jnp.bfloat16
MESH = pl.DeviceIdType.MESH
ORDER = (0, 2, 3, 4, 5, 6, 7, 1)


def cell_terms(prim):
    rho, vel, mag, pres = prim[0], prim[1:4], prim[4:7], prim[7]
    field_sq = mag[0] * mag[0] + mag[1] * mag[1] + mag[2] * mag[2]
    vel_sq = vel[0] * vel[0] + vel[1] * vel[1] + vel[2] * vel[2]
    half_sq = 0.5 * field_sq
    energy = pres * (1.0 / (GAMMA - 1.0)) + 0.5 * rho * vel_sq + half_sq
    total_p = pres + half_sq
    v_dot_b = vel[0] * mag[0] + vel[1] * mag[1] + vel[2] * mag[2]
    inv = 1.0 / rho
    sound_sq = GAMMA * pres * inv
    both = sound_sq + field_sq * inv
    momentum = [rho * v for v in vel]
    state = [rho] + momentum + list(mag) + [energy]
    return state, total_p, v_dot_b, sound_sq * inv, both


def flux_of(prim, terms, d):
    state, total_p, v_dot_b = terms[:3]
    vel, mag = prim[1:4], prim[4:7]
    vn, bn = vel[d], mag[d]
    flux = [state[1 + d]]
    for e in range(3):
        m = state[1 + e] * vn - mag[e] * bn
        flux.append(m + total_p if e == d else m)
    for e in range(3):
        flux.append(None if e == d else mag[e] * vn - bn * vel[e])
    flux.append((state[7] + total_p) * vn - bn * v_dot_b)
    return flux


def speed_of(prim, terms, d):
    sound_over, both = terms[3:]
    vn, bn = prim[1 + d], prim[4 + d]
    spread = both * both - 4.0 * sound_over * bn * bn
    fast = jnp.sqrt(0.5 * (both + jnp.sqrt(jnp.maximum(spread, 0.0))))
    return jnp.abs(vn) + fast


def face(f_lo, f_hi, u_lo, u_hi, largest):
    jump = largest * (u_hi - u_lo)
    return -0.5 * jump if f_lo is None else 0.5 * ((f_lo + f_hi) - jump)


def roll(values, shift, axis):
    return pltpu.roll(values, shift % values.shape[axis], axis)


def east(a):
    return roll(a, -1, 1)


def west(a):
    return roll(a, 1, 1)


def up(a):
    return roll(a, 1, 0)


def down(a):
    return roll(a, -1, 0)


def swap_by(cols, a):
    h = a.shape[0] // 2
    other = jnp.concatenate([a[h:], a[:h]], axis=0)
    return jnp.take_along_axis(other, cols, axis=1)


def flux_kernel(sizes, rho, vel, mag, pres, owner, line_row, ped, hall, shift,
                out, src_out, coef_out, cols_out,
                win, fwin, pstage, pin, part, part_in, shared, cwin, own_v, row_v, shift_s,
                loc_sem, xs, xr, ls, lr, ys, yr, ds, dr, ps, pr, cs, cr, as_, ar, hs, hr, far):
    nx, ny = sizes
    cx, cy, nz = rho.shape
    ri = ped.shape[0]
    g, p = lax.axis_index("gx"), lax.axis_index("pb")
    n = nx * ny
    half = n // 2
    pairs = nx // 2
    b = g * ny + p
    wide = cy + 2 * PAD

    def dev(flat):
        return (lax.div(flat, ny), lax.rem(flat, ny))

    beside = {o: dev(lax.rem(b + o + n, n)) for o in (-1, 1)}

    barrier = pltpu.get_barrier_semaphore()

    for dg in (1, -1, 0, 2, -2):
        inside = (g + dg >= 0) & (g + dg < nx)

        @pl.when(inside)
        def _(to=jnp.clip(g + dg, 0, nx - 1), same=dg == 0):
            for o in (0, 1, -1):
                if o or not same:
                    pl.semaphore_signal(
                        barrier, inc=1, device_id=(to, beside[o][1] if o else p), device_id_type=MESH)

    for o in (0, 1, -1):
        pl.semaphore_signal(barrier, inc=1, device_id=dev(lax.rem(b + half + o, n)), device_id_type=MESH)
    at_end = (b == 0) | (b == n - 1)

    @pl.when(at_end)
    def _():
        pl.semaphore_signal(barrier, inc=1, device_id=dev(n - 1 - b), device_id_type=MESH)

    doubling = [1 << i for i in range(1, 32) if 1 << i < nx]

    def pass_on(r):
        for to in (g + r, g - r):
            @pl.when((to >= 0) & (to < nx))
            def _(to=jnp.clip(to, 0, nx - 1), at=doubling.index(r)):
                pl.semaphore_signal(far.at[at], inc=1, device_id=(to, p), device_id_type=MESH)

    def hear(r):
        count = (g + r < nx).astype(jnp.int32) + (g - r >= 0).astype(jnp.int32)
        pl.semaphore_wait(far.at[doubling.index(r)], count)

    rows = pl.ds(PAD, cy)
    mid = pl.ds(1, cx)
    loads = [
        (rho, win.at[0, mid, rows]), (vel, win.at[pl.ds(2, 3), mid, rows]),
        (mag, win.at[pl.ds(5, 3), mid, rows]), (pres, win.at[1, mid, rows]),
        (ped, cwin.at[1, 0]), (hall, cwin.at[1, 1]), (shift, shift_s),
        (owner, own_v), (line_row, row_v)]
    loads = [pltpu.make_async_copy(s, d, loc_sem.at[i]) for i, (s, d) in enumerate(loads)]
    for c in loads:
        c.start()
    for c in loads:
        c.wait()

    row8 = lax.broadcasted_iota(jnp.int32, (ri, nz), 0)
    sh = jnp.zeros((ri, nz), F32)
    for i in range(ri):
        sh = jnp.where(row8 == i, shift_s[i].astype(F32), sh)
    cwin[1, 2] = sh

    lane = lax.broadcasted_iota(jnp.int32, (cx, cy, nz), 2)
    first, last = lane == 0, lane == nz - 1

    def z_dn(a):
        return jnp.where(first[:, :a.shape[1]], a, roll(a, 1, 2))

    def z_change(u, f, largest):
        low = face(None if f is None else z_dn(f), f, z_dn(u), u, largest)
        top = jnp.zeros_like(u) if f is None else f
        high = jnp.where(last[:, :u.shape[1]], top, roll(low, -1, 2))
        return high - low

    prim = [win[v, 1:1 + cx, PAD:PAD + cy, :] for v in ORDER]
    terms = cell_terms(prim)
    win[8, 1:1 + cx, PAD:PAD + cy, :] = speed_of(prim, terms, 0)
    flux, speed = flux_of(prim, terms, 2), speed_of(prim, terms, 2)
    largest = jnp.maximum(speed, z_dn(speed))
    for v in range(8):
        out[v] = terms[0][v] - COURANT * z_change(terms[0][v], flux[v], largest)

    pl.semaphore_wait(barrier, 3 * (jnp.minimum(g + 2, nx - 1) - jnp.maximum(g - 2, 0) + 1) + 2 + at_end.astype(jnp.int32))
    for r in doubling[:1]:
        pass_on(r)

    def remote(src, dst, send, recv, where):
        return pltpu.make_async_remote_copy(
            src_ref=src, dst_ref=dst, send_sem=send, recv_sem=recv,
            device_id=where, device_id_type=MESH)

    g_up, g_dn = jnp.minimum(g + 1, nx - 1), jnp.maximum(g - 1, 0)
    p_up, p_dn = jnp.minimum(p + 1, ny - 1), jnp.maximum(p - 1, 0)
    has_xu, has_xd, has_yu, has_yd = g < nx - 1, g > 0, p < ny - 1, p > 0

    def each(cond, copies, act):
        @pl.when(cond)
        def _():
            for c in copies:
                getattr(c, act)()

    def x_pair(at, count, send, recv):
        return [
            remote(win.at[pl.ds(at, count), s, rows], win.at[pl.ds(at, count), d, rows],
                   send.at[way], recv.at[way], (where, p))
            for way, (s, d, where) in enumerate(((cx, 0, g_up), (1, cx + 1, g_dn)))]

    xc = x_pair(2, 7, xs, xr)
    xlate = x_pair(0, 2, ls, lr)
    yc = [
        remote(win.at[pl.ds(0, 8), mid, pl.ds(s, PAD)], win.at[pl.ds(0, 8), mid, pl.ds(d, PAD)],
               ys.at[way], yr.at[way], (g, where))
        for way, (s, d, where) in enumerate(((cy, 0, p_up), (PAD, PAD + cy, p_dn)))]
    diag = []
    for i, (xu, yu) in enumerate(((1, 1), (1, 0), (0, 1), (0, 0))):
        s_x, d_x, to_g = (cx, 0, g_up) if xu else (1, cx + 1, g_dn)
        s_y, d_y, to_p = (PAD + cy - 1, PAD - 1, p_up) if yu else (PAD, PAD + cy, p_dn)
        c = remote(win.at[pl.ds(0, 8), s_x, pl.ds(s_y, 1)], win.at[pl.ds(0, 8), d_x, pl.ds(d_y, 1)],
                   ds.at[i], dr.at[i], (to_g, to_p))
        to = (has_xu if xu else has_xd) & (has_yu if yu else has_yd)
        come = (has_xd if xu else has_xu) & (has_yd if yu else has_yu)
        diag.append((c, to, come))
    ion = [
        (lax.rem(b + 1, n), 0),
        (lax.rem(b + n - 1, n), 2),
        (lax.rem(b + half + 1, n), 3),
        (lax.rem(b + half, n), 4),
        (lax.rem(b + half + n - 1, n), 5),
    ]
    cond_copies = [
        remote(cwin.at[1, pl.ds(0, 3 if slot < 3 else 2)], cwin.at[slot, pl.ds(0, 3 if slot < 3 else 2)],
               cs.at[slot], cr.at[slot], dev(flat)) for flat, slot in ion]

    each(has_yu, yc[:1], "start")
    each(has_yd, yc[1:], "start")
    for c, to, _ in diag:
        each(to, [c], "start")
    each(has_xu, xc[:1], "start")
    each(has_xd, xc[1:], "start")
    for c in cond_copies:
        c.start()

    each(has_yd, yc[:1], "wait_recv")
    each(has_yu, yc[1:], "wait_recv")

    @pl.when(p == 0)
    def _():
        for v in range(8):
            win[v, 1:1 + cx, PAD - 1:PAD, :] = win[v, 1:1 + cx, PAD:PAD + 1, :]

    @pl.when(p == ny - 1)
    def _():
        for v in range(8):
            win[v, 1:1 + cx, PAD + cy:PAD + cy + 1, :] = win[v, 1:1 + cx, PAD + cy - 1:PAD + cy, :]

    def x_inner(values, u, f):
        if cx == 1:
            return values
        speed = win[8, 1:1 + cx, PAD:PAD + cy, :]
        lows = face(None if f is None else f[:-1], None if f is None else f[1:], u[:-1], u[1:],
                    jnp.maximum(speed[:-1], speed[1:]))
        none = jnp.zeros_like(lows[:1])
        return values - COURANT * (jnp.concatenate([lows, none], 0) - jnp.concatenate([none, lows], 0))

    prim = [win[v, 1:1 + cx] for v in ORDER]
    terms = cell_terms(prim)
    flux, speed = flux_of(prim, terms, 1), speed_of(prim, terms, 1)
    largest = jnp.maximum(speed, roll(speed, 1, 1))

    def y_change(v):
        u, f = terms[0][v], flux[v]
        low = face(None if f is None else roll(f, 1, 1), f, roll(u, 1, 1), u, largest)
        return roll(low, -1, 1) - low

    def ends(a):
        return jnp.concatenate([a[:, :PAD], a[:, PAD + cy:]], axis=1)

    side = {}
    for v in (5, 6, 4):
        diff = y_change(v)
        if v != 5:
            side[v] = ends(diff)
        u = win[v + 1, 1:1 + cx, PAD:PAD + cy, :]
        f = None
        if v != 4:
            f = u * win[2, 1:1 + cx, PAD:PAD + cy, :] - (
                win[5, 1:1 + cx, PAD:PAD + cy, :] * win[v - 2, 1:1 + cx, PAD:PAD + cy, :])
        done = x_inner(out[v] - COURANT * diff[:, PAD:PAD + cy, :], u, f)
        if v == 4:
            out[v] = done
        else:
            pstage[v - 5] = done
        if v == 6:
            pc = [
                remote(pstage.at[:, s], pin.at[way], ps.at[way], pr.at[way], (where, p))
                for way, (s, where) in enumerate(((cx - 1, g_up), (0, g_dn)))]
            each(has_xu, pc[:1], "start")
            each(has_xd, pc[1:], "start")
    for at, r in enumerate(doubling[:-1]):
        hear(r)
        pass_on(doubling[at + 1])
    for v in (0, 1, 2, 3, 7):
        out[v] = out[v] - COURANT * y_change(v)[:, PAD:PAD + cy, :]

    for c, _, come in diag:
        each(come, [c], "wait_recv")

    def edge_planes(which, at, count):
        at = pl.ds(at, count)

        @pl.when(g == 0)
        def _():
            for v in which:
                win[v, 0, at, :] = win[v, 1, at, :]

        @pl.when(g == nx - 1)
        def _():
            for v in which:
                win[v, cx + 1, at, :] = win[v, cx, at, :]

    edge_planes(range(8), 0, PAD)
    edge_planes(range(8), PAD + cy, PAD)
    prim = [jnp.concatenate([win[v, :, :PAD, :], win[v, :, PAD + cy:, :]], axis=1) for v in ORDER]
    terms = cell_terms(prim)
    own = [a[1:1 + cx] for a in prim]
    speed_z = speed_of(own, (None, None, None, terms[3][1:1 + cx], terms[4][1:1 + cx]), 2)
    largest_z = jnp.maximum(speed_z, z_dn(speed_z))
    speed_x = speed_of(prim, terms, 0)
    largest_x = jnp.maximum(speed_x[:-1], speed_x[1:])
    for v in (4, 6):
        u = prim[v]
        fz = None if v == 6 else own[v] * own[3] - own[6] * own[v - 3]
        fx = None if v == 4 else u * prim[1] - prim[4] * prim[v - 3]
        lows = face(None if fx is None else fx[:-1], None if fx is None else fx[1:], u[:-1], u[1:], largest_x)
        new = own[v] - COURANT * (z_change(own[v], fz, largest_z) + side[v] + (lows[1:] - lows[:-1]))
        fwin[v // 6, :, 0:PAD, :] = new[:, :PAD]
        fwin[v // 6, :, PAD + cy:, :] = new[:, PAD:]

    each(has_xd, xc[:1], "wait_recv")
    each(has_xu, xc[1:], "wait_recv")
    for r in doubling[-1:]:
        hear(r)
    edge_planes(range(2, 9), PAD, cy)

    def outer_faces(v, f_of):
        faces = []
        for lo in (0, cx):
            u = [win[v + 1, lo + i, PAD:PAD + cy, :] for i in range(2)]
            f = [f_of(v, lo + i) for i in range(2)]
            most = jnp.maximum(win[8, lo, PAD:PAD + cy, :], win[8, lo + 1, PAD:PAD + cy, :])
            faces.append(COURANT * face(f[0], f[1], u[0], u[1], most))
        return faces

    def b_flux(v, at):
        if v == 4:
            return None
        q = [win[i, at, PAD:PAD + cy, :] for i in (v + 1, 2, 5, v - 2)]
        return q[0] * q[1] - q[2] * q[3]

    def close(values, faces):
        planes = [values[i] for i in range(cx)]
        planes[0] = planes[0] + faces[0]
        planes[-1] = planes[-1] - faces[1]
        return planes

    field, outer = {}, {}
    for v in (4, 6, 5):
        outer[v] = outer_faces(v, b_flux)
        field[v] = close(out[v] if v == 4 else pstage[v - 5], outer[v])
        for i in range(cx):
            out[v, i] = field[v][i]
            if v != 5:
                fwin[v // 6, i, PAD:PAD + cy, :] = field[v][i]

    @pl.when(p == 0)
    def _():
        fwin[:, :, PAD - 1:PAD, :] = fwin[:, :, PAD:PAD + 1, :]

    @pl.when(p == ny - 1)
    def _():
        fwin[:, :, PAD + cy:PAD + cy + 1, :] = fwin[:, :, PAD + cy - 1:PAD + cy, :]

    def d_y(v):
        a = fwin[v // 6]
        return 0.5 * (roll(a, -1, 1) - roll(a, 1, 1))[:, PAD:PAD + cy, :]

    def d_z(a):
        return 0.5 * (jnp.where(last, a, roll(a, -1, 2)) - z_dn(a))

    bx, by, bz = [jnp.stack(field[v]) for v in (4, 5, 6)]
    jx = d_y(6) - d_z(by)
    size = jnp.sqrt(bx * bx + by * by + bz * bz)
    dzx, dyx = d_z(bx), d_y(4)

    each(has_xd, pc[:1], "wait_recv")
    each(has_xu, pc[1:], "wait_recv")

    def d_x(v):
        lo = jnp.where(g == 0, field[v][0], pin[0, v - 5] - outer[v][0])
        hi = jnp.where(g == nx - 1, field[v][-1], pin[1, v - 5] + outer[v][1])
        a = jnp.stack([lo] + field[v] + [hi])
        return 0.5 * (a[2:] - a[:-2])

    jy = dzx - d_x(6)
    jz = d_x(5) - dyx
    current = (jx * bx + jy * by + jz * bz) / jnp.maximum(size, 1.0)
    current = current.reshape(cx * cy, nz)

    key = own_v[0] * ri + row_v[...]
    at = lax.broadcasted_iota(jnp.int32, (nx * ri, cx * cy), 0)
    pair, rest = at // (2 * ri), at % (2 * ri)
    hot = (key == (pair + (rest // ri) * pairs) * ri + rest % ri).astype(BF16)
    head = current.astype(BF16)
    tail = current - head.astype(F32)
    body_ = tail.astype(BF16)
    tail = (tail - body_.astype(F32)).astype(BF16)
    sums = jnp.dot(jnp.concatenate([hot, hot, hot], axis=1), jnp.concatenate([head, body_, tail], axis=0),
                   preferred_element_type=F32)
    part[...] = sums.reshape(pairs, 2, ri, nz)

    odd = lax.rem(p, 2)
    mate = (g, p + 1 - 2 * odd)
    out_g, out_p = jnp.where(odd == 1, beside[1][0], beside[-1][0]), jnp.where(odd == 1, beside[1][1], beside[-1][1])
    step = lax.rem(out_g - g + nx, nx)

    def own_copy(to):
        return remote(part.at[lax.rem(to, pairs)], part_in.at[0, g], as_.at[0], ar.at[0], (to, p))

    def outer_copy(to, first_row):
        some = pl.ds(first_row, ri - 1)
        return remote(part.at[lax.rem(to, pairs), :, some], part_in.at[1, g, :, some], as_.at[1], ar.at[1],
                      (lax.rem(to + step, nx), out_p))

    def send_own(k, carry):
        own_copy(lax.rem(g + k, nx)).start()
        return carry

    def send_outer(first_row):
        def send(k, carry):
            outer_copy(lax.rem(g + k, nx), first_row).start()
            return carry

        lax.fori_loop(0, nx, send, 0, unroll=nx <= 8)

    lax.fori_loop(1, nx, send_own, 0, unroll=nx <= 8)
    pl.when(odd == 1)(lambda: send_outer(1))
    pl.when(odd == 0)(lambda: send_outer(0))
    each(has_xu, xlate[:1], "start")
    each(has_xd, xlate[1:], "start")

    for c in cond_copies:
        c.wait_recv()
    lines = 6 * ri
    row = lax.broadcasted_iota(jnp.int32, (lines, nz), 0)
    row = jnp.where(row >= 3 * ri, row - 3 * ri, row)
    place = lax.rem(b, half)
    low_row = jnp.where(place == half // 2, ri, 0)
    high_row = jnp.where(place == half // 2 - 1, 2 * ri, 3 * ri)
    valid = (row >= low_row) & (row < high_row)
    pw = jnp.where(valid, cwin[:, 0].reshape(lines, nz), 0.0)
    hw = jnp.where(valid, cwin[:, 1].reshape(lines, nz), 0.0)
    own_shift = cwin[0:3, 2].reshape(3 * ri, nz).astype(jnp.int32)
    col = lax.broadcasted_iota(jnp.int32, (3 * ri, nz), 1)
    cols = jnp.concatenate(
        [(col + own_shift) % nz, (col + (nz - own_shift)) % nz], axis=0)
    he, hwst = east(hw), west(hw)
    coef = [
        0.5 * (pw + up(pw)), 0.5 * (pw + down(pw)),
        0.5 * (pw + east(pw)), 0.5 * (pw + west(pw)),
        0.125 * (hw + up(he)), 0.125 * (hw + up(hwst)),
        0.125 * (hw + down(he)), 0.125 * (hw + down(hwst)),
    ]
    center = coef[0]
    for c in coef[1:]:
        center = center + c
    inv = jnp.where(valid, 1.0 / jnp.where(valid, center, 1.0), 0.0)
    pm = swap_by(cols, pw)
    both = jnp.where(valid, pw + pm, 1.0)
    for i, c in enumerate(coef):
        coef_out[i] = c * inv
    coef_out[8] = inv
    coef_out[9] = jnp.where(valid, pw / both, 0.0)
    coef_out[10] = jnp.where(valid, pm / both, 0.0)
    cols_out[...] = cols

    def taken(slot, sems):
        some = part_in.at[slot, pl.ds(0, nx - 1 if slot == 0 else nx), :, pl.ds(0, ri if slot == 0 else ri - 1)]
        pltpu.make_async_copy(some, some, sems.at[slot]).wait()

    def total_of(slot):
        def add(at, total):
            return total + part_in[slot, at]
        return lax.fori_loop(1, nx, add, part_in[slot, 0], unroll=nx <= 8)

    taken(0, ar)
    part_in[0, g] = part[lax.rem(g, pairs)]
    shared[0] = total_of(0)
    to_mate = remote(shared.at[0], shared.at[1], hs.at[0], hr.at[0], mate)
    to_mate.start()
    def planes(v):
        return win[v, :, PAD:PAD + cy, :]

    each(has_xd, xlate[:1], "wait_recv")
    each(has_xu, xlate[1:], "wait_recv")
    edge_planes((0, 1), PAD, cy)
    prim = [planes(v) for v in ORDER]
    terms = cell_terms(prim)
    flux = flux_of(prim, terms, 0)
    speed = planes(8)
    largest = jnp.maximum(speed[:-1], speed[1:])
    for v in (0, 1, 2, 3, 7):
        u, f = terms[0][v], flux[v]
        lows = face(f[:-1], f[1:], u[:-1], u[1:], largest)
        out[v] = out[v] - COURANT * (lows[1:] - lows[:-1])

    taken(1, ar)
    outer_sum = total_of(1)
    to_mate.wait_recv()

    def place_sums(slot, total, block):
        northern = block < half
        src_out[0, slot] = jnp.where(northern, total[0], total[1])
        src_out[1, slot] = jnp.where(northern, total[1], total[0])

    mate_sum = shared[1]
    place_sums(0, jnp.where(odd == 1, mate_sum, outer_sum), lax.rem(b + n - 1, n))
    place_sums(1, shared[0], b)
    place_sums(2, jnp.where(odd == 1, outer_sum, mate_sum), lax.rem(b + 1, n))

    each(has_xu, [xc[0], xlate[0], pc[0]], "wait_send")
    each(has_xd, [xc[1], xlate[1], pc[1]], "wait_send")
    each(has_yu, yc[:1], "wait_send")
    each(has_yd, yc[1:], "wait_send")
    for c, to, _ in diag:
        each(to, [c], "wait_send")
    for c in cond_copies:
        c.wait_send()
    to_mate.wait_send()
    taken(0, as_)
    taken(1, as_)


def sweep_kernel(con, src, coef, cols_ref, out, phi_out, phi_v, sems):
    write = pltpu.make_async_copy(con, out, sems.at[0])
    write.start()
    cu, cd, ce, cw, cue, cuw, cde, cdw, inv, wa, wb = [coef[i] for i in range(COEFS)]
    cols = cols_ref[...]
    ri = phi_v.shape[0]
    source = src[...].reshape(inv.shape) * inv

    def couple(phi):
        return wa * phi + wb * swap_by(cols, phi)

    phi = couple(source)
    for _ in range(SWEEPS - 1):
        e, w = east(phi), west(phi)
        acc = source + ce * e + cw * w
        acc = acc + up_terms(phi, e, w, cu, cue, cuw, up)
        acc = acc + up_terms(phi, e, w, cd, -cde, -cdw, down)
        phi = couple(acc)
    phi_v[...] = phi[ri:2 * ri]
    last = pltpu.make_async_copy(phi_v, phi_out, sems.at[1])
    last.start()
    write.wait()
    last.wait()


def up_terms(phi, e, w, straight, plus, minus, move):
    return straight * move(phi) + plus * move(e) - minus * move(w)


def body(sizes, density, velocity, magnetic, pressure, line_owner, line_row, pedersen, hall, mirror_shift):
    cx, cy, nz = density.shape
    ri = pedersen.shape[0]
    nx = sizes[0]
    any_ = pl.BlockSpec(memory_space=pl.ANY)
    vmem = pl.BlockSpec(memory_space=pltpu.VMEM)
    dma = pltpu.SemaphoreType.DMA
    con, src, coef, cols = pl.pallas_call(
        functools.partial(flux_kernel, sizes),
        out_shape=(
            pltpu.VMEM((8, cx, cy, nz), F32),
            pltpu.VMEM((2, 3, ri, nz), F32),
            pltpu.VMEM((COEFS, 6 * ri, nz), F32),
            pltpu.VMEM((6 * ri, nz), jnp.int32),
        ),
        in_specs=[any_] * 9,
        out_specs=(vmem,) * 4,
        scratch_shapes=[
            pltpu.VMEM((9, cx + 2, cy + 2 * PAD, nz), F32),
            pltpu.VMEM((2, cx, cy + 2 * PAD, nz), F32),
            pltpu.VMEM((2, cx, cy, nz), F32),
            pltpu.VMEM((2, 2, cy, nz), F32),
            pltpu.VMEM((nx // 2, 2, ri, nz), F32),
            pltpu.VMEM((2, nx, 2, ri, nz), F32),
            pltpu.VMEM((2, 2, ri, nz), F32),
            pltpu.VMEM((6, 3, ri, nz), F32),
            pltpu.VMEM((1, 1, cx * cy), jnp.int32),
            pltpu.VMEM((1, cx * cy), jnp.int32),
            pltpu.SMEM((ri,), jnp.int32),
            dma((9,)),
            dma((2,)), dma((2,)), dma((2,)), dma((2,)), dma((2,)), dma((2,)),
            dma((4,)), dma((4,)), dma((2,)), dma((2,)), dma((6,)), dma((6,)),
            dma((2,)), dma((2,)), dma((1,)), dma((1,)),
            pltpu.SemaphoreType.REGULAR((8,)),
        ],
        compiler_params=pltpu.CompilerParams(collective_id=0, has_side_effects=True),
        name="flux_and_sources",
    )(density, velocity, magnetic, pressure, line_owner.reshape(1, 1, cx * cy), line_row.reshape(1, cx * cy),
      pedersen, hall, mirror_shift)
    return pl.pallas_call(
        sweep_kernel,
        out_shape=(
            jax.ShapeDtypeStruct((8, cx, cy, nz), F32),
            jax.ShapeDtypeStruct((ri, nz), F32),
        ),
        in_specs=[vmem] * 4,
        out_specs=(any_, any_),
        scratch_shapes=[pltpu.VMEM((ri, nz), F32), dma((2,))],
        name="sweeps",
    )(*[pltpu.with_memory_space_constraint(a, pltpu.VMEM) for a in (con, src, coef, cols)])


def solution(mesh):
    sizes = (mesh.shape["gx"], mesh.shape["pb"])
    in_specs = (
        P("gx", "pb", None),
        P(None, "gx", "pb", None),
        P(None, "gx", "pb", None),
        P("gx", "pb", None),
        P("gx", "pb", None, None),
        P("gx", "pb", None),
        P(("gx", "pb"), None),
        P(("gx", "pb"), None),
        P(("gx", "pb")),
    )
    out_specs = (P(None, "gx", "pb", None), P(("gx", "pb"), None))
    return jax.shard_map(
        functools.partial(body, sizes), mesh=mesh, in_specs=in_specs, out_specs=out_specs,
        check_vma=False)
```

```python
import functools

import jax
import jax.numpy as jnp
from jax import lax
from jax.experimental import pallas as pl
from jax.experimental.pallas import tpu as pltpu
from jax.sharding import PartitionSpec as P

SWEEPS = 8
GAMMA = 5.0 / 3.0
COURANT = 0.08
PAD = 8
COEFS = 11
F32 = jnp.float32
BF16 = jnp.bfloat16
MESH = pl.DeviceIdType.MESH
ORDER = (0, 2, 3, 4, 5, 6, 7, 1)


def cell_terms(prim):
    rho, vel, mag, pres = prim[0], prim[1:4], prim[4:7], prim[7]
    field_sq = mag[0] * mag[0] + mag[1] * mag[1] + mag[2] * mag[2]
    vel_sq = vel[0] * vel[0] + vel[1] * vel[1] + vel[2] * vel[2]
    half_sq = 0.5 * field_sq
    energy = pres * (1.0 / (GAMMA - 1.0)) + 0.5 * rho * vel_sq + half_sq
    total_p = pres + half_sq
    v_dot_b = vel[0] * mag[0] + vel[1] * mag[1] + vel[2] * mag[2]
    inv = 1.0 / rho
    sound_sq = GAMMA * pres * inv
    both = sound_sq + field_sq * inv
    momentum = [rho * v for v in vel]
    state = [rho] + momentum + list(mag) + [energy]
    return state, total_p, v_dot_b, sound_sq * inv, both


def flux_of(prim, terms, d):
    state, total_p, v_dot_b = terms[:3]
    vel, mag = prim[1:4], prim[4:7]
    vn, bn = vel[d], mag[d]
    flux = [state[1 + d]]
    for e in range(3):
        m = state[1 + e] * vn - mag[e] * bn
        flux.append(m + total_p if e == d else m)
    for e in range(3):
        flux.append(None if e == d else mag[e] * vn - bn * vel[e])
    flux.append((state[7] + total_p) * vn - bn * v_dot_b)
    return flux


def speed_of(prim, terms, d):
    sound_over, both = terms[3:]
    vn, bn = prim[1 + d], prim[4 + d]
    spread = both * both - 4.0 * sound_over * bn * bn
    fast = jnp.sqrt(0.5 * (both + jnp.sqrt(jnp.maximum(spread, 0.0))))
    return jnp.abs(vn) + fast


def face(f_lo, f_hi, u_lo, u_hi, largest):
    jump = largest * (u_hi - u_lo)
    return -0.5 * jump if f_lo is None else 0.5 * ((f_lo + f_hi) - jump)


def roll(values, shift, axis):
    return pltpu.roll(values, shift % values.shape[axis], axis)


def east(a):
    return roll(a, -1, 1)


def west(a):
    return roll(a, 1, 1)


def up(a):
    return roll(a, 1, 0)


def down(a):
    return roll(a, -1, 0)


def swap_by(cols, a):
    h = a.shape[0] // 2
    other = jnp.concatenate([a[h:], a[:h]], axis=0)
    return jnp.take_along_axis(other, cols, axis=1)


def flux_kernel(sizes, rho, vel, mag, pres, owner, line_row, ped, hall, shift,
                out, src_out, coef_out, cols_out,
                win, fwin, pstage, pin, part, part_in, shared, cwin, own_v, row_v, shift_s,
                loc_sem, xs, xr, ls, lr, ys, yr, ds, dr, ps, pr, cs, cr, as_, ar, hs, hr, far):
    nx, ny = sizes
    cx, cy, nz = rho.shape
    ri = ped.shape[0]
    g, p = lax.axis_index("gx"), lax.axis_index("pb")
    n = nx * ny
    half = n // 2
    pairs = nx // 2
    b = g * ny + p
    wide = cy + 2 * PAD

    def dev(flat):
        return (lax.div(flat, ny), lax.rem(flat, ny))

    beside = {o: dev(lax.rem(b + o + n, n)) for o in (-1, 1)}

    barrier = pltpu.get_barrier_semaphore()

    for dg in (1, -1, 0, 2, -2):
        inside = (g + dg >= 0) & (g + dg < nx)

        @pl.when(inside)
        def _(to=jnp.clip(g + dg, 0, nx - 1), same=dg == 0):
            for o in (0, 1, -1):
                if o or not same:
                    pl.semaphore_signal(
                        barrier, inc=1, device_id=(to, beside[o][1] if o else p), device_id_type=MESH)

    for o in (0, 1, -1):
        pl.semaphore_signal(barrier, inc=1, device_id=dev(lax.rem(b + half + o, n)), device_id_type=MESH)
    at_end = (b == 0) | (b == n - 1)

    @pl.when(at_end)
    def _():
        pl.semaphore_signal(barrier, inc=1, device_id=dev(n - 1 - b), device_id_type=MESH)

    doubling = [1 << i for i in range(1, 32) if 1 << i < nx]

    def pass_on(r):
        for to in (g + r, g - r):
            @pl.when((to >= 0) & (to < nx))
            def _(to=jnp.clip(to, 0, nx - 1), at=doubling.index(r)):
                pl.semaphore_signal(far.at[at], inc=1, device_id=(to, p), device_id_type=MESH)

    def hear(r):
        count = (g + r < nx).astype(jnp.int32) + (g - r >= 0).astype(jnp.int32)
        pl.semaphore_wait(far.at[doubling.index(r)], count)

    rows = pl.ds(PAD, cy)
    mid = pl.ds(1, cx)
    loads = [
        (rho, win.at[0, mid, rows]), (vel, win.at[pl.ds(2, 3), mid, rows]),
        (mag, win.at[pl.ds(5, 3), mid, rows]), (pres, win.at[1, mid, rows]),
        (ped, cwin.at[1, 0]), (hall, cwin.at[1, 1]), (shift, shift_s),
        (owner, own_v), (line_row, row_v)]
    loads = [pltpu.make_async_copy(s, d, loc_sem.at[i]) for i, (s, d) in enumerate(loads)]
    for c in loads:
        c.start()
    for c in loads:
        c.wait()

    row8 = lax.broadcasted_iota(jnp.int32, (ri, nz), 0)
    sh = jnp.zeros((ri, nz), F32)
    for i in range(ri):
        sh = jnp.where(row8 == i, shift_s[i].astype(F32), sh)
    cwin[1, 2] = sh

    lane = lax.broadcasted_iota(jnp.int32, (cx, cy, nz), 2)
    first, last = lane == 0, lane == nz - 1

    def z_dn(a):
        return jnp.where(first[:, :a.shape[1]], a, roll(a, 1, 2))

    def z_change(u, f, largest):
        low = face(None if f is None else z_dn(f), f, z_dn(u), u, largest)
        top = jnp.zeros_like(u) if f is None else f
        high = jnp.where(last[:, :u.shape[1]], top, roll(low, -1, 2))
        return high - low

    prim = [win[v, 1:1 + cx, PAD:PAD + cy, :] for v in ORDER]
    terms = cell_terms(prim)
    win[8, 1:1 + cx, PAD:PAD + cy, :] = speed_of(prim, terms, 0)
    for v in (5, 6):
        win[v + 4, 1:1 + cx, PAD:PAD + cy, :] = prim[v] * prim[1] - prim[4] * prim[v - 3]
    flux, speed = flux_of(prim, terms, 2), speed_of(prim, terms, 2)
    largest = jnp.maximum(speed, z_dn(speed))
    for v in range(8):
        out[v] = terms[0][v] - COURANT * z_change(terms[0][v], flux[v], largest)

    pl.semaphore_wait(barrier, 3 * (jnp.minimum(g + 2, nx - 1) - jnp.maximum(g - 2, 0) + 1) + 2 + at_end.astype(jnp.int32))
    for r in doubling[:1]:
        pass_on(r)

    def remote(src, dst, send, recv, where):
        return pltpu.make_async_remote_copy(
            src_ref=src, dst_ref=dst, send_sem=send, recv_sem=recv,
            device_id=where, device_id_type=MESH)

    g_up, g_dn = jnp.minimum(g + 1, nx - 1), jnp.maximum(g - 1, 0)
    p_up, p_dn = jnp.minimum(p + 1, ny - 1), jnp.maximum(p - 1, 0)
    has_xu, has_xd, has_yu, has_yd = g < nx - 1, g > 0, p < ny - 1, p > 0

    def each(cond, copies, act):
        @pl.when(cond)
        def _():
            for c in copies:
                getattr(c, act)()

    def x_pair(at, count, send, recv):
        return [
            remote(win.at[pl.ds(at, count), s, rows], win.at[pl.ds(at, count), d, rows],
                   send.at[way], recv.at[way], (where, p))
            for way, (s, d, where) in enumerate(((cx, 0, g_up), (1, cx + 1, g_dn)))]

    xc = x_pair(5, 6, xs, xr)
    xlate = x_pair(0, 5, ls, lr)
    yc = [
        remote(win.at[pl.ds(0, 8), mid, pl.ds(s, PAD)], win.at[pl.ds(0, 8), mid, pl.ds(d, PAD)],
               ys.at[way], yr.at[way], (g, where))
        for way, (s, d, where) in enumerate(((cy, 0, p_up), (PAD, PAD + cy, p_dn)))]
    diag = []
    for i, (xu, yu) in enumerate(((1, 1), (1, 0), (0, 1), (0, 0))):
        s_x, d_x, to_g = (cx, 0, g_up) if xu else (1, cx + 1, g_dn)
        s_y, d_y, to_p = (PAD + cy - 1, PAD - 1, p_up) if yu else (PAD, PAD + cy, p_dn)
        c = remote(win.at[pl.ds(0, 8), s_x, pl.ds(s_y, 1)], win.at[pl.ds(0, 8), d_x, pl.ds(d_y, 1)],
                   ds.at[i], dr.at[i], (to_g, to_p))
        to = (has_xu if xu else has_xd) & (has_yu if yu else has_yd)
        come = (has_xd if xu else has_xu) & (has_yd if yu else has_yu)
        diag.append((c, to, come))
    ion = [
        (lax.rem(b + 1, n), 0),
        (lax.rem(b + n - 1, n), 2),
        (lax.rem(b + half + 1, n), 3),
        (lax.rem(b + half, n), 4),
        (lax.rem(b + half + n - 1, n), 5),
    ]
    cond_copies = [
        remote(cwin.at[1, pl.ds(0, 3 if slot < 3 else 2)], cwin.at[slot, pl.ds(0, 3 if slot < 3 else 2)],
               cs.at[slot], cr.at[slot], dev(flat)) for flat, slot in ion]

    each(has_yu, yc[:1], "start")
    each(has_yd, yc[1:], "start")
    for c, to, _ in diag:
        each(to, [c], "start")
    each(has_xu, xc[:1], "start")
    each(has_xd, xc[1:], "start")
    for c in cond_copies:
        c.start()

    each(has_yd, yc[:1], "wait_recv")
    each(has_yu, yc[1:], "wait_recv")

    @pl.when(p == 0)
    def _():
        for v in range(8):
            win[v, 1:1 + cx, PAD - 1:PAD, :] = win[v, 1:1 + cx, PAD:PAD + 1, :]

    @pl.when(p == ny - 1)
    def _():
        for v in range(8):
            win[v, 1:1 + cx, PAD + cy:PAD + cy + 1, :] = win[v, 1:1 + cx, PAD + cy - 1:PAD + cy, :]

    def x_inner(values, u, f):
        if cx == 1:
            return values
        speed = win[8, 1:1 + cx, PAD:PAD + cy, :]
        lows = face(None if f is None else f[:-1], None if f is None else f[1:], u[:-1], u[1:],
                    jnp.maximum(speed[:-1], speed[1:]))
        none = jnp.zeros_like(lows[:1])
        return values - COURANT * (jnp.concatenate([lows, none], 0) - jnp.concatenate([none, lows], 0))

    prim = [win[v, 1:1 + cx] for v in ORDER]
    terms = cell_terms(prim)
    flux, speed = flux_of(prim, terms, 1), speed_of(prim, terms, 1)
    largest = jnp.maximum(speed, roll(speed, 1, 1))

    def y_change(v):
        u, f = terms[0][v], flux[v]
        low = face(None if f is None else roll(f, 1, 1), f, roll(u, 1, 1), u, largest)
        return roll(low, -1, 1) - low

    def ends(a):
        return jnp.concatenate([a[:, :PAD], a[:, PAD + cy:]], axis=1)

    side = {}
    for v in (5, 6, 4):
        diff = y_change(v)
        if v != 5:
            side[v] = ends(diff)
        u = win[v + 1, 1:1 + cx, PAD:PAD + cy, :]
        f = None if v == 4 else win[v + 4, 1:1 + cx, PAD:PAD + cy, :]
        done = x_inner(out[v] - COURANT * diff[:, PAD:PAD + cy, :], u, f)
        if v == 4:
            out[v] = done
        else:
            pstage[v - 5] = done
        if v == 6:
            pc = [
                remote(pstage.at[:, s], pin.at[way], ps.at[way], pr.at[way], (where, p))
                for way, (s, where) in enumerate(((cx - 1, g_up), (0, g_dn)))]
            each(has_xu, pc[:1], "start")
            each(has_xd, pc[1:], "start")
    for at, r in enumerate(doubling[:-1]):
        hear(r)
        pass_on(doubling[at + 1])
    for v in (0, 1, 2, 3, 7):
        out[v] = out[v] - COURANT * y_change(v)[:, PAD:PAD + cy, :]

    for c, _, come in diag:
        each(come, [c], "wait_recv")

    def edge_planes(which, at, count):
        at = pl.ds(at, count)

        @pl.when(g == 0)
        def _():
            for v in which:
                win[v, 0, at, :] = win[v, 1, at, :]

        @pl.when(g == nx - 1)
        def _():
            for v in which:
                win[v, cx + 1, at, :] = win[v, cx, at, :]

    edge_planes(range(8), 0, PAD)
    edge_planes(range(8), PAD + cy, PAD)
    prim = [jnp.concatenate([win[v, :, :PAD, :], win[v, :, PAD + cy:, :]], axis=1) for v in ORDER]
    terms = cell_terms(prim)
    own = [a[1:1 + cx] for a in prim]
    speed_z = speed_of(own, (None, None, None, terms[3][1:1 + cx], terms[4][1:1 + cx]), 2)
    largest_z = jnp.maximum(speed_z, z_dn(speed_z))
    speed_x = speed_of(prim, terms, 0)
    largest_x = jnp.maximum(speed_x[:-1], speed_x[1:])
    for v in (4, 6):
        u = prim[v]
        fz = None if v == 6 else own[v] * own[3] - own[6] * own[v - 3]
        fx = None if v == 4 else u * prim[1] - prim[4] * prim[v - 3]
        lows = face(None if fx is None else fx[:-1], None if fx is None else fx[1:], u[:-1], u[1:], largest_x)
        new = own[v] - COURANT * (z_change(own[v], fz, largest_z) + side[v] + (lows[1:] - lows[:-1]))
        fwin[v // 6, :, 0:PAD, :] = new[:, :PAD]
        fwin[v // 6, :, PAD + cy:, :] = new[:, PAD:]

    each(has_xd, xc[:1], "wait_recv")
    each(has_xu, xc[1:], "wait_recv")
    for r in doubling[-1:]:
        hear(r)
    edge_planes(range(5, 11), PAD, cy)

    def outer_faces(v, f_of):
        faces = []
        for lo in (0, cx):
            u = [win[v + 1, lo + i, PAD:PAD + cy, :] for i in range(2)]
            f = [f_of(v, lo + i) for i in range(2)]
            most = jnp.maximum(win[8, lo, PAD:PAD + cy, :], win[8, lo + 1, PAD:PAD + cy, :])
            faces.append(COURANT * face(f[0], f[1], u[0], u[1], most))
        return faces

    def b_flux(v, at):
        return None if v == 4 else win[v + 4, at, PAD:PAD + cy, :]

    def close(values, faces):
        planes = [values[i] for i in range(cx)]
        planes[0] = planes[0] + faces[0]
        planes[-1] = planes[-1] - faces[1]
        return planes

    field, outer = {}, {}
    for v in (4, 6, 5):
        outer[v] = outer_faces(v, b_flux)
        field[v] = close(out[v] if v == 4 else pstage[v - 5], outer[v])
        for i in range(cx):
            out[v, i] = field[v][i]
            if v != 5:
                fwin[v // 6, i, PAD:PAD + cy, :] = field[v][i]

    @pl.when(p == 0)
    def _():
        fwin[:, :, PAD - 1:PAD, :] = fwin[:, :, PAD:PAD + 1, :]

    @pl.when(p == ny - 1)
    def _():
        fwin[:, :, PAD + cy:PAD + cy + 1, :] = fwin[:, :, PAD + cy - 1:PAD + cy, :]

    def d_y(v):
        a = fwin[v // 6]
        return 0.5 * (roll(a, -1, 1) - roll(a, 1, 1))[:, PAD:PAD + cy, :]

    def d_z(a):
        return 0.5 * (jnp.where(last, a, roll(a, -1, 2)) - z_dn(a))

    bx, by, bz = [jnp.stack(field[v]) for v in (4, 5, 6)]
    jx = d_y(6) - d_z(by)
    size = jnp.sqrt(bx * bx + by * by + bz * bz)
    dzx, dyx = d_z(bx), d_y(4)

    each(has_xd, pc[:1], "wait_recv")
    each(has_xu, pc[1:], "wait_recv")

    def d_x(v):
        lo = jnp.where(g == 0, field[v][0], pin[0, v - 5] - outer[v][0])
        hi = jnp.where(g == nx - 1, field[v][-1], pin[1, v - 5] + outer[v][1])
        a = jnp.stack([lo] + field[v] + [hi])
        return 0.5 * (a[2:] - a[:-2])

    jy = dzx - d_x(6)
    jz = d_x(5) - dyx
    current = (jx * bx + jy * by + jz * bz) / jnp.maximum(size, 1.0)
    current = current.reshape(cx * cy, nz)

    key = own_v[0] * ri + row_v[...]
    at = lax.broadcasted_iota(jnp.int32, (nx * ri, cx * cy), 0)
    pair, rest = at // (2 * ri), at % (2 * ri)
    hot = (key == (pair + (rest // ri) * pairs) * ri + rest % ri).astype(BF16)
    head = current.astype(BF16)
    tail = current - head.astype(F32)
    body_ = tail.astype(BF16)
    tail = (tail - body_.astype(F32)).astype(BF16)
    sums = jnp.dot(jnp.concatenate([hot, hot, hot], axis=1), jnp.concatenate([head, body_, tail], axis=0),
                   preferred_element_type=F32)
    part[...] = sums.reshape(pairs, 2, ri, nz)

    odd = lax.rem(p, 2)
    mate = (g, p + 1 - 2 * odd)
    out_g, out_p = jnp.where(odd == 1, beside[1][0], beside[-1][0]), jnp.where(odd == 1, beside[1][1], beside[-1][1])
    step = lax.rem(out_g - g + nx, nx)

    def own_copy(to):
        return remote(part.at[lax.rem(to, pairs)], part_in.at[0, g], as_.at[0], ar.at[0], (to, p))

    def outer_copy(to, first_row):
        some = pl.ds(first_row, ri - 1)
        return remote(part.at[lax.rem(to, pairs), :, some], part_in.at[1, g, :, some], as_.at[1], ar.at[1],
                      (lax.rem(to + step, nx), out_p))

    def send_own(k, carry):
        own_copy(lax.rem(g + k, nx)).start()
        return carry

    def send_outer(first_row):
        def send(k, carry):
            outer_copy(lax.rem(g + k, nx), first_row).start()
            return carry

        lax.fori_loop(0, nx, send, 0, unroll=nx <= 8)

    lax.fori_loop(1, nx, send_own, 0, unroll=nx <= 8)
    pl.when(odd == 1)(lambda: send_outer(1))
    pl.when(odd == 0)(lambda: send_outer(0))
    each(has_xu, xlate[:1], "start")
    each(has_xd, xlate[1:], "start")

    for c in cond_copies:
        c.wait_recv()
    lines = 6 * ri
    row = lax.broadcasted_iota(jnp.int32, (lines, nz), 0)
    row = jnp.where(row >= 3 * ri, row - 3 * ri, row)
    place = lax.rem(b, half)
    low_row = jnp.where(place == half // 2, ri, 0)
    high_row = jnp.where(place == half // 2 - 1, 2 * ri, 3 * ri)
    valid = (row >= low_row) & (row < high_row)
    pw = jnp.where(valid, cwin[:, 0].reshape(lines, nz), 0.0)
    hw = jnp.where(valid, cwin[:, 1].reshape(lines, nz), 0.0)
    own_shift = cwin[0:3, 2].reshape(3 * ri, nz).astype(jnp.int32)
    col = lax.broadcasted_iota(jnp.int32, (3 * ri, nz), 1)
    cols = jnp.concatenate(
        [(col + own_shift) % nz, (col + (nz - own_shift)) % nz], axis=0)
    he, hwst = east(hw), west(hw)
    coef = [
        0.5 * (pw + up(pw)), 0.5 * (pw + down(pw)),
        0.5 * (pw + east(pw)), 0.5 * (pw + west(pw)),
        0.125 * (hw + up(he)), 0.125 * (hw + up(hwst)),
        0.125 * (hw + down(he)), 0.125 * (hw + down(hwst)),
    ]
    center = coef[0]
    for c in coef[1:]:
        center = center + c
    inv = jnp.where(valid, 1.0 / jnp.where(valid, center, 1.0), 0.0)
    pm = swap_by(cols, pw)
    both = jnp.where(valid, pw + pm, 1.0)
    for i, c in enumerate(coef):
        coef_out[i] = c * inv
    coef_out[8] = inv
    coef_out[9] = jnp.where(valid, pw / both, 0.0)
    coef_out[10] = jnp.where(valid, pm / both, 0.0)
    cols_out[...] = cols

    def taken(slot, sems):
        some = part_in.at[slot, pl.ds(0, nx - 1 if slot == 0 else nx), :, pl.ds(0, ri if slot == 0 else ri - 1)]
        pltpu.make_async_copy(some, some, sems.at[slot]).wait()

    def total_of(slot):
        def add(at, total):
            return total + part_in[slot, at]
        return lax.fori_loop(1, nx, add, part_in[slot, 0], unroll=nx <= 8)

    taken(0, ar)
    part_in[0, g] = part[lax.rem(g, pairs)]
    shared[0] = total_of(0)
    to_mate = remote(shared.at[0], shared.at[1], hs.at[0], hr.at[0], mate)
    to_mate.start()
    def planes(v):
        return win[v, :, PAD:PAD + cy, :]

    each(has_xd, xlate[:1], "wait_recv")
    each(has_xu, xlate[1:], "wait_recv")
    edge_planes(range(5), PAD, cy)
    prim = [planes(v) for v in ORDER]
    terms = cell_terms(prim)
    flux = flux_of(prim, terms, 0)
    speed = planes(8)
    largest = jnp.maximum(speed[:-1], speed[1:])
    for v in (0, 1, 2, 3, 7):
        u, f = terms[0][v], flux[v]
        lows = face(f[:-1], f[1:], u[:-1], u[1:], largest)
        out[v] = out[v] - COURANT * (lows[1:] - lows[:-1])

    taken(1, ar)
    outer_sum = total_of(1)
    to_mate.wait_recv()

    def place_sums(slot, total, block):
        northern = block < half
        src_out[0, slot] = jnp.where(northern, total[0], total[1])
        src_out[1, slot] = jnp.where(northern, total[1], total[0])

    mate_sum = shared[1]
    place_sums(0, jnp.where(odd == 1, mate_sum, outer_sum), lax.rem(b + n - 1, n))
    place_sums(1, shared[0], b)
    place_sums(2, jnp.where(odd == 1, outer_sum, mate_sum), lax.rem(b + 1, n))

    each(has_xu, [xc[0], xlate[0], pc[0]], "wait_send")
    each(has_xd, [xc[1], xlate[1], pc[1]], "wait_send")
    each(has_yu, yc[:1], "wait_send")
    each(has_yd, yc[1:], "wait_send")
    for c, to, _ in diag:
        each(to, [c], "wait_send")
    for c in cond_copies:
        c.wait_send()
    to_mate.wait_send()
    taken(0, as_)
    taken(1, as_)


def sweep_kernel(con, src, coef, cols_ref, out, phi_out, phi_v, sems):
    write = pltpu.make_async_copy(con, out, sems.at[0])
    write.start()
    cu, cd, ce, cw, cue, cuw, cde, cdw, inv, wa, wb = [coef[i] for i in range(COEFS)]
    cols = cols_ref[...]
    ri = phi_v.shape[0]
    source = src[...].reshape(inv.shape) * inv

    def couple(phi):
        return wa * phi + wb * swap_by(cols, phi)

    wae, waw, wbe, wbw = east(wa), west(wa), east(wb), west(wb)
    colse, colsw = east(cols), west(cols)
    u0, u1, u2 = down(cu), down(cue), -down(cuw)
    d0, d1, d2 = up(cd), -up(cde), up(cdw)

    def triple(a):
        h = a.shape[0] // 2
        other = jnp.concatenate([a[h:], a[:h]], axis=0)
        take = lambda c: jnp.take_along_axis(other, c, axis=1)
        return wa * a + wb * take(cols), wae * east(a) + wbe * take(colse), waw * west(a) + wbw * take(colsw)

    acc = source
    for _ in range(SWEEPS - 1):
        phi, e, w = triple(acc)
        acc = (source + (ce * e + cw * w)) + (up(u0 * phi + u1 * e + u2 * w) + down(d0 * phi + d1 * e + d2 * w))
    phi = couple(acc)
    phi_v[...] = phi[ri:2 * ri]
    last = pltpu.make_async_copy(phi_v, phi_out, sems.at[1])
    last.start()
    write.wait()
    last.wait()


def body(sizes, density, velocity, magnetic, pressure, line_owner, line_row, pedersen, hall, mirror_shift):
    cx, cy, nz = density.shape
    ri = pedersen.shape[0]
    nx = sizes[0]
    any_ = pl.BlockSpec(memory_space=pl.ANY)
    vmem = pl.BlockSpec(memory_space=pltpu.VMEM)
    dma = pltpu.SemaphoreType.DMA
    con, src, coef, cols = pl.pallas_call(
        functools.partial(flux_kernel, sizes),
        out_shape=(
            pltpu.VMEM((8, cx, cy, nz), F32),
            pltpu.VMEM((2, 3, ri, nz), F32),
            pltpu.VMEM((COEFS, 6 * ri, nz), F32),
            pltpu.VMEM((6 * ri, nz), jnp.int32),
        ),
        in_specs=[any_] * 9,
        out_specs=(vmem,) * 4,
        scratch_shapes=[
            pltpu.VMEM((11, cx + 2, cy + 2 * PAD, nz), F32),
            pltpu.VMEM((2, cx, cy + 2 * PAD, nz), F32),
            pltpu.VMEM((2, cx, cy, nz), F32),
            pltpu.VMEM((2, 2, cy, nz), F32),
            pltpu.VMEM((nx // 2, 2, ri, nz), F32),
            pltpu.VMEM((2, nx, 2, ri, nz), F32),
            pltpu.VMEM((2, 2, ri, nz), F32),
            pltpu.VMEM((6, 3, ri, nz), F32),
            pltpu.VMEM((1, 1, cx * cy), jnp.int32),
            pltpu.VMEM((1, cx * cy), jnp.int32),
            pltpu.SMEM((ri,), jnp.int32),
            dma((9,)),
            dma((2,)), dma((2,)), dma((2,)), dma((2,)), dma((2,)), dma((2,)),
            dma((4,)), dma((4,)), dma((2,)), dma((2,)), dma((6,)), dma((6,)),
            dma((2,)), dma((2,)), dma((1,)), dma((1,)),
            pltpu.SemaphoreType.REGULAR((8,)),
        ],
        compiler_params=pltpu.CompilerParams(collective_id=0, has_side_effects=True),
        name="flux_and_sources",
    )(density, velocity, magnetic, pressure, line_owner.reshape(1, 1, cx * cy), line_row.reshape(1, cx * cy),
      pedersen, hall, mirror_shift)
    return pl.pallas_call(
        sweep_kernel,
        out_shape=(
            jax.ShapeDtypeStruct((8, cx, cy, nz), F32),
            jax.ShapeDtypeStruct((ri, nz), F32),
        ),
        in_specs=[vmem] * 4,
        out_specs=(any_, any_),
        scratch_shapes=[pltpu.VMEM((ri, nz), F32), dma((2,))],
        name="sweeps",
    )(*[pltpu.with_memory_space_constraint(a, pltpu.VMEM) for a in (con, src, coef, cols)])


def solution(mesh):
    sizes = (mesh.shape["gx"], mesh.shape["pb"])
    in_specs = (
        P("gx", "pb", None),
        P(None, "gx", "pb", None),
        P(None, "gx", "pb", None),
        P("gx", "pb", None),
        P("gx", "pb", None, None),
        P("gx", "pb", None),
        P(("gx", "pb"), None),
        P(("gx", "pb"), None),
        P(("gx", "pb")),
    )
    out_specs = (P(None, "gx", "pb", None), P(("gx", "pb"), None))
    return jax.shard_map(
        functools.partial(body, sizes), mesh=mesh, in_specs=in_specs, out_specs=out_specs,
        check_vma=False)
```

```python
import functools

import jax
import jax.numpy as jnp
from jax import lax
from jax.experimental import pallas as pl
from jax.experimental.pallas import tpu as pltpu
from jax.sharding import PartitionSpec as P

SWEEPS = 8
GAMMA = 5.0 / 3.0
COURANT = 0.08
PAD = 8
COEFS = 11
F32 = jnp.float32
BF16 = jnp.bfloat16
MESH = pl.DeviceIdType.MESH
ORDER = (0, 2, 3, 4, 6, 5, 7, 1)
FIELD = {4: 6, 5: 5, 6: 7}
SPEED = 8
FLUX = {6: 9, 5: 10}


def cell_terms(prim):
    rho, vel, mag, pres = prim[0], prim[1:4], prim[4:7], prim[7]
    field_sq = mag[0] * mag[0] + mag[1] * mag[1] + mag[2] * mag[2]
    vel_sq = vel[0] * vel[0] + vel[1] * vel[1] + vel[2] * vel[2]
    half_sq = 0.5 * field_sq
    energy = pres * (1.0 / (GAMMA - 1.0)) + 0.5 * rho * vel_sq + half_sq
    total_p = pres + half_sq
    v_dot_b = vel[0] * mag[0] + vel[1] * mag[1] + vel[2] * mag[2]
    inv = 1.0 / rho
    sound_sq = GAMMA * pres * inv
    both = sound_sq + field_sq * inv
    momentum = [rho * v for v in vel]
    state = [rho] + momentum + list(mag) + [energy]
    return state, total_p, v_dot_b, sound_sq * inv, both


def flux_of(prim, terms, d):
    state, total_p, v_dot_b = terms[:3]
    vel, mag = prim[1:4], prim[4:7]
    vn, bn = vel[d], mag[d]
    flux = [state[1 + d]]
    for e in range(3):
        m = state[1 + e] * vn - mag[e] * bn
        flux.append(m + total_p if e == d else m)
    for e in range(3):
        flux.append(None if e == d else mag[e] * vn - bn * vel[e])
    flux.append((state[7] + total_p) * vn - bn * v_dot_b)
    return flux


def speed_of(prim, terms, d):
    sound_over, both = terms[3:]
    vn, bn = prim[1 + d], prim[4 + d]
    spread = both * both - 4.0 * sound_over * bn * bn
    fast = jnp.sqrt(0.5 * (both + jnp.sqrt(jnp.maximum(spread, 0.0))))
    return jnp.abs(vn) + fast


def face(f_lo, f_hi, u_lo, u_hi, largest):
    jump = largest * (u_hi - u_lo)
    return -0.5 * jump if f_lo is None else 0.5 * ((f_lo + f_hi) - jump)


def roll(values, shift, axis):
    return pltpu.roll(values, shift % values.shape[axis], axis)


def east(a):
    return roll(a, -1, 1)


def west(a):
    return roll(a, 1, 1)


def up(a):
    return roll(a, 1, 0)


def down(a):
    return roll(a, -1, 0)


def swap_by(cols, a):
    h = a.shape[0] // 2
    other = jnp.concatenate([a[h:], a[:h]], axis=0)
    return jnp.take_along_axis(other, cols, axis=1)


def flux_kernel(sizes, rho, vel, mag, pres, owner, line_row, ped, hall, shift,
                out, src_out, coef_out, cols_out,
                win, fwin, pstage, pin, edge, part, part_in, shared, cwin, own_v, row_v, shift_s,
                loc_sem, xs, xr, ls, lr, ys, yr, ds, dr, ps, pr, cs, cr, as_, ar, hs, hr, far):
    nx, ny = sizes
    cx, cy, nz = rho.shape
    ri = ped.shape[0]
    g, p = lax.axis_index("gx"), lax.axis_index("pb")
    n = nx * ny
    half = n // 2
    pairs = nx // 2
    b = g * ny + p
    wide = cy + 2 * PAD

    def dev(flat):
        return (lax.div(flat, ny), lax.rem(flat, ny))

    beside = {o: dev(lax.rem(b + o + n, n)) for o in (-1, 1)}

    barrier = pltpu.get_barrier_semaphore()

    for dg in (1, -1, 0, 2, -2):
        inside = (g + dg >= 0) & (g + dg < nx)

        @pl.when(inside)
        def _(to=jnp.clip(g + dg, 0, nx - 1), same=dg == 0):
            for o in (0, 1, -1):
                if o or not same:
                    pl.semaphore_signal(
                        barrier, inc=1, device_id=(to, beside[o][1] if o else p), device_id_type=MESH)

    for o in (0, 1, -1):
        pl.semaphore_signal(barrier, inc=1, device_id=dev(lax.rem(b + half + o, n)), device_id_type=MESH)
    at_end = (b == 0) | (b == n - 1)

    @pl.when(at_end)
    def _():
        pl.semaphore_signal(barrier, inc=1, device_id=dev(n - 1 - b), device_id_type=MESH)

    doubling = [1 << i for i in range(1, 32) if 1 << i < nx]

    def pass_on(r):
        for to in (g + r, g - r):
            @pl.when((to >= 0) & (to < nx))
            def _(to=jnp.clip(to, 0, nx - 1), at=doubling.index(r)):
                pl.semaphore_signal(far.at[at], inc=1, device_id=(to, p), device_id_type=MESH)

    def hear(r):
        count = (g + r < nx).astype(jnp.int32) + (g - r >= 0).astype(jnp.int32)
        pl.semaphore_wait(far.at[doubling.index(r)], count)

    rows = pl.ds(PAD, cy)
    mid = pl.ds(1, cx)
    loads = [
        (rho, win.at[0, mid, rows]), (vel, win.at[pl.ds(2, 3), mid, rows]),
        (pres, win.at[1, mid, rows]),
        (ped, cwin.at[1, 0]), (hall, cwin.at[1, 1]), (shift, shift_s),
        (owner, own_v), (line_row, row_v)]
    loads += [(mag.at[v - 4], win.at[FIELD[v], mid, rows]) for v in FIELD]
    loads = [pltpu.make_async_copy(s, d, loc_sem.at[i]) for i, (s, d) in enumerate(loads)]
    for c in loads:
        c.start()
    for c in loads:
        c.wait()

    row8 = lax.broadcasted_iota(jnp.int32, (ri, nz), 0)
    sh = jnp.zeros((ri, nz), F32)
    for i in range(ri):
        sh = jnp.where(row8 == i, shift_s[i].astype(F32), sh)
    cwin[1, 2] = sh

    lane = lax.broadcasted_iota(jnp.int32, (cx, cy, nz), 2)
    first, last = lane == 0, lane == nz - 1

    def z_dn(a):
        return jnp.where(first[:, :a.shape[1]], a, roll(a, 1, 2))

    def z_change(u, f, largest):
        low = face(None if f is None else z_dn(f), f, z_dn(u), u, largest)
        top = jnp.zeros_like(u) if f is None else f
        high = jnp.where(last[:, :u.shape[1]], top, roll(low, -1, 2))
        return high - low

    prim = [win[v, 1:1 + cx, PAD:PAD + cy, :] for v in ORDER]
    terms = cell_terms(prim)
    win[SPEED, 1:1 + cx, PAD:PAD + cy, :] = speed_of(prim, terms, 0)
    for v in FLUX:
        win[FLUX[v], 1:1 + cx, PAD:PAD + cy, :] = prim[v] * prim[1] - prim[4] * prim[v - 3]
    flux, speed = flux_of(prim, terms, 2), speed_of(prim, terms, 2)
    largest = jnp.maximum(speed, z_dn(speed))
    for v in range(8):
        out[v] = terms[0][v] - COURANT * z_change(terms[0][v], flux[v], largest)

    pl.semaphore_wait(barrier, 3 * (jnp.minimum(g + 2, nx - 1) - jnp.maximum(g - 2, 0) + 1) + 2 + at_end.astype(jnp.int32))
    for r in doubling[:1]:
        pass_on(r)

    def remote(src, dst, send, recv, where):
        return pltpu.make_async_remote_copy(
            src_ref=src, dst_ref=dst, send_sem=send, recv_sem=recv,
            device_id=where, device_id_type=MESH)

    g_up, g_dn = jnp.minimum(g + 1, nx - 1), jnp.maximum(g - 1, 0)
    p_up, p_dn = jnp.minimum(p + 1, ny - 1), jnp.maximum(p - 1, 0)
    has_xu, has_xd, has_yu, has_yd = g < nx - 1, g > 0, p < ny - 1, p > 0

    def each(cond, copies, act):
        @pl.when(cond)
        def _():
            for c in copies:
                getattr(c, act)()

    def x_pair(at, count, send, recv):
        return [
            remote(win.at[pl.ds(at, count), s, rows], win.at[pl.ds(at, count), d, rows],
                   send.at[way], recv.at[way], (where, p))
            for way, (s, d, where) in enumerate(((cx, 0, g_up), (1, cx + 1, g_dn)))]

    xc = x_pair(5, 6, xs, xr)
    xlate = x_pair(0, 5, ls, lr)
    yc = [
        remote(win.at[pl.ds(0, 8), mid, pl.ds(s, PAD)], win.at[pl.ds(0, 8), mid, pl.ds(d, PAD)],
               ys.at[way], yr.at[way], (g, where))
        for way, (s, d, where) in enumerate(((cy, 0, p_up), (PAD, PAD + cy, p_dn)))]
    diag = []
    for i, (xu, yu) in enumerate(((1, 1), (1, 0), (0, 1), (0, 0))):
        s_x, d_x, to_g = (cx, 0, g_up) if xu else (1, cx + 1, g_dn)
        s_y, d_y, to_p = (PAD + cy - 1, PAD - 1, p_up) if yu else (PAD, PAD + cy, p_dn)
        c = remote(win.at[pl.ds(6, 4), s_x, pl.ds(s_y, 1)], win.at[pl.ds(6, 4), d_x, pl.ds(d_y, 1)],
                   ds.at[i], dr.at[i], (to_g, to_p))
        to = (has_xu if xu else has_xd) & (has_yu if yu else has_yd)
        come = (has_xd if xu else has_xu) & (has_yd if yu else has_yu)
        diag.append((c, to, come))
    ion = [
        (lax.rem(b + 1, n), 0),
        (lax.rem(b + n - 1, n), 2),
        (lax.rem(b + half + 1, n), 3),
        (lax.rem(b + half, n), 4),
        (lax.rem(b + half + n - 1, n), 5),
    ]
    cond_copies = [
        remote(cwin.at[1, pl.ds(0, 3 if slot < 3 else 2)], cwin.at[slot, pl.ds(0, 3 if slot < 3 else 2)],
               cs.at[slot], cr.at[slot], dev(flat)) for flat, slot in ion]

    each(has_yu, yc[:1], "start")
    each(has_yd, yc[1:], "start")
    for c, to, _ in diag:
        each(to, [c], "start")
    each(has_xu, xc[:1], "start")
    each(has_xd, xc[1:], "start")
    for c in cond_copies:
        c.start()

    each(has_yd, yc[:1], "wait_recv")
    each(has_yu, yc[1:], "wait_recv")

    @pl.when(p == 0)
    def _():
        for v in range(8):
            win[v, 1:1 + cx, PAD - 1:PAD, :] = win[v, 1:1 + cx, PAD:PAD + 1, :]

    @pl.when(p == ny - 1)
    def _():
        for v in range(8):
            win[v, 1:1 + cx, PAD + cy:PAD + cy + 1, :] = win[v, 1:1 + cx, PAD + cy - 1:PAD + cy, :]

    def x_inner(values, u, f):
        if cx == 1:
            return values
        speed = win[SPEED, 1:1 + cx, PAD:PAD + cy, :]
        lows = face(None if f is None else f[:-1], None if f is None else f[1:], u[:-1], u[1:],
                    jnp.maximum(speed[:-1], speed[1:]))
        none = jnp.zeros_like(lows[:1])
        return values - COURANT * (jnp.concatenate([lows, none], 0) - jnp.concatenate([none, lows], 0))

    prim = [win[v, 1:1 + cx] for v in ORDER]
    terms = cell_terms(prim)
    flux, speed = flux_of(prim, terms, 1), speed_of(prim, terms, 1)
    largest = jnp.maximum(speed, roll(speed, 1, 1))

    def y_change(v):
        u, f = terms[0][v], flux[v]
        low = face(None if f is None else roll(f, 1, 1), f, roll(u, 1, 1), u, largest)
        return roll(low, -1, 1) - low

    def ends(a):
        return jnp.concatenate([a[:, :PAD], a[:, PAD + cy:]], axis=1)

    side = {}
    for v in (5, 6, 4):
        diff = y_change(v)
        if v != 5:
            side[v] = ends(diff)
        u = win[FIELD[v], 1:1 + cx, PAD:PAD + cy, :]
        f = None if v == 4 else win[FLUX[v], 1:1 + cx, PAD:PAD + cy, :]
        done = x_inner(out[v] - COURANT * diff[:, PAD:PAD + cy, :], u, f)
        if v == 4:
            out[v] = done
        else:
            pstage[v - 5] = done
        if v == 6:
            pc = [
                remote(pstage.at[:, s], pin.at[way], ps.at[way], pr.at[way], (where, p))
                for way, (s, where) in enumerate(((cx - 1, g_up), (0, g_dn)))]
            each(has_xu, pc[:1], "start")
            each(has_xd, pc[1:], "start")
    for at, r in enumerate(doubling[:-1]):
        hear(r)
        pass_on(doubling[at + 1])
    for v in (0, 1, 2, 3, 7):
        out[v] = out[v] - COURANT * y_change(v)[:, PAD:PAD + cy, :]

    for c, _, come in diag:
        each(come, [c], "wait_recv")

    def edge_planes(which, at, count):
        at = pl.ds(at, count)

        @pl.when(g == 0)
        def _():
            for v in which:
                win[v, 0, at, :] = win[v, 1, at, :]

        @pl.when(g == nx - 1)
        def _():
            for v in which:
                win[v, cx + 1, at, :] = win[v, cx, at, :]

    def tiles(v, at):
        return jnp.concatenate([win[v, at, :PAD, :], win[v, at, PAD + cy:, :]], axis=1)

    own = [tiles(v, slice(1, 1 + cx)) for v in ORDER]
    terms = cell_terms(own)
    for v, value in ((SPEED, speed_of(own, terms, 0)), (FLUX[6], own[6] * own[1] - own[4] * own[3])):
        win[v, 1:1 + cx, :PAD, :] = value[:, :PAD]
        win[v, 1:1 + cx, PAD + cy:, :] = value[:, PAD:]
    edge_planes(range(6, 10), 0, PAD)
    edge_planes(range(6, 10), PAD + cy, PAD)
    speed_z = speed_of(own, terms, 2)
    largest_z = jnp.maximum(speed_z, z_dn(speed_z))
    around = slice(0, cx + 2)
    speed_x = tiles(SPEED, around)
    largest_x = jnp.maximum(speed_x[:-1], speed_x[1:])
    for v in (4, 6):
        u = tiles(FIELD[v], around)
        fz = None if v == 6 else own[v] * own[3] - own[6] * own[v - 3]
        fx = None if v == 4 else tiles(FLUX[v], around)
        lows = face(None if fx is None else fx[:-1], None if fx is None else fx[1:], u[:-1], u[1:], largest_x)
        new = own[v] - COURANT * (z_change(own[v], fz, largest_z) + side[v] + (lows[1:] - lows[:-1]))
        fwin[v // 6, :, 0:PAD, :] = new[:, :PAD]
        fwin[v // 6, :, PAD + cy:, :] = new[:, PAD:]

    key = own_v[0] * ri + row_v[...]
    at = lax.broadcasted_iota(jnp.int32, (nx * ri, cx * cy), 0)
    pair, rest = at // (2 * ri), at % (2 * ri)
    hot = (key == (pair + (rest // ri) * pairs) * ri + rest % ri).astype(BF16)
    hot = jnp.concatenate([hot, hot, hot], axis=1)

    each(has_xd, xc[:1], "wait_recv")
    each(has_xu, xc[1:], "wait_recv")
    for r in doubling[-1:]:
        hear(r)
    edge_planes(range(5, 11), PAD, cy)

    def outer_faces(v, f_of):
        faces = []
        for lo in (0, cx):
            u = [win[FIELD[v], lo + i, PAD:PAD + cy, :] for i in range(2)]
            f = [f_of(v, lo + i) for i in range(2)]
            most = jnp.maximum(win[SPEED, lo, PAD:PAD + cy, :], win[SPEED, lo + 1, PAD:PAD + cy, :])
            faces.append(COURANT * face(f[0], f[1], u[0], u[1], most))
        return faces

    def b_flux(v, at):
        return None if v == 4 else win[FLUX[v], at, PAD:PAD + cy, :]

    def close(values, faces):
        planes = [values[i] for i in range(cx)]
        planes[0] = planes[0] + faces[0]
        planes[-1] = planes[-1] - faces[1]
        return planes

    field, outer = {}, {}
    for v in (4, 6, 5):
        outer[v] = outer_faces(v, b_flux)
        field[v] = close(out[v] if v == 4 else pstage[v - 5], outer[v])
        for i in range(cx):
            out[v, i] = field[v][i]
            if v != 5:
                fwin[v // 6, i, PAD:PAD + cy, :] = field[v][i]

    @pl.when(p == 0)
    def _():
        fwin[:, :, PAD - 1:PAD, :] = fwin[:, :, PAD:PAD + 1, :]

    @pl.when(p == ny - 1)
    def _():
        fwin[:, :, PAD + cy:PAD + cy + 1, :] = fwin[:, :, PAD + cy - 1:PAD + cy, :]

    def d_y(v):
        a = fwin[v // 6]
        return 0.5 * (roll(a, -1, 1) - roll(a, 1, 1))[:, PAD:PAD + cy, :]

    def d_z(a):
        return 0.5 * (jnp.where(last, a, roll(a, -1, 2)) - z_dn(a))

    bx, by, bz = [jnp.stack(field[v]) for v in (4, 5, 6)]
    jx = d_y(6) - d_z(by)
    size = jnp.sqrt(bx * bx + by * by + bz * bz)
    dzx, dyx = d_z(bx), d_y(4)

    each(has_xd, pc[:1], "wait_recv")
    each(has_xu, pc[1:], "wait_recv")

    def d_x(v):
        lo = jnp.where(g == 0, field[v][0], pin[0, v - 5] - outer[v][0])
        hi = jnp.where(g == nx - 1, field[v][-1], pin[1, v - 5] + outer[v][1])
        a = jnp.stack([lo] + field[v] + [hi])
        return 0.5 * (a[2:] - a[:-2])

    jy = dzx - d_x(6)
    jz = d_x(5) - dyx
    current = (jx * bx + jy * by + jz * bz) / jnp.maximum(size, 1.0)
    current = current.reshape(cx * cy, nz)

    head = current.astype(BF16)
    tail = current - head.astype(F32)
    body_ = tail.astype(BF16)
    tail = (tail - body_.astype(F32)).astype(BF16)
    sums = jnp.dot(hot, jnp.concatenate([head, body_, tail], axis=0),
                   preferred_element_type=F32)
    part[...] = sums.reshape(pairs, 2, ri, nz)

    odd = lax.rem(p, 2)
    mate = (g, p + 1 - 2 * odd)
    out_g, out_p = jnp.where(odd == 1, beside[1][0], beside[-1][0]), jnp.where(odd == 1, beside[1][1], beside[-1][1])
    step = lax.rem(out_g - g + nx, nx)

    def own_copy(to):
        return remote(part.at[lax.rem(to, pairs)], part_in.at[0, g], as_.at[0], ar.at[0], (to, p))

    def outer_copy(to, first_row):
        some = pl.ds(first_row, ri - 1)
        return remote(part.at[lax.rem(to, pairs), :, some], part_in.at[1, g, :, some], as_.at[1], ar.at[1],
                      (lax.rem(to + step, nx), out_p))

    def send_own(k, carry):
        own_copy(lax.rem(g + k, nx)).start()
        return carry

    def send_outer(first_row):
        def send(k, carry):
            outer_copy(lax.rem(g + k, nx), first_row).start()
            return carry

        lax.fori_loop(0, nx, send, 0, unroll=nx <= 8)

    lax.fori_loop(1, nx, send_own, 0, unroll=nx <= 8)
    pl.when(odd == 1)(lambda: send_outer(1))
    pl.when(odd == 0)(lambda: send_outer(0))
    each(has_xu, xlate[:1], "start")
    each(has_xd, xlate[1:], "start")

    for c in cond_copies:
        c.wait_recv()
    lines = 6 * ri
    row = lax.broadcasted_iota(jnp.int32, (lines, nz), 0)
    row = jnp.where(row >= 3 * ri, row - 3 * ri, row)
    place = lax.rem(b, half)
    low_row = jnp.where(place == half // 2, ri, 0)
    high_row = jnp.where(place == half // 2 - 1, 2 * ri, 3 * ri)
    valid = (row >= low_row) & (row < high_row)
    pw = jnp.where(valid, cwin[:, 0].reshape(lines, nz), 0.0)
    hw = jnp.where(valid, cwin[:, 1].reshape(lines, nz), 0.0)
    own_shift = cwin[0:3, 2].reshape(3 * ri, nz).astype(jnp.int32)
    col = lax.broadcasted_iota(jnp.int32, (3 * ri, nz), 1)
    cols = jnp.concatenate(
        [(col + own_shift) % nz, (col + (nz - own_shift)) % nz], axis=0)
    he, hwst = east(hw), west(hw)
    coef = [
        0.5 * (pw + up(pw)), 0.5 * (pw + down(pw)),
        0.5 * (pw + east(pw)), 0.5 * (pw + west(pw)),
        0.125 * (hw + up(he)), 0.125 * (hw + up(hwst)),
        0.125 * (hw + down(he)), 0.125 * (hw + down(hwst)),
    ]
    center = coef[0]
    for c in coef[1:]:
        center = center + c
    inv = jnp.where(valid, 1.0 / jnp.where(valid, center, 1.0), 0.0)
    pm = swap_by(cols, pw)
    both = jnp.where(valid, pw + pm, 1.0)
    for i, c in enumerate(coef):
        coef_out[i] = c * inv
    coef_out[8] = inv
    coef_out[9] = jnp.where(valid, pw / both, 0.0)
    coef_out[10] = jnp.where(valid, pm / both, 0.0)
    cols_out[...] = cols

    rest = (0, 1, 2, 3, 7)
    prim = [win[v, 1:1 + cx, PAD:PAD + cy, :] for v in ORDER]
    terms = cell_terms(prim)
    flux = flux_of(prim, terms, 0)
    for at, v in enumerate(rest):
        out[v] = x_inner(out[v], terms[0][v], flux[v])
        for side_at, plane in enumerate((0, cx - 1)):
            edge[0, at, side_at] = terms[0][v][plane]
            edge[1, at, side_at] = flux[v][plane]

    def taken(slot, sems):
        some = part_in.at[slot, pl.ds(0, nx - 1 if slot == 0 else nx), :, pl.ds(0, ri if slot == 0 else ri - 1)]
        pltpu.make_async_copy(some, some, sems.at[slot]).wait()

    def total_of(slot):
        def add(at, total):
            return total + part_in[slot, at]
        return lax.fori_loop(1, nx, add, part_in[slot, 0], unroll=nx <= 8)

    taken(0, ar)
    part_in[0, g] = part[lax.rem(g, pairs)]
    shared[0] = total_of(0)
    to_mate = remote(shared.at[0], shared.at[1], hs.at[0], hr.at[0], mate)
    to_mate.start()
    each(has_xd, xlate[:1], "wait_recv")
    each(has_xu, xlate[1:], "wait_recv")

    def ghosts(v):
        return jnp.stack([win[v, at, PAD:PAD + cy, :] for at in (0, cx + 1)])

    prim = [ghosts(v) for v in ORDER]
    terms = cell_terms(prim)
    flux = flux_of(prim, terms, 0)
    speed = jnp.maximum(ghosts(SPEED), jnp.stack([win[SPEED, at, PAD:PAD + cy, :] for at in (1, cx)]))
    for at, v in enumerate(rest):
        u, f = terms[0][v], flux[v]
        own_u, own_f = edge[0, at], edge[1, at]
        low = face(f[0], own_f[0], u[0], own_u[0], speed[0])
        high = face(own_f[1], f[1], own_u[1], u[1], speed[1])
        low = jnp.where(g == 0, own_f[0], low)
        high = jnp.where(g == nx - 1, own_f[1], high)
        out[v, 0] = out[v, 0] + COURANT * low
        out[v, cx - 1] = out[v, cx - 1] - COURANT * high

    taken(1, ar)
    outer_sum = total_of(1)
    to_mate.wait_recv()

    def place_sums(slot, total, block):
        northern = block < half
        src_out[0, slot] = jnp.where(northern, total[0], total[1])
        src_out[1, slot] = jnp.where(northern, total[1], total[0])

    mate_sum = shared[1]
    place_sums(0, jnp.where(odd == 1, mate_sum, outer_sum), lax.rem(b + n - 1, n))
    place_sums(1, shared[0], b)
    place_sums(2, jnp.where(odd == 1, outer_sum, mate_sum), lax.rem(b + 1, n))

    each(has_xu, [xc[0], xlate[0], pc[0]], "wait_send")
    each(has_xd, [xc[1], xlate[1], pc[1]], "wait_send")
    each(has_yu, yc[:1], "wait_send")
    each(has_yd, yc[1:], "wait_send")
    for c, to, _ in diag:
        each(to, [c], "wait_send")
    for c in cond_copies:
        c.wait_send()
    to_mate.wait_send()
    taken(0, as_)
    taken(1, as_)


def sweep_kernel(con, src, coef, cols_ref, out, phi_out, phi_v, sems):
    write = pltpu.make_async_copy(con, out, sems.at[0])
    write.start()
    cu, cd, ce, cw, cue, cuw, cde, cdw, inv, wa, wb = [coef[i] for i in range(COEFS)]
    cols = cols_ref[...]
    ri = phi_v.shape[0]
    source = src[...].reshape(inv.shape) * inv

    def couple(phi):
        return wa * phi + wb * swap_by(cols, phi)

    wae, waw, wbe, wbw = east(wa), west(wa), east(wb), west(wb)
    colse, colsw = east(cols), west(cols)
    u0, u1, u2 = down(cu), down(cue), -down(cuw)
    d0, d1, d2 = up(cd), -up(cde), up(cdw)

    def triple(a):
        h = a.shape[0] // 2
        other = jnp.concatenate([a[h:], a[:h]], axis=0)
        take = lambda c: jnp.take_along_axis(other, c, axis=1)
        return wa * a + wb * take(cols), wae * east(a) + wbe * take(colse), waw * west(a) + wbw * take(colsw)

    acc = source
    for _ in range(SWEEPS - 1):
        phi, e, w = triple(acc)
        acc = (source + (ce * e + cw * w)) + (up(u0 * phi + u1 * e + u2 * w) + down(d0 * phi + d1 * e + d2 * w))
    phi = couple(acc)
    phi_v[...] = phi[ri:2 * ri]
    last = pltpu.make_async_copy(phi_v, phi_out, sems.at[1])
    last.start()
    write.wait()
    last.wait()


def body(sizes, density, velocity, magnetic, pressure, line_owner, line_row, pedersen, hall, mirror_shift):
    cx, cy, nz = density.shape
    ri = pedersen.shape[0]
    nx = sizes[0]
    any_ = pl.BlockSpec(memory_space=pl.ANY)
    vmem = pl.BlockSpec(memory_space=pltpu.VMEM)
    dma = pltpu.SemaphoreType.DMA
    con, src, coef, cols = pl.pallas_call(
        functools.partial(flux_kernel, sizes),
        out_shape=(
            pltpu.VMEM((8, cx, cy, nz), F32),
            pltpu.VMEM((2, 3, ri, nz), F32),
            pltpu.VMEM((COEFS, 6 * ri, nz), F32),
            pltpu.VMEM((6 * ri, nz), jnp.int32),
        ),
        in_specs=[any_] * 9,
        out_specs=(vmem,) * 4,
        scratch_shapes=[
            pltpu.VMEM((11, cx + 2, cy + 2 * PAD, nz), F32),
            pltpu.VMEM((2, cx, cy + 2 * PAD, nz), F32),
            pltpu.VMEM((2, cx, cy, nz), F32),
            pltpu.VMEM((2, 2, cy, nz), F32),
            pltpu.VMEM((2, 5, 2, cy, nz), F32),
            pltpu.VMEM((nx // 2, 2, ri, nz), F32),
            pltpu.VMEM((2, nx, 2, ri, nz), F32),
            pltpu.VMEM((2, 2, ri, nz), F32),
            pltpu.VMEM((6, 3, ri, nz), F32),
            pltpu.VMEM((1, 1, cx * cy), jnp.int32),
            pltpu.VMEM((1, cx * cy), jnp.int32),
            pltpu.SMEM((ri,), jnp.int32),
            dma((11,)),
            dma((2,)), dma((2,)), dma((2,)), dma((2,)), dma((2,)), dma((2,)),
            dma((4,)), dma((4,)), dma((2,)), dma((2,)), dma((6,)), dma((6,)),
            dma((2,)), dma((2,)), dma((1,)), dma((1,)),
            pltpu.SemaphoreType.REGULAR((8,)),
        ],
        compiler_params=pltpu.CompilerParams(collective_id=0, has_side_effects=True),
        name="flux_and_sources",
    )(density, velocity, magnetic, pressure, line_owner.reshape(1, 1, cx * cy), line_row.reshape(1, cx * cy),
      pedersen, hall, mirror_shift)
    return pl.pallas_call(
        sweep_kernel,
        out_shape=(
            jax.ShapeDtypeStruct((8, cx, cy, nz), F32),
            jax.ShapeDtypeStruct((ri, nz), F32),
        ),
        in_specs=[vmem] * 4,
        out_specs=(any_, any_),
        scratch_shapes=[pltpu.VMEM((ri, nz), F32), dma((2,))],
        name="sweeps",
    )(*[pltpu.with_memory_space_constraint(a, pltpu.VMEM) for a in (con, src, coef, cols)])


def solution(mesh):
    sizes = (mesh.shape["gx"], mesh.shape["pb"])
    in_specs = (
        P("gx", "pb", None),
        P(None, "gx", "pb", None),
        P(None, "gx", "pb", None),
        P("gx", "pb", None),
        P("gx", "pb", None, None),
        P("gx", "pb", None),
        P(("gx", "pb"), None),
        P(("gx", "pb"), None),
        P(("gx", "pb")),
    )
    out_specs = (P(None, "gx", "pb", None), P(("gx", "pb"), None))
    return jax.shard_map(
        functools.partial(body, sizes), mesh=mesh, in_specs=in_specs, out_specs=out_specs,
        check_vma=False)
```

```python
import functools

import jax
import jax.numpy as jnp
from jax import lax
from jax.experimental import pallas as pl
from jax.experimental.pallas import tpu as pltpu
from jax.sharding import PartitionSpec as P

SWEEPS = 8
GAMMA = 5.0 / 3.0
COURANT = 0.08
PAD = 8
COEFS = 11
F32 = jnp.float32
BF16 = jnp.bfloat16
MESH = pl.DeviceIdType.MESH
ORDER = (0, 2, 3, 4, 6, 5, 7, 1)
FIELD = {4: 6, 5: 5, 6: 7}
SPEED = 8
FLUX = {6: 9, 5: 10}


def cell_terms(prim):
    rho, vel, mag, pres = prim[0], prim[1:4], prim[4:7], prim[7]
    field_sq = mag[0] * mag[0] + mag[1] * mag[1] + mag[2] * mag[2]
    vel_sq = vel[0] * vel[0] + vel[1] * vel[1] + vel[2] * vel[2]
    half_sq = 0.5 * field_sq
    energy = pres * (1.0 / (GAMMA - 1.0)) + 0.5 * rho * vel_sq + half_sq
    total_p = pres + half_sq
    v_dot_b = vel[0] * mag[0] + vel[1] * mag[1] + vel[2] * mag[2]
    inv = 1.0 / rho
    sound_sq = GAMMA * pres * inv
    both = sound_sq + field_sq * inv
    momentum = [rho * v for v in vel]
    state = [rho] + momentum + list(mag) + [energy]
    return state, total_p, v_dot_b, sound_sq * inv, both


def flux_of(prim, terms, d):
    state, total_p, v_dot_b = terms[:3]
    vel, mag = prim[1:4], prim[4:7]
    vn, bn = vel[d], mag[d]
    flux = [state[1 + d]]
    for e in range(3):
        m = state[1 + e] * vn - mag[e] * bn
        flux.append(m + total_p if e == d else m)
    for e in range(3):
        flux.append(None if e == d else mag[e] * vn - bn * vel[e])
    flux.append((state[7] + total_p) * vn - bn * v_dot_b)
    return flux


def speed_of(prim, terms, d):
    sound_over, both = terms[3:]
    vn, bn = prim[1 + d], prim[4 + d]
    spread = both * both - 4.0 * sound_over * bn * bn
    fast = jnp.sqrt(0.5 * (both + jnp.sqrt(jnp.maximum(spread, 0.0))))
    return jnp.abs(vn) + fast


def face(f_lo, f_hi, u_lo, u_hi, largest):
    jump = largest * (u_hi - u_lo)
    return -0.5 * jump if f_lo is None else 0.5 * ((f_lo + f_hi) - jump)


def roll(values, shift, axis):
    return pltpu.roll(values, shift % values.shape[axis], axis)


def east(a):
    return roll(a, -1, 1)


def west(a):
    return roll(a, 1, 1)


def up(a):
    return roll(a, 1, 0)


def down(a):
    return roll(a, -1, 0)


def swap_by(cols, a):
    h = a.shape[0] // 2
    other = jnp.concatenate([a[h:], a[:h]], axis=0)
    return jnp.take_along_axis(other, cols, axis=1)


def flux_kernel(sizes, rho, vel, mag, pres, owner, line_row, ped, hall, shift,
                out, src_out, coef_out, cols_out,
                win, fwin, pstage, pin, edge, part, part_in, shared, cwin, own_v, row_v, shift_s,
                loc_sem, xs, xr, ls, lr, ys, yr, ds, dr, ps, pr, cs, cr, as_, ar, hs, hr, far):
    nx, ny = sizes
    cx, cy, nz = rho.shape
    ri = ped.shape[0]
    g, p = lax.axis_index("gx"), lax.axis_index("pb")
    n = nx * ny
    half = n // 2
    pairs = nx // 2
    b = g * ny + p
    wide = cy + 2 * PAD

    def dev(flat):
        return (lax.div(flat, ny), lax.rem(flat, ny))

    beside = {o: dev(lax.rem(b + o + n, n)) for o in (-1, 1)}

    barrier = pltpu.get_barrier_semaphore()

    for dg in (1, -1, 0, 2, -2):
        inside = (g + dg >= 0) & (g + dg < nx)

        @pl.when(inside)
        def _(to=jnp.clip(g + dg, 0, nx - 1), same=dg == 0):
            for o in (0, 1, -1):
                if o or not same:
                    pl.semaphore_signal(
                        barrier, inc=1, device_id=(to, beside[o][1] if o else p), device_id_type=MESH)

    at_end = (b == 0) | (b == n - 1)

    @pl.when(at_end)
    def _():
        pl.semaphore_signal(barrier, inc=1, device_id=dev(n - 1 - b), device_id_type=MESH)

    doubling = [1 << i for i in range(1, 32) if 1 << i < nx]

    def pass_on(r):
        for to in (g + r, g - r):
            @pl.when((to >= 0) & (to < nx))
            def _(to=jnp.clip(to, 0, nx - 1), at=doubling.index(r)):
                pl.semaphore_signal(far.at[at], inc=1, device_id=(to, p), device_id_type=MESH)

    def hear(r):
        count = (g + r < nx).astype(jnp.int32) + (g - r >= 0).astype(jnp.int32)
        pl.semaphore_wait(far.at[doubling.index(r)], count)

    rows = pl.ds(PAD, cy)
    mid = pl.ds(1, cx)
    loads = [
        (rho, win.at[0, mid, rows]), (vel, win.at[pl.ds(2, 3), mid, rows]),
        (pres, win.at[1, mid, rows]),
        (ped, cwin.at[1, 0]), (hall, cwin.at[1, 1]), (shift, shift_s),
        (owner, own_v), (line_row, row_v)]
    loads += [(mag.at[v - 4], win.at[FIELD[v], mid, rows]) for v in FIELD]
    loads = [pltpu.make_async_copy(s, d, loc_sem.at[i]) for i, (s, d) in enumerate(loads)]
    for c in loads:
        c.start()
    for c in loads:
        c.wait()

    row8 = lax.broadcasted_iota(jnp.int32, (ri, nz), 0)
    sh = jnp.zeros((ri, nz), F32)
    for i in range(ri):
        sh = jnp.where(row8 == i, shift_s[i].astype(F32), sh)
    cwin[1, 2] = sh

    lane = lax.broadcasted_iota(jnp.int32, (cx, cy, nz), 2)
    first, last = lane == 0, lane == nz - 1

    def z_dn(a):
        return jnp.where(first[:, :a.shape[1]], a, roll(a, 1, 2))

    def z_change(u, f, largest):
        low = face(None if f is None else z_dn(f), f, z_dn(u), u, largest)
        top = jnp.zeros_like(u) if f is None else f
        high = jnp.where(last[:, :u.shape[1]], top, roll(low, -1, 2))
        return high - low

    prim = [win[v, 1:1 + cx, PAD:PAD + cy, :] for v in ORDER]
    terms = cell_terms(prim)
    win[SPEED, 1:1 + cx, PAD:PAD + cy, :] = speed_of(prim, terms, 0)
    for v in FLUX:
        win[FLUX[v], 1:1 + cx, PAD:PAD + cy, :] = prim[v] * prim[1] - prim[4] * prim[v - 3]
    flux, speed = flux_of(prim, terms, 2), speed_of(prim, terms, 2)
    largest = jnp.maximum(speed, z_dn(speed))
    for v in range(8):
        out[v] = terms[0][v] - COURANT * z_change(terms[0][v], flux[v], largest)

    pl.semaphore_wait(barrier, 3 * (jnp.minimum(g + 2, nx - 1) - jnp.maximum(g - 2, 0) + 1) - 1 + at_end.astype(jnp.int32))
    for r in doubling[:1]:
        pass_on(r)

    def remote(src, dst, send, recv, where):
        return pltpu.make_async_remote_copy(
            src_ref=src, dst_ref=dst, send_sem=send, recv_sem=recv,
            device_id=where, device_id_type=MESH)

    g_up, g_dn = jnp.minimum(g + 1, nx - 1), jnp.maximum(g - 1, 0)
    p_up, p_dn = jnp.minimum(p + 1, ny - 1), jnp.maximum(p - 1, 0)
    has_xu, has_xd, has_yu, has_yd = g < nx - 1, g > 0, p < ny - 1, p > 0

    def each(cond, copies, act):
        @pl.when(cond)
        def _():
            for c in copies:
                getattr(c, act)()

    def x_pair(at, count, send, recv):
        return [
            remote(win.at[pl.ds(at, count), s, rows], win.at[pl.ds(at, count), d, rows],
                   send.at[way], recv.at[way], (where, p))
            for way, (s, d, where) in enumerate(((cx, 0, g_up), (1, cx + 1, g_dn)))]

    xc = x_pair(5, 6, xs, xr)
    xlate = x_pair(0, 5, ls, lr)
    yc = [
        remote(win.at[pl.ds(0, 8), mid, pl.ds(s, PAD)], win.at[pl.ds(0, 8), mid, pl.ds(d, PAD)],
               ys.at[way], yr.at[way], (g, where))
        for way, (s, d, where) in enumerate(((cy, 0, p_up), (PAD, PAD + cy, p_dn)))]
    diag = []
    for i, (xu, yu) in enumerate(((1, 1), (1, 0), (0, 1), (0, 0))):
        s_x, d_x, to_g = (cx, 0, g_up) if xu else (1, cx + 1, g_dn)
        s_y, d_y, to_p = (PAD + cy - 1, PAD - 1, p_up) if yu else (PAD, PAD + cy, p_dn)
        c = remote(win.at[pl.ds(6, 4), s_x, pl.ds(s_y, 1)], win.at[pl.ds(6, 4), d_x, pl.ds(d_y, 1)],
                   ds.at[i], dr.at[i], (to_g, to_p))
        to = (has_xu if xu else has_xd) & (has_yu if yu else has_yd)
        come = (has_xd if xu else has_xu) & (has_yd if yu else has_yu)
        diag.append((c, to, come))
    ion = [
        (lax.rem(b + 1, n), 0),
        (lax.rem(b + n - 1, n), 2),
        (lax.rem(b + half + 1, n), 3),
        (lax.rem(b + half, n), 4),
        (lax.rem(b + half + n - 1, n), 5),
    ]
    cond_copies = [
        remote(cwin.at[1, pl.ds(0, 3 if slot < 3 else 2)], cwin.at[slot, pl.ds(0, 3 if slot < 3 else 2)],
               cs.at[slot], cr.at[slot], dev(flat)) for flat, slot in ion]

    each(has_yu, yc[:1], "start")
    each(has_yd, yc[1:], "start")
    for c, to, _ in diag:
        each(to, [c], "start")
    each(has_xu, xc[:1], "start")
    each(has_xd, xc[1:], "start")
    for c in cond_copies[:2]:
        c.start()

    each(has_yd, yc[:1], "wait_recv")
    each(has_yu, yc[1:], "wait_recv")

    @pl.when(p == 0)
    def _():
        for v in range(8):
            win[v, 1:1 + cx, PAD - 1:PAD, :] = win[v, 1:1 + cx, PAD:PAD + 1, :]

    @pl.when(p == ny - 1)
    def _():
        for v in range(8):
            win[v, 1:1 + cx, PAD + cy:PAD + cy + 1, :] = win[v, 1:1 + cx, PAD + cy - 1:PAD + cy, :]

    def x_inner(values, u, f):
        if cx == 1:
            return values
        speed = win[SPEED, 1:1 + cx, PAD:PAD + cy, :]
        lows = face(None if f is None else f[:-1], None if f is None else f[1:], u[:-1], u[1:],
                    jnp.maximum(speed[:-1], speed[1:]))
        none = jnp.zeros_like(lows[:1])
        return values - COURANT * (jnp.concatenate([lows, none], 0) - jnp.concatenate([none, lows], 0))

    prim = [win[v, 1:1 + cx] for v in ORDER]
    terms = cell_terms(prim)
    flux, speed = flux_of(prim, terms, 1), speed_of(prim, terms, 1)
    largest = jnp.maximum(speed, roll(speed, 1, 1))

    def y_change(v):
        u, f = terms[0][v], flux[v]
        low = face(None if f is None else roll(f, 1, 1), f, roll(u, 1, 1), u, largest)
        return roll(low, -1, 1) - low

    def ends(a):
        return jnp.concatenate([a[:, :PAD], a[:, PAD + cy:]], axis=1)

    side = {}
    for v in (5, 6, 4):
        diff = y_change(v)
        if v != 5:
            side[v] = ends(diff)
        u = win[FIELD[v], 1:1 + cx, PAD:PAD + cy, :]
        f = None if v == 4 else win[FLUX[v], 1:1 + cx, PAD:PAD + cy, :]
        done = x_inner(out[v] - COURANT * diff[:, PAD:PAD + cy, :], u, f)
        if v == 4:
            out[v] = done
        else:
            pstage[v - 5] = done
        if v == 6:
            pc = [
                remote(pstage.at[:, s], pin.at[way], ps.at[way], pr.at[way], (where, p))
                for way, (s, where) in enumerate(((cx - 1, g_up), (0, g_dn)))]
            each(has_xu, pc[:1], "start")
            each(has_xd, pc[1:], "start")
            for at, r in enumerate(doubling[:-1]):
                hear(r)
                pass_on(doubling[at + 1])
    for v in (0, 1, 2, 3, 7):
        out[v] = out[v] - COURANT * y_change(v)[:, PAD:PAD + cy, :]

    for c, _, come in diag:
        each(come, [c], "wait_recv")

    def edge_planes(which, at, count):
        at = pl.ds(at, count)

        @pl.when(g == 0)
        def _():
            for v in which:
                win[v, 0, at, :] = win[v, 1, at, :]

        @pl.when(g == nx - 1)
        def _():
            for v in which:
                win[v, cx + 1, at, :] = win[v, cx, at, :]

    def tiles(v, at):
        return jnp.concatenate([win[v, at, :PAD, :], win[v, at, PAD + cy:, :]], axis=1)

    own = [tiles(v, slice(1, 1 + cx)) for v in ORDER]
    terms = cell_terms(own)
    for v, value in ((SPEED, speed_of(own, terms, 0)), (FLUX[6], own[6] * own[1] - own[4] * own[3])):
        win[v, 1:1 + cx, :PAD, :] = value[:, :PAD]
        win[v, 1:1 + cx, PAD + cy:, :] = value[:, PAD:]
    edge_planes(range(6, 10), 0, PAD)
    edge_planes(range(6, 10), PAD + cy, PAD)
    speed_z = speed_of(own, terms, 2)
    largest_z = jnp.maximum(speed_z, z_dn(speed_z))
    around = slice(0, cx + 2)
    speed_x = tiles(SPEED, around)
    largest_x = jnp.maximum(speed_x[:-1], speed_x[1:])
    for v in (4, 6):
        u = tiles(FIELD[v], around)
        fz = None if v == 6 else own[v] * own[3] - own[6] * own[v - 3]
        fx = None if v == 4 else tiles(FLUX[v], around)
        lows = face(None if fx is None else fx[:-1], None if fx is None else fx[1:], u[:-1], u[1:], largest_x)
        new = own[v] - COURANT * (z_change(own[v], fz, largest_z) + side[v] + (lows[1:] - lows[:-1]))
        fwin[v // 6, :, 0:PAD, :] = new[:, :PAD]
        fwin[v // 6, :, PAD + cy:, :] = new[:, PAD:]

    key = own_v[0] * ri + row_v[...]
    at = lax.broadcasted_iota(jnp.int32, (nx * ri, cx * cy), 0)
    pair, rest = at // (2 * ri), at % (2 * ri)
    hot = (key == (pair + (rest // ri) * pairs) * ri + rest % ri).astype(BF16)
    hot = jnp.concatenate([hot, hot, hot], axis=1)

    for r in doubling[-1:]:
        hear(r)
    for c in cond_copies[2:]:
        c.start()
    each(has_xd, xc[:1], "wait_recv")
    each(has_xu, xc[1:], "wait_recv")
    edge_planes(range(5, 11), PAD, cy)

    def outer_faces(v, f_of):
        faces = []
        for lo in (0, cx):
            u = [win[FIELD[v], lo + i, PAD:PAD + cy, :] for i in range(2)]
            f = [f_of(v, lo + i) for i in range(2)]
            most = jnp.maximum(win[SPEED, lo, PAD:PAD + cy, :], win[SPEED, lo + 1, PAD:PAD + cy, :])
            faces.append(COURANT * face(f[0], f[1], u[0], u[1], most))
        return faces

    def b_flux(v, at):
        return None if v == 4 else win[FLUX[v], at, PAD:PAD + cy, :]

    def close(values, faces):
        planes = [values[i] for i in range(cx)]
        planes[0] = planes[0] + faces[0]
        planes[-1] = planes[-1] - faces[1]
        return planes

    field, outer = {}, {}
    for v in (4, 6, 5):
        outer[v] = outer_faces(v, b_flux)
        field[v] = close(out[v] if v == 4 else pstage[v - 5], outer[v])
        for i in range(cx):
            out[v, i] = field[v][i]
            if v != 5:
                fwin[v // 6, i, PAD:PAD + cy, :] = field[v][i]

    @pl.when(p == 0)
    def _():
        fwin[:, :, PAD - 1:PAD, :] = fwin[:, :, PAD:PAD + 1, :]

    @pl.when(p == ny - 1)
    def _():
        fwin[:, :, PAD + cy:PAD + cy + 1, :] = fwin[:, :, PAD + cy - 1:PAD + cy, :]

    def d_y(v):
        a = fwin[v // 6]
        return 0.5 * (roll(a, -1, 1) - roll(a, 1, 1))[:, PAD:PAD + cy, :]

    def d_z(a):
        return 0.5 * (jnp.where(last, a, roll(a, -1, 2)) - z_dn(a))

    bx, by, bz = [jnp.stack(field[v]) for v in (4, 5, 6)]
    jx = d_y(6) - d_z(by)
    size = jnp.sqrt(bx * bx + by * by + bz * bz)
    dzx, dyx = d_z(bx), d_y(4)

    each(has_xd, pc[:1], "wait_recv")
    each(has_xu, pc[1:], "wait_recv")

    def d_x(v):
        lo = jnp.where(g == 0, field[v][0], pin[0, v - 5] - outer[v][0])
        hi = jnp.where(g == nx - 1, field[v][-1], pin[1, v - 5] + outer[v][1])
        a = jnp.stack([lo] + field[v] + [hi])
        return 0.5 * (a[2:] - a[:-2])

    jy = dzx - d_x(6)
    jz = d_x(5) - dyx
    current = (jx * bx + jy * by + jz * bz) / jnp.maximum(size, 1.0)
    current = current.reshape(cx * cy, nz)

    head = current.astype(BF16)
    tail = current - head.astype(F32)
    body_ = tail.astype(BF16)
    tail = (tail - body_.astype(F32)).astype(BF16)
    sums = jnp.dot(hot, jnp.concatenate([head, body_, tail], axis=0),
                   preferred_element_type=F32)
    part[...] = sums.reshape(pairs, 2, ri, nz)

    odd = lax.rem(p, 2)
    mate = (g, p + 1 - 2 * odd)
    out_g, out_p = jnp.where(odd == 1, beside[1][0], beside[-1][0]), jnp.where(odd == 1, beside[1][1], beside[-1][1])
    step = lax.rem(out_g - g + nx, nx)

    def own_copy(to):
        return remote(part.at[lax.rem(to, pairs)], part_in.at[0, g], as_.at[0], ar.at[0], (to, p))

    def outer_copy(to, first_row):
        some = pl.ds(first_row, ri - 1)
        return remote(part.at[lax.rem(to, pairs), :, some], part_in.at[1, g, :, some], as_.at[1], ar.at[1],
                      (lax.rem(to + step, nx), out_p))

    def send_own(k, carry):
        own_copy(lax.rem(g + k, nx)).start()
        return carry

    def send_outer(first_row):
        def send(k, carry):
            outer_copy(lax.rem(g + k, nx), first_row).start()
            return carry

        lax.fori_loop(0, nx, send, 0, unroll=nx <= 8)

    lax.fori_loop(1, nx, send_own, 0, unroll=nx <= 8)
    pl.when(odd == 1)(lambda: send_outer(1))
    pl.when(odd == 0)(lambda: send_outer(0))
    each(has_xu, xlate[:1], "start")
    each(has_xd, xlate[1:], "start")

    for c in cond_copies:
        c.wait_recv()
    lines = 6 * ri
    row = lax.broadcasted_iota(jnp.int32, (lines, nz), 0)
    row = jnp.where(row >= 3 * ri, row - 3 * ri, row)
    place = lax.rem(b, half)
    low_row = jnp.where(place == half // 2, ri, 0)
    high_row = jnp.where(place == half // 2 - 1, 2 * ri, 3 * ri)
    valid = (row >= low_row) & (row < high_row)
    pw = jnp.where(valid, cwin[:, 0].reshape(lines, nz), 0.0)
    hw = jnp.where(valid, cwin[:, 1].reshape(lines, nz), 0.0)
    own_shift = cwin[0:3, 2].reshape(3 * ri, nz).astype(jnp.int32)
    col = lax.broadcasted_iota(jnp.int32, (3 * ri, nz), 1)
    cols = jnp.concatenate(
        [(col + own_shift) % nz, (col + (nz - own_shift)) % nz], axis=0)
    he, hwst = east(hw), west(hw)
    coef = [
        0.5 * (pw + up(pw)), 0.5 * (pw + down(pw)),
        0.5 * (pw + east(pw)), 0.5 * (pw + west(pw)),
        0.125 * (hw + up(he)), 0.125 * (hw + up(hwst)),
        0.125 * (hw + down(he)), 0.125 * (hw + down(hwst)),
    ]
    center = coef[0]
    for c in coef[1:]:
        center = center + c
    inv = jnp.where(valid, 1.0 / jnp.where(valid, center, 1.0), 0.0)
    pm = swap_by(cols, pw)
    both = jnp.where(valid, pw + pm, 1.0)
    for i, c in enumerate(coef):
        coef_out[i] = c * inv
    coef_out[8] = inv
    coef_out[9] = jnp.where(valid, pw / both, 0.0)
    coef_out[10] = jnp.where(valid, pm / both, 0.0)
    cols_out[...] = cols

    rest = (0, 1, 2, 3, 7)
    prim = [win[v, 1:1 + cx, PAD:PAD + cy, :] for v in ORDER]
    terms = cell_terms(prim)
    flux = flux_of(prim, terms, 0)
    for at, v in enumerate(rest):
        out[v] = x_inner(out[v], terms[0][v], flux[v])
        for side_at, plane in enumerate((0, cx - 1)):
            edge[0, at, side_at] = terms[0][v][plane]
            edge[1, at, side_at] = flux[v][plane]

    def taken(slot, sems):
        some = part_in.at[slot, pl.ds(0, nx - 1 if slot == 0 else nx), :, pl.ds(0, ri if slot == 0 else ri - 1)]
        pltpu.make_async_copy(some, some, sems.at[slot]).wait()

    def total_of(slot):
        def add(at, total):
            return total + part_in[slot, at]
        return lax.fori_loop(1, nx, add, part_in[slot, 0], unroll=nx <= 8)

    taken(0, ar)
    part_in[0, g] = part[lax.rem(g, pairs)]
    shared[0] = total_of(0)
    to_mate = remote(shared.at[0], shared.at[1], hs.at[0], hr.at[0], mate)
    to_mate.start()
    each(has_xd, xlate[:1], "wait_recv")
    each(has_xu, xlate[1:], "wait_recv")

    def ghosts(v):
        return jnp.stack([win[v, at, PAD:PAD + cy, :] for at in (0, cx + 1)])

    prim = [ghosts(v) for v in ORDER]
    terms = cell_terms(prim)
    flux = flux_of(prim, terms, 0)
    speed = jnp.maximum(ghosts(SPEED), jnp.stack([win[SPEED, at, PAD:PAD + cy, :] for at in (1, cx)]))
    for at, v in enumerate(rest):
        u, f = terms[0][v], flux[v]
        own_u, own_f = edge[0, at], edge[1, at]
        low = face(f[0], own_f[0], u[0], own_u[0], speed[0])
        high = face(own_f[1], f[1], own_u[1], u[1], speed[1])
        low = jnp.where(g == 0, own_f[0], low)
        high = jnp.where(g == nx - 1, own_f[1], high)
        out[v, 0] = out[v, 0] + COURANT * low
        out[v, cx - 1] = out[v, cx - 1] - COURANT * high

    taken(1, ar)
    outer_sum = total_of(1)
    to_mate.wait_recv()

    def place_sums(slot, total, block):
        northern = block < half
        src_out[0, slot] = jnp.where(northern, total[0], total[1])
        src_out[1, slot] = jnp.where(northern, total[1], total[0])

    mate_sum = shared[1]
    place_sums(0, jnp.where(odd == 1, mate_sum, outer_sum), lax.rem(b + n - 1, n))
    place_sums(1, shared[0], b)
    place_sums(2, jnp.where(odd == 1, outer_sum, mate_sum), lax.rem(b + 1, n))

    each(has_xu, [xc[0], xlate[0], pc[0]], "wait_send")
    each(has_xd, [xc[1], xlate[1], pc[1]], "wait_send")
    each(has_yu, yc[:1], "wait_send")
    each(has_yd, yc[1:], "wait_send")
    for c, to, _ in diag:
        each(to, [c], "wait_send")
    for c in cond_copies:
        c.wait_send()
    to_mate.wait_send()
    taken(0, as_)
    taken(1, as_)


def sweep_kernel(con, src, coef, cols_ref, out, phi_out, phi_v, sems):
    write = pltpu.make_async_copy(con, out, sems.at[0])
    write.start()
    cu, cd, ce, cw, cue, cuw, cde, cdw, inv, wa, wb = [coef[i] for i in range(COEFS)]
    cols = cols_ref[...]
    ri = phi_v.shape[0]
    source = src[...].reshape(inv.shape) * inv

    def couple(phi):
        return wa * phi + wb * swap_by(cols, phi)

    wae, waw, wbe, wbw = east(wa), west(wa), east(wb), west(wb)
    colse, colsw = east(cols), west(cols)
    u0, u1, u2 = down(cu), down(cue), -down(cuw)
    d0, d1, d2 = up(cd), -up(cde), up(cdw)

    def triple(a):
        h = a.shape[0] // 2
        other = jnp.concatenate([a[h:], a[:h]], axis=0)
        take = lambda c: jnp.take_along_axis(other, c, axis=1)
        return wa * a + wb * take(cols), wae * east(a) + wbe * take(colse), waw * west(a) + wbw * take(colsw)

    acc = source
    for _ in range(SWEEPS - 1):
        phi, e, w = triple(acc)
        acc = (source + (ce * e + cw * w)) + (up(u0 * phi + u1 * e + u2 * w) + down(d0 * phi + d1 * e + d2 * w))
    phi = couple(acc)
    phi_v[...] = phi[ri:2 * ri]
    last = pltpu.make_async_copy(phi_v, phi_out, sems.at[1])
    last.start()
    write.wait()
    last.wait()


def body(sizes, density, velocity, magnetic, pressure, line_owner, line_row, pedersen, hall, mirror_shift):
    cx, cy, nz = density.shape
    ri = pedersen.shape[0]
    nx = sizes[0]
    any_ = pl.BlockSpec(memory_space=pl.ANY)
    vmem = pl.BlockSpec(memory_space=pltpu.VMEM)
    dma = pltpu.SemaphoreType.DMA
    con, src, coef, cols = pl.pallas_call(
        functools.partial(flux_kernel, sizes),
        out_shape=(
            pltpu.VMEM((8, cx, cy, nz), F32),
            pltpu.VMEM((2, 3, ri, nz), F32),
            pltpu.VMEM((COEFS, 6 * ri, nz), F32),
            pltpu.VMEM((6 * ri, nz), jnp.int32),
        ),
        in_specs=[any_] * 9,
        out_specs=(vmem,) * 4,
        scratch_shapes=[
            pltpu.VMEM((11, cx + 2, cy + 2 * PAD, nz), F32),
            pltpu.VMEM((2, cx, cy + 2 * PAD, nz), F32),
            pltpu.VMEM((2, cx, cy, nz), F32),
            pltpu.VMEM((2, 2, cy, nz), F32),
            pltpu.VMEM((2, 5, 2, cy, nz), F32),
            pltpu.VMEM((nx // 2, 2, ri, nz), F32),
            pltpu.VMEM((2, nx, 2, ri, nz), F32),
            pltpu.VMEM((2, 2, ri, nz), F32),
            pltpu.VMEM((6, 3, ri, nz), F32),
            pltpu.VMEM((1, 1, cx * cy), jnp.int32),
            pltpu.VMEM((1, cx * cy), jnp.int32),
            pltpu.SMEM((ri,), jnp.int32),
            dma((11,)),
            dma((2,)), dma((2,)), dma((2,)), dma((2,)), dma((2,)), dma((2,)),
            dma((4,)), dma((4,)), dma((2,)), dma((2,)), dma((6,)), dma((6,)),
            dma((2,)), dma((2,)), dma((1,)), dma((1,)),
            pltpu.SemaphoreType.REGULAR((8,)),
        ],
        compiler_params=pltpu.CompilerParams(collective_id=0, has_side_effects=True),
        name="flux_and_sources",
    )(density, velocity, magnetic, pressure, line_owner.reshape(1, 1, cx * cy), line_row.reshape(1, cx * cy),
      pedersen, hall, mirror_shift)
    return pl.pallas_call(
        sweep_kernel,
        out_shape=(
            jax.ShapeDtypeStruct((8, cx, cy, nz), F32),
            jax.ShapeDtypeStruct((ri, nz), F32),
        ),
        in_specs=[vmem] * 4,
        out_specs=(any_, any_),
        scratch_shapes=[pltpu.VMEM((ri, nz), F32), dma((2,))],
        name="sweeps",
    )(*[pltpu.with_memory_space_constraint(a, pltpu.VMEM) for a in (con, src, coef, cols)])


def solution(mesh):
    sizes = (mesh.shape["gx"], mesh.shape["pb"])
    in_specs = (
        P("gx", "pb", None),
        P(None, "gx", "pb", None),
        P(None, "gx", "pb", None),
        P("gx", "pb", None),
        P("gx", "pb", None, None),
        P("gx", "pb", None),
        P(("gx", "pb"), None),
        P(("gx", "pb"), None),
        P(("gx", "pb")),
    )
    out_specs = (P(None, "gx", "pb", None), P(("gx", "pb"), None))
    return jax.shard_map(
        functools.partial(body, sizes), mesh=mesh, in_specs=in_specs, out_specs=out_specs,
        check_vma=False)
```

```python
import functools

import jax
import jax.numpy as jnp
from jax import lax
from jax.experimental import pallas as pl
from jax.experimental.pallas import tpu as pltpu
from jax.sharding import PartitionSpec as P

SWEEPS = 8
GAMMA = 5.0 / 3.0
COURANT = 0.08
PAD = 8
COEFS = 15
F32 = jnp.float32
BF16 = jnp.bfloat16
MESH = pl.DeviceIdType.MESH
ORDER = (0, 2, 3, 4, 6, 5, 7, 1)
FIELD = {4: 6, 5: 5, 6: 7}
SPEED = 8
FLUX = {6: 9, 5: 10}


def cell_terms(prim):
    rho, vel, mag, pres = prim[0], prim[1:4], prim[4:7], prim[7]
    field_sq = mag[0] * mag[0] + mag[1] * mag[1] + mag[2] * mag[2]
    vel_sq = vel[0] * vel[0] + vel[1] * vel[1] + vel[2] * vel[2]
    half_sq = 0.5 * field_sq
    energy = pres * (1.0 / (GAMMA - 1.0)) + 0.5 * rho * vel_sq + half_sq
    total_p = pres + half_sq
    v_dot_b = vel[0] * mag[0] + vel[1] * mag[1] + vel[2] * mag[2]
    inv = 1.0 / rho
    sound_sq = GAMMA * pres * inv
    both = sound_sq + field_sq * inv
    momentum = [rho * v for v in vel]
    state = [rho] + momentum + list(mag) + [energy]
    return state, total_p, v_dot_b, sound_sq * inv, both


def flux_of(prim, terms, d):
    state, total_p, v_dot_b = terms[:3]
    vel, mag = prim[1:4], prim[4:7]
    vn, bn = vel[d], mag[d]
    flux = [state[1 + d]]
    for e in range(3):
        m = state[1 + e] * vn - mag[e] * bn
        flux.append(m + total_p if e == d else m)
    for e in range(3):
        flux.append(None if e == d else mag[e] * vn - bn * vel[e])
    flux.append((state[7] + total_p) * vn - bn * v_dot_b)
    return flux


def speed_of(prim, terms, d):
    sound_over, both = terms[3:]
    vn, bn = prim[1 + d], prim[4 + d]
    spread = both * both - 4.0 * sound_over * bn * bn
    fast = jnp.sqrt(0.5 * (both + jnp.sqrt(jnp.maximum(spread, 0.0))))
    return jnp.abs(vn) + fast


def face(f_lo, f_hi, u_lo, u_hi, largest):
    jump = largest * (u_hi - u_lo)
    return -0.5 * jump if f_lo is None else 0.5 * ((f_lo + f_hi) - jump)


def roll(values, shift, axis):
    return pltpu.roll(values, shift % values.shape[axis], axis)


def east(a):
    return roll(a, -1, 1)


def west(a):
    return roll(a, 1, 1)


def up(a):
    return roll(a, 1, 0)


def down(a):
    return roll(a, -1, 0)


def swap_by(cols, a):
    h = a.shape[0] // 2
    other = jnp.concatenate([a[h:], a[:h]], axis=0)
    return jnp.take_along_axis(other, cols, axis=1)


def flux_kernel(sizes, rho, vel, mag, pres, owner, line_row, ped, hall, shift,
                out, src_out, coef_out, cols_out,
                win, fwin, pstage, pin, edge, part, part_in, shared, cwin, own_v, row_v, shift_s,
                loc_sem, xs, xr, ls, lr, ys, yr, ds, dr, ps, pr, cs, cr, as_, ar, hs, hr, far):
    nx, ny = sizes
    cx, cy, nz = rho.shape
    ri = ped.shape[0]
    g, p = lax.axis_index("gx"), lax.axis_index("pb")
    n = nx * ny
    half = n // 2
    pairs = nx // 2
    b = g * ny + p
    wide = cy + 2 * PAD

    def dev(flat):
        return (lax.div(flat, ny), lax.rem(flat, ny))

    beside = {o: dev(lax.rem(b + o + n, n)) for o in (-1, 1)}

    barrier = pltpu.get_barrier_semaphore()

    for dg in (1, -1, 0, 2, -2):
        inside = (g + dg >= 0) & (g + dg < nx)

        @pl.when(inside)
        def _(to=jnp.clip(g + dg, 0, nx - 1), same=dg == 0):
            for o in (0, 1, -1):
                if o or not same:
                    pl.semaphore_signal(
                        barrier, inc=1, device_id=(to, beside[o][1] if o else p), device_id_type=MESH)

    at_end = (b == 0) | (b == n - 1)

    @pl.when(at_end)
    def _():
        pl.semaphore_signal(barrier, inc=1, device_id=dev(n - 1 - b), device_id_type=MESH)

    doubling = [1 << i for i in range(1, 32) if 1 << i < nx]

    def pass_on(r):
        for to in (g + r, g - r):
            @pl.when((to >= 0) & (to < nx))
            def _(to=jnp.clip(to, 0, nx - 1), at=doubling.index(r)):
                pl.semaphore_signal(far.at[at], inc=1, device_id=(to, p), device_id_type=MESH)

    def hear(r):
        count = (g + r < nx).astype(jnp.int32) + (g - r >= 0).astype(jnp.int32)
        pl.semaphore_wait(far.at[doubling.index(r)], count)

    rows = pl.ds(PAD, cy)
    mid = pl.ds(1, cx)
    loads = [
        (rho, win.at[0, mid, rows]), (vel, win.at[pl.ds(2, 3), mid, rows]),
        (pres, win.at[1, mid, rows]),
        (ped, cwin.at[1, 0]), (hall, cwin.at[1, 1]), (shift, shift_s),
        (owner, own_v), (line_row, row_v)]
    loads += [(mag.at[v - 4], win.at[FIELD[v], mid, rows]) for v in FIELD]
    loads = [pltpu.make_async_copy(s, d, loc_sem.at[i]) for i, (s, d) in enumerate(loads)]
    for c in loads:
        c.start()
    for c in loads:
        c.wait()

    row8 = lax.broadcasted_iota(jnp.int32, (ri, nz), 0)
    sh = jnp.zeros((ri, nz), F32)
    for i in range(ri):
        sh = jnp.where(row8 == i, shift_s[i].astype(F32), sh)
    cwin[1, 2] = sh

    lane = lax.broadcasted_iota(jnp.int32, (cx, cy, nz), 2)
    first, last = lane == 0, lane == nz - 1

    def z_dn(a):
        return jnp.where(first[:, :a.shape[1]], a, roll(a, 1, 2))

    def z_change(u, f, largest):
        low = face(None if f is None else z_dn(f), f, z_dn(u), u, largest)
        top = jnp.zeros_like(u) if f is None else f
        high = jnp.where(last[:, :u.shape[1]], top, roll(low, -1, 2))
        return high - low

    prim = [win[v, 1:1 + cx, PAD:PAD + cy, :] for v in ORDER]
    terms = cell_terms(prim)
    win[SPEED, 1:1 + cx, PAD:PAD + cy, :] = speed_of(prim, terms, 0)
    for v in FLUX:
        win[FLUX[v], 1:1 + cx, PAD:PAD + cy, :] = prim[v] * prim[1] - prim[4] * prim[v - 3]
    flux, speed = flux_of(prim, terms, 2), speed_of(prim, terms, 2)
    largest = jnp.maximum(speed, z_dn(speed))
    for v in range(8):
        out[v] = terms[0][v] - COURANT * z_change(terms[0][v], flux[v], largest)

    pl.semaphore_wait(barrier, 3 * (jnp.minimum(g + 2, nx - 1) - jnp.maximum(g - 2, 0) + 1) - 1 + at_end.astype(jnp.int32))
    for r in doubling[:1]:
        pass_on(r)

    def remote(src, dst, send, recv, where):
        return pltpu.make_async_remote_copy(
            src_ref=src, dst_ref=dst, send_sem=send, recv_sem=recv,
            device_id=where, device_id_type=MESH)

    g_up, g_dn = jnp.minimum(g + 1, nx - 1), jnp.maximum(g - 1, 0)
    p_up, p_dn = jnp.minimum(p + 1, ny - 1), jnp.maximum(p - 1, 0)
    has_xu, has_xd, has_yu, has_yd = g < nx - 1, g > 0, p < ny - 1, p > 0

    def each(cond, copies, act):
        @pl.when(cond)
        def _():
            for c in copies:
                getattr(c, act)()

    def x_pair(at, count, send, recv):
        return [
            remote(win.at[pl.ds(at, count), s, rows], win.at[pl.ds(at, count), d, rows],
                   send.at[way], recv.at[way], (where, p))
            for way, (s, d, where) in enumerate(((cx, 0, g_up), (1, cx + 1, g_dn)))]

    xc = x_pair(5, 6, xs, xr)
    xlate = x_pair(0, 5, ls, lr)
    yc = [
        remote(win.at[pl.ds(0, 8), mid, pl.ds(s, PAD)], win.at[pl.ds(0, 8), mid, pl.ds(d, PAD)],
               ys.at[way], yr.at[way], (g, where))
        for way, (s, d, where) in enumerate(((cy, 0, p_up), (PAD, PAD + cy, p_dn)))]
    diag = []
    for i, (xu, yu) in enumerate(((1, 1), (1, 0), (0, 1), (0, 0))):
        s_x, d_x, to_g = (cx, 0, g_up) if xu else (1, cx + 1, g_dn)
        s_y, d_y, to_p = (PAD + cy - 1, PAD - 1, p_up) if yu else (PAD, PAD + cy, p_dn)
        c = remote(win.at[pl.ds(6, 4), s_x, pl.ds(s_y, 1)], win.at[pl.ds(6, 4), d_x, pl.ds(d_y, 1)],
                   ds.at[i], dr.at[i], (to_g, to_p))
        to = (has_xu if xu else has_xd) & (has_yu if yu else has_yd)
        come = (has_xd if xu else has_xu) & (has_yd if yu else has_yu)
        diag.append((c, to, come))
    ion = [
        (lax.rem(b + 1, n), 0),
        (lax.rem(b + n - 1, n), 2),
        (lax.rem(b + half + 1, n), 3),
        (lax.rem(b + half, n), 4),
        (lax.rem(b + half + n - 1, n), 5),
    ]
    cond_copies = [
        remote(cwin.at[1, pl.ds(0, 3 if slot < 3 else 2)], cwin.at[slot, pl.ds(0, 3 if slot < 3 else 2)],
               cs.at[slot], cr.at[slot], dev(flat)) for flat, slot in ion]

    each(has_yu, yc[:1], "start")
    each(has_yd, yc[1:], "start")
    for c, to, _ in diag:
        each(to, [c], "start")
    each(has_xu, xc[:1], "start")
    each(has_xd, xc[1:], "start")
    for c in cond_copies[:2]:
        c.start()

    each(has_yd, yc[:1], "wait_recv")
    each(has_yu, yc[1:], "wait_recv")

    @pl.when(p == 0)
    def _():
        for v in range(8):
            win[v, 1:1 + cx, PAD - 1:PAD, :] = win[v, 1:1 + cx, PAD:PAD + 1, :]

    @pl.when(p == ny - 1)
    def _():
        for v in range(8):
            win[v, 1:1 + cx, PAD + cy:PAD + cy + 1, :] = win[v, 1:1 + cx, PAD + cy - 1:PAD + cy, :]

    def x_inner(values, u, f):
        if cx == 1:
            return values
        speed = win[SPEED, 1:1 + cx, PAD:PAD + cy, :]
        lows = face(None if f is None else f[:-1], None if f is None else f[1:], u[:-1], u[1:],
                    jnp.maximum(speed[:-1], speed[1:]))
        none = jnp.zeros_like(lows[:1])
        return values - COURANT * (jnp.concatenate([lows, none], 0) - jnp.concatenate([none, lows], 0))

    prim = [win[v, 1:1 + cx] for v in ORDER]
    terms = cell_terms(prim)
    flux, speed = flux_of(prim, terms, 1), speed_of(prim, terms, 1)
    largest = jnp.maximum(speed, roll(speed, 1, 1))

    def y_change(v):
        u, f = terms[0][v], flux[v]
        low = face(None if f is None else roll(f, 1, 1), f, roll(u, 1, 1), u, largest)
        return roll(low, -1, 1) - low

    def ends(a):
        return jnp.concatenate([a[:, :PAD], a[:, PAD + cy:]], axis=1)

    side = {}
    for v in (5, 6, 4):
        diff = y_change(v)
        if v != 5:
            side[v] = ends(diff)
        u = win[FIELD[v], 1:1 + cx, PAD:PAD + cy, :]
        f = None if v == 4 else win[FLUX[v], 1:1 + cx, PAD:PAD + cy, :]
        done = x_inner(out[v] - COURANT * diff[:, PAD:PAD + cy, :], u, f)
        if v == 4:
            out[v] = done
        else:
            pstage[v - 5] = done
        if v == 6:
            pc = [
                remote(pstage.at[:, s], pin.at[way], ps.at[way], pr.at[way], (where, p))
                for way, (s, where) in enumerate(((cx - 1, g_up), (0, g_dn)))]
            each(has_xu, pc[:1], "start")
            each(has_xd, pc[1:], "start")
            for at, r in enumerate(doubling[:-1]):
                hear(r)
                pass_on(doubling[at + 1])
    for v in (0, 1, 2, 3, 7):
        out[v] = out[v] - COURANT * y_change(v)[:, PAD:PAD + cy, :]

    for c, _, come in diag:
        each(come, [c], "wait_recv")

    def edge_planes(which, at, count):
        at = pl.ds(at, count)

        @pl.when(g == 0)
        def _():
            for v in which:
                win[v, 0, at, :] = win[v, 1, at, :]

        @pl.when(g == nx - 1)
        def _():
            for v in which:
                win[v, cx + 1, at, :] = win[v, cx, at, :]

    def tiles(v, at):
        return jnp.concatenate([win[v, at, :PAD, :], win[v, at, PAD + cy:, :]], axis=1)

    own = [tiles(v, slice(1, 1 + cx)) for v in ORDER]
    terms = cell_terms(own)
    for v, value in ((SPEED, speed_of(own, terms, 0)), (FLUX[6], own[6] * own[1] - own[4] * own[3])):
        win[v, 1:1 + cx, :PAD, :] = value[:, :PAD]
        win[v, 1:1 + cx, PAD + cy:, :] = value[:, PAD:]
    edge_planes(range(6, 10), 0, PAD)
    edge_planes(range(6, 10), PAD + cy, PAD)
    speed_z = speed_of(own, terms, 2)
    largest_z = jnp.maximum(speed_z, z_dn(speed_z))
    around = slice(0, cx + 2)
    speed_x = tiles(SPEED, around)
    largest_x = jnp.maximum(speed_x[:-1], speed_x[1:])
    for v in (4, 6):
        u = tiles(FIELD[v], around)
        fz = None if v == 6 else own[v] * own[3] - own[6] * own[v - 3]
        fx = None if v == 4 else tiles(FLUX[v], around)
        lows = face(None if fx is None else fx[:-1], None if fx is None else fx[1:], u[:-1], u[1:], largest_x)
        new = own[v] - COURANT * (z_change(own[v], fz, largest_z) + side[v] + (lows[1:] - lows[:-1]))
        fwin[v // 6, :, 0:PAD, :] = new[:, :PAD]
        fwin[v // 6, :, PAD + cy:, :] = new[:, PAD:]

    key = own_v[0] * ri + row_v[...]
    at = lax.broadcasted_iota(jnp.int32, (nx * ri, cx * cy), 0)
    pair, rest = at // (2 * ri), at % (2 * ri)
    hot = (key == (pair + (rest // ri) * pairs) * ri + rest % ri).astype(BF16)
    hot = jnp.concatenate([hot, hot, hot], axis=1)

    for r in doubling[-1:]:
        hear(r)
    for c in cond_copies[2:]:
        c.start()
    each(has_xd, xc[:1], "wait_recv")
    each(has_xu, xc[1:], "wait_recv")
    edge_planes(range(5, 11), PAD, cy)

    def outer_faces(v, f_of):
        faces = []
        for lo in (0, cx):
            u = [win[FIELD[v], lo + i, PAD:PAD + cy, :] for i in range(2)]
            f = [f_of(v, lo + i) for i in range(2)]
            most = jnp.maximum(win[SPEED, lo, PAD:PAD + cy, :], win[SPEED, lo + 1, PAD:PAD + cy, :])
            faces.append(COURANT * face(f[0], f[1], u[0], u[1], most))
        return faces

    def b_flux(v, at):
        return None if v == 4 else win[FLUX[v], at, PAD:PAD + cy, :]

    def close(values, faces):
        planes = [values[i] for i in range(cx)]
        planes[0] = planes[0] + faces[0]
        planes[-1] = planes[-1] - faces[1]
        return planes

    field, outer = {}, {}
    for v in (4, 6, 5):
        outer[v] = outer_faces(v, b_flux)
        field[v] = close(out[v] if v == 4 else pstage[v - 5], outer[v])
        for i in range(cx):
            out[v, i] = field[v][i]
            if v != 5:
                fwin[v // 6, i, PAD:PAD + cy, :] = field[v][i]

    @pl.when(p == 0)
    def _():
        fwin[:, :, PAD - 1:PAD, :] = fwin[:, :, PAD:PAD + 1, :]

    @pl.when(p == ny - 1)
    def _():
        fwin[:, :, PAD + cy:PAD + cy + 1, :] = fwin[:, :, PAD + cy - 1:PAD + cy, :]

    def d_y(v):
        a = fwin[v // 6]
        return 0.5 * (roll(a, -1, 1) - roll(a, 1, 1))[:, PAD:PAD + cy, :]

    def d_z(a):
        return 0.5 * (jnp.where(last, a, roll(a, -1, 2)) - z_dn(a))

    bx, by, bz = [jnp.stack(field[v]) for v in (4, 5, 6)]
    jx = d_y(6) - d_z(by)
    size = jnp.sqrt(bx * bx + by * by + bz * bz)
    dzx, dyx = d_z(bx), d_y(4)

    each(has_xd, pc[:1], "wait_recv")
    each(has_xu, pc[1:], "wait_recv")

    def d_x(v):
        lo = jnp.where(g == 0, field[v][0], pin[0, v - 5] - outer[v][0])
        hi = jnp.where(g == nx - 1, field[v][-1], pin[1, v - 5] + outer[v][1])
        a = jnp.stack([lo] + field[v] + [hi])
        return 0.5 * (a[2:] - a[:-2])

    jy = dzx - d_x(6)
    jz = d_x(5) - dyx
    current = (jx * bx + jy * by + jz * bz) / jnp.maximum(size, 1.0)
    current = current.reshape(cx * cy, nz)

    head = current.astype(BF16)
    tail = current - head.astype(F32)
    body_ = tail.astype(BF16)
    tail = (tail - body_.astype(F32)).astype(BF16)
    sums = jnp.dot(hot, jnp.concatenate([head, body_, tail], axis=0),
                   preferred_element_type=F32)
    part[...] = sums.reshape(pairs, 2, ri, nz)

    odd = lax.rem(p, 2)
    mate = (g, p + 1 - 2 * odd)
    out_g, out_p = jnp.where(odd == 1, beside[1][0], beside[-1][0]), jnp.where(odd == 1, beside[1][1], beside[-1][1])
    step = lax.rem(out_g - g + nx, nx)

    def own_copy(to):
        return remote(part.at[lax.rem(to, pairs)], part_in.at[0, g], as_.at[0], ar.at[0], (to, p))

    def outer_copy(to, first_row):
        some = pl.ds(first_row, ri - 1)
        return remote(part.at[lax.rem(to, pairs), :, some], part_in.at[1, g, :, some], as_.at[1], ar.at[1],
                      (lax.rem(to + step, nx), out_p))

    def send_own(k, carry):
        own_copy(lax.rem(g + k, nx)).start()
        return carry

    def send_outer(first_row):
        def send(k, carry):
            outer_copy(lax.rem(g + k, nx), first_row).start()
            return carry

        lax.fori_loop(0, nx, send, 0, unroll=nx <= 8)

    lax.fori_loop(1, nx, send_own, 0, unroll=nx <= 8)
    pl.when(odd == 1)(lambda: send_outer(1))
    pl.when(odd == 0)(lambda: send_outer(0))
    each(has_xu, xlate[:1], "start")
    each(has_xd, xlate[1:], "start")

    for c in cond_copies:
        c.wait_recv()
    lines = 6 * ri
    row = lax.broadcasted_iota(jnp.int32, (lines, nz), 0)
    row = jnp.where(row >= 3 * ri, row - 3 * ri, row)
    place = lax.rem(b, half)
    low_row = jnp.where(place == half // 2, ri, 0)
    high_row = jnp.where(place == half // 2 - 1, 2 * ri, 3 * ri)
    valid = (row >= low_row) & (row < high_row)
    pw = jnp.where(valid, cwin[:, 0].reshape(lines, nz), 0.0)
    hw = jnp.where(valid, cwin[:, 1].reshape(lines, nz), 0.0)
    own_shift = cwin[0:3, 2].reshape(3 * ri, nz).astype(jnp.int32)
    col = lax.broadcasted_iota(jnp.int32, (3 * ri, nz), 1)
    cols = jnp.concatenate(
        [(col + own_shift) % nz, (col + (nz - own_shift)) % nz], axis=0)
    he, hwst = east(hw), west(hw)
    coef = [
        0.5 * (pw + up(pw)), 0.5 * (pw + down(pw)),
        0.5 * (pw + east(pw)), 0.5 * (pw + west(pw)),
        0.125 * (hw + up(he)), 0.125 * (hw + up(hwst)),
        0.125 * (hw + down(he)), 0.125 * (hw + down(hwst)),
    ]
    center = coef[0]
    for c in coef[1:]:
        center = center + c
    inv = jnp.where(valid, 1.0 / jnp.where(valid, center, 1.0), 0.0)
    pm = swap_by(cols, pw)
    both = jnp.where(valid, pw + pm, 1.0)
    c_up, c_down, c_east, c_west, c_ue, c_uw, c_de, c_dw = [c * inv for c in coef]
    wa, wb = jnp.where(valid, pw / both, 0.0), jnp.where(valid, pm / both, 0.0)
    for i, c in enumerate((
            inv, c_east, c_west, down(c_up), down(c_ue), -down(c_uw), up(c_down), -up(c_de), up(c_dw),
            wa, wb, east(wa), east(wb), west(wa), west(wb))):
        coef_out[i] = c
    for i, c in enumerate((cols, east(cols), west(cols))):
        cols_out[i] = c

    rest = (0, 1, 2, 3, 7)
    prim = [win[v, 1:1 + cx, PAD:PAD + cy, :] for v in ORDER]
    terms = cell_terms(prim)
    flux = flux_of(prim, terms, 0)
    for at, v in enumerate(rest):
        out[v] = x_inner(out[v], terms[0][v], flux[v])
        for side_at, plane in enumerate((0, cx - 1)):
            edge[0, at, side_at] = terms[0][v][plane]
            edge[1, at, side_at] = flux[v][plane]

    each(has_xu, [xc[0], pc[0]], "wait_send")
    each(has_xd, [xc[1], pc[1]], "wait_send")
    each(has_yu, yc[:1], "wait_send")
    each(has_yd, yc[1:], "wait_send")
    for c, to, _ in diag:
        each(to, [c], "wait_send")
    for c in cond_copies:
        c.wait_send()
    def taken(slot, sems):
        some = part_in.at[slot, pl.ds(0, nx - 1 if slot == 0 else nx), :, pl.ds(0, ri if slot == 0 else ri - 1)]
        pltpu.make_async_copy(some, some, sems.at[slot]).wait()

    def total_of(slot):
        def add(at, total):
            return total + part_in[slot, at]
        return lax.fori_loop(1, nx, add, part_in[slot, 0], unroll=nx <= 8)

    taken(0, ar)
    part_in[0, g] = part[lax.rem(g, pairs)]
    shared[0] = total_of(0)
    to_mate = remote(shared.at[0], shared.at[1], hs.at[0], hr.at[0], mate)
    to_mate.start()
    each(has_xd, xlate[:1], "wait_recv")
    each(has_xu, xlate[1:], "wait_recv")

    def ghosts(v):
        return jnp.stack([win[v, at, PAD:PAD + cy, :] for at in (0, cx + 1)])

    prim = [ghosts(v) for v in ORDER]
    terms = cell_terms(prim)
    flux = flux_of(prim, terms, 0)
    speed = jnp.maximum(ghosts(SPEED), jnp.stack([win[SPEED, at, PAD:PAD + cy, :] for at in (1, cx)]))
    for at, v in enumerate(rest):
        u, f = terms[0][v], flux[v]
        own_u, own_f = edge[0, at], edge[1, at]
        low = face(f[0], own_f[0], u[0], own_u[0], speed[0])
        high = face(own_f[1], f[1], own_u[1], u[1], speed[1])
        low = jnp.where(g == 0, own_f[0], low)
        high = jnp.where(g == nx - 1, own_f[1], high)
        out[v, 0] = out[v, 0] + COURANT * low
        out[v, cx - 1] = out[v, cx - 1] - COURANT * high

    each(has_xu, xlate[:1], "wait_send")
    each(has_xd, xlate[1:], "wait_send")
    taken(0, as_)
    taken(1, as_)
    taken(1, ar)
    outer_sum = total_of(1)
    to_mate.wait_recv()

    def place_sums(slot, total, block):
        northern = block < half
        src_out[0, slot] = jnp.where(northern, total[0], total[1])
        src_out[1, slot] = jnp.where(northern, total[1], total[0])

    mate_sum = shared[1]
    place_sums(0, jnp.where(odd == 1, mate_sum, outer_sum), lax.rem(b + n - 1, n))
    place_sums(1, shared[0], b)
    place_sums(2, jnp.where(odd == 1, outer_sum, mate_sum), lax.rem(b + 1, n))

    to_mate.wait_send()


def sweep_kernel(con, src, coef, cols_ref, out, phi_out, phi_v, sems):
    write = pltpu.make_async_copy(con, out, sems.at[0])
    write.start()
    inv, ce, cw, u0, u1, u2, d0, d1, d2, wa, wb, wae, wbe, waw, wbw = [coef[i] for i in range(COEFS)]
    cols, colse, colsw = [cols_ref[i] for i in range(3)]
    ri = phi_v.shape[0]
    source = src[...].reshape(inv.shape) * inv

    def triple(a):
        h = a.shape[0] // 2
        other = jnp.concatenate([a[h:], a[:h]], axis=0)
        take = lambda c: jnp.take_along_axis(other, c, axis=1)
        return wa * a + wb * take(cols), wae * east(a) + wbe * take(colse), waw * west(a) + wbw * take(colsw)

    acc = source
    for _ in range(SWEEPS - 1):
        phi, e, w = triple(acc)
        acc = (source + (ce * e + cw * w)) + (up(u0 * phi + u1 * e + u2 * w) + down(d0 * phi + d1 * e + d2 * w))
    phi = wa * acc + wb * swap_by(cols, acc)
    phi_v[...] = phi[ri:2 * ri]
    last = pltpu.make_async_copy(phi_v, phi_out, sems.at[1])
    last.start()
    write.wait()
    last.wait()


def body(sizes, density, velocity, magnetic, pressure, line_owner, line_row, pedersen, hall, mirror_shift):
    cx, cy, nz = density.shape
    ri = pedersen.shape[0]
    nx = sizes[0]
    any_ = pl.BlockSpec(memory_space=pl.ANY)
    vmem = pl.BlockSpec(memory_space=pltpu.VMEM)
    dma = pltpu.SemaphoreType.DMA
    con, src, coef, cols = pl.pallas_call(
        functools.partial(flux_kernel, sizes),
        out_shape=(
            pltpu.VMEM((8, cx, cy, nz), F32),
            pltpu.VMEM((2, 3, ri, nz), F32),
            pltpu.VMEM((COEFS, 6 * ri, nz), F32),
            pltpu.VMEM((3, 6 * ri, nz), jnp.int32),
        ),
        in_specs=[any_] * 9,
        out_specs=(vmem,) * 4,
        scratch_shapes=[
            pltpu.VMEM((11, cx + 2, cy + 2 * PAD, nz), F32),
            pltpu.VMEM((2, cx, cy + 2 * PAD, nz), F32),
            pltpu.VMEM((2, cx, cy, nz), F32),
            pltpu.VMEM((2, 2, cy, nz), F32),
            pltpu.VMEM((2, 5, 2, cy, nz), F32),
            pltpu.VMEM((nx // 2, 2, ri, nz), F32),
            pltpu.VMEM((2, nx, 2, ri, nz), F32),
            pltpu.VMEM((2, 2, ri, nz), F32),
            pltpu.VMEM((6, 3, ri, nz), F32),
            pltpu.VMEM((1, 1, cx * cy), jnp.int32),
            pltpu.VMEM((1, cx * cy), jnp.int32),
            pltpu.SMEM((ri,), jnp.int32),
            dma((11,)),
            dma((2,)), dma((2,)), dma((2,)), dma((2,)), dma((2,)), dma((2,)),
            dma((4,)), dma((4,)), dma((2,)), dma((2,)), dma((6,)), dma((6,)),
            dma((2,)), dma((2,)), dma((1,)), dma((1,)),
            pltpu.SemaphoreType.REGULAR((8,)),
        ],
        compiler_params=pltpu.CompilerParams(collective_id=0, has_side_effects=True),
        name="flux_and_sources",
    )(density, velocity, magnetic, pressure, line_owner.reshape(1, 1, cx * cy), line_row.reshape(1, cx * cy),
      pedersen, hall, mirror_shift)
    return pl.pallas_call(
        sweep_kernel,
        out_shape=(
            jax.ShapeDtypeStruct((8, cx, cy, nz), F32),
            jax.ShapeDtypeStruct((ri, nz), F32),
        ),
        in_specs=[vmem] * 4,
        out_specs=(any_, any_),
        scratch_shapes=[pltpu.VMEM((ri, nz), F32), dma((2,))],
        name="sweeps",
    )(*[pltpu.with_memory_space_constraint(a, pltpu.VMEM) for a in (con, src, coef, cols)])


def solution(mesh):
    sizes = (mesh.shape["gx"], mesh.shape["pb"])
    in_specs = (
        P("gx", "pb", None),
        P(None, "gx", "pb", None),
        P(None, "gx", "pb", None),
        P("gx", "pb", None),
        P("gx", "pb", None, None),
        P("gx", "pb", None),
        P(("gx", "pb"), None),
        P(("gx", "pb"), None),
        P(("gx", "pb")),
    )
    out_specs = (P(None, "gx", "pb", None), P(("gx", "pb"), None))
    return jax.shard_map(
        functools.partial(body, sizes), mesh=mesh, in_specs=in_specs, out_specs=out_specs,
        check_vma=False)
```

```python
import functools

import jax
import jax.numpy as jnp
from jax import lax
from jax.experimental import pallas as pl
from jax.experimental.pallas import tpu as pltpu
from jax.sharding import PartitionSpec as P

SWEEPS = 8
GAMMA = 5.0 / 3.0
COURANT = 0.08
PAD = 8
COEFS = 15
F32 = jnp.float32
BF16 = jnp.bfloat16
MESH = pl.DeviceIdType.MESH
ORDER = (0, 2, 3, 4, 6, 5, 7, 1)
FIELD = {4: 6, 5: 5, 6: 7}
SPEED = 8
FLUX = {6: 9, 5: 10}


def cell_terms(prim):
    rho, vel, mag, pres = prim[0], prim[1:4], prim[4:7], prim[7]
    field_sq = mag[0] * mag[0] + mag[1] * mag[1] + mag[2] * mag[2]
    vel_sq = vel[0] * vel[0] + vel[1] * vel[1] + vel[2] * vel[2]
    half_sq = 0.5 * field_sq
    energy = pres * (1.0 / (GAMMA - 1.0)) + 0.5 * rho * vel_sq + half_sq
    total_p = pres + half_sq
    v_dot_b = vel[0] * mag[0] + vel[1] * mag[1] + vel[2] * mag[2]
    inv = 1.0 / rho
    sound_sq = GAMMA * pres * inv
    both = sound_sq + field_sq * inv
    momentum = [rho * v for v in vel]
    state = [rho] + momentum + list(mag) + [energy]
    return state, total_p, v_dot_b, sound_sq * inv, both


def flux_of(prim, terms, d):
    state, total_p, v_dot_b = terms[:3]
    vel, mag = prim[1:4], prim[4:7]
    vn, bn = vel[d], mag[d]
    flux = [state[1 + d]]
    for e in range(3):
        m = state[1 + e] * vn - mag[e] * bn
        flux.append(m + total_p if e == d else m)
    for e in range(3):
        flux.append(None if e == d else mag[e] * vn - bn * vel[e])
    flux.append((state[7] + total_p) * vn - bn * v_dot_b)
    return flux


def speed_of(prim, terms, d):
    sound_over, both = terms[3:]
    vn, bn = prim[1 + d], prim[4 + d]
    spread = both * both - 4.0 * sound_over * bn * bn
    fast = jnp.sqrt(0.5 * (both + jnp.sqrt(jnp.maximum(spread, 0.0))))
    return jnp.abs(vn) + fast


def face(f_lo, f_hi, u_lo, u_hi, largest):
    jump = largest * (u_hi - u_lo)
    return -0.5 * jump if f_lo is None else 0.5 * ((f_lo + f_hi) - jump)


def roll(values, shift, axis):
    return pltpu.roll(values, shift % values.shape[axis], axis)


def east(a):
    return roll(a, -1, 1)


def west(a):
    return roll(a, 1, 1)


def up(a):
    return roll(a, 1, 0)


def down(a):
    return roll(a, -1, 0)


def swap_by(cols, a):
    h = a.shape[0] // 2
    other = jnp.concatenate([a[h:], a[:h]], axis=0)
    return jnp.take_along_axis(other, cols, axis=1)


def flux_kernel(sizes, rho, vel, mag, pres, owner, line_row, ped, hall, shift,
                out, src_out, coef_out, cols_out,
                win, fwin, pstage, pin, edge, part, part_in, shared, cwin, own_v, row_v, shift_s,
                loc_sem, xs, xr, ls, lr, ys, yr, ds, dr, ps, pr, cs, cr, as_, ar, hs, hr, far):
    nx, ny = sizes
    cx, cy, nz = rho.shape
    ri = ped.shape[0]
    g, p = lax.axis_index("gx"), lax.axis_index("pb")
    n = nx * ny
    half = n // 2
    pairs = nx // 2
    b = g * ny + p
    wide = cy + 2 * PAD

    def dev(flat):
        return (lax.div(flat, ny), lax.rem(flat, ny))

    beside = {o: dev(lax.rem(b + o + n, n)) for o in (-1, 1)}

    barrier = pltpu.get_barrier_semaphore()

    for dg in (1, -1, 0, 2, -2):
        inside = (g + dg >= 0) & (g + dg < nx)

        @pl.when(inside)
        def _(to=jnp.clip(g + dg, 0, nx - 1), dg=dg):
            for o in (0, 1, -1):
                if (o or dg) and (o == 0 or abs(dg) < 2):
                    pl.semaphore_signal(
                        barrier, inc=1, device_id=(to, beside[o][1] if o else p), device_id_type=MESH)

    at_end = (b == 0) | (b == n - 1)

    @pl.when(at_end)
    def _():
        pl.semaphore_signal(barrier, inc=1, device_id=dev(n - 1 - b), device_id_type=MESH)

    doubling = [1 << i for i in range(1, 32) if 1 << i < nx]

    def pass_on(r):
        for to in (g + r, g - r):
            @pl.when((to >= 0) & (to < nx))
            def _(to=jnp.clip(to, 0, nx - 1), at=doubling.index(r)):
                pl.semaphore_signal(far.at[at], inc=1, device_id=(to, p), device_id_type=MESH)

    def hear(r):
        count = (g + r < nx).astype(jnp.int32) + (g - r >= 0).astype(jnp.int32)
        pl.semaphore_wait(far.at[doubling.index(r)], count)

    rows = pl.ds(PAD, cy)
    mid = pl.ds(1, cx)
    loads = [
        (rho, win.at[0, mid, rows]), (vel, win.at[pl.ds(2, 3), mid, rows]),
        (pres, win.at[1, mid, rows]),
        (ped, cwin.at[1, 0]), (hall, cwin.at[1, 1]), (shift, shift_s),
        (owner, own_v), (line_row, row_v)]
    loads += [(mag.at[v - 4], win.at[FIELD[v], mid, rows]) for v in FIELD]
    loads = [pltpu.make_async_copy(s, d, loc_sem.at[i]) for i, (s, d) in enumerate(loads)]
    for c in loads:
        c.start()
    for c in loads:
        c.wait()

    row8 = lax.broadcasted_iota(jnp.int32, (ri, nz), 0)
    sh = jnp.zeros((ri, nz), F32)
    for i in range(ri):
        sh = jnp.where(row8 == i, shift_s[i].astype(F32), sh)
    cwin[1, 2] = sh

    lane = lax.broadcasted_iota(jnp.int32, (cx, cy, nz), 2)
    first, last = lane == 0, lane == nz - 1

    def z_dn(a):
        return jnp.where(first[:, :a.shape[1]], a, roll(a, 1, 2))

    def z_change(u, f, largest):
        low = face(None if f is None else z_dn(f), f, z_dn(u), u, largest)
        top = jnp.zeros_like(u) if f is None else f
        high = jnp.where(last[:, :u.shape[1]], top, roll(low, -1, 2))
        return high - low

    prim = [win[v, 1:1 + cx, PAD:PAD + cy, :] for v in ORDER]
    terms = cell_terms(prim)
    win[SPEED, 1:1 + cx, PAD:PAD + cy, :] = speed_of(prim, terms, 0)
    for v in FLUX:
        win[FLUX[v], 1:1 + cx, PAD:PAD + cy, :] = prim[v] * prim[1] - prim[4] * prim[v - 3]
    flux, speed = flux_of(prim, terms, 2), speed_of(prim, terms, 2)
    largest = jnp.maximum(speed, z_dn(speed))
    for v in range(8):
        out[v] = terms[0][v] - COURANT * z_change(terms[0][v], flux[v], largest)

    greeted = 3 * (jnp.minimum(g + 1, nx - 1) - jnp.maximum(g - 1, 0) + 1) - 1
    for cond in (g + 2 < nx, g >= 2, at_end):
        greeted = greeted + cond.astype(jnp.int32)
    pl.semaphore_wait(barrier, greeted)
    for r in doubling[:1]:
        pass_on(r)

    def remote(src, dst, send, recv, where):
        return pltpu.make_async_remote_copy(
            src_ref=src, dst_ref=dst, send_sem=send, recv_sem=recv,
            device_id=where, device_id_type=MESH)

    g_up, g_dn = jnp.minimum(g + 1, nx - 1), jnp.maximum(g - 1, 0)
    p_up, p_dn = jnp.minimum(p + 1, ny - 1), jnp.maximum(p - 1, 0)
    has_xu, has_xd, has_yu, has_yd = g < nx - 1, g > 0, p < ny - 1, p > 0

    def each(cond, copies, act):
        @pl.when(cond)
        def _():
            for c in copies:
                getattr(c, act)()

    def x_pair(at, count, send, recv):
        return [
            remote(win.at[pl.ds(at, count), s, rows], win.at[pl.ds(at, count), d, rows],
                   send.at[way], recv.at[way], (where, p))
            for way, (s, d, where) in enumerate(((cx, 0, g_up), (1, cx + 1, g_dn)))]

    xc = x_pair(5, 6, xs, xr)
    xlate = x_pair(0, 5, ls, lr)
    yc = [
        remote(win.at[pl.ds(0, 8), mid, pl.ds(s, PAD)], win.at[pl.ds(0, 8), mid, pl.ds(d, PAD)],
               ys.at[way], yr.at[way], (g, where))
        for way, (s, d, where) in enumerate(((cy, 0, p_up), (PAD, PAD + cy, p_dn)))]
    diag = []
    for i, (xu, yu) in enumerate(((1, 1), (1, 0), (0, 1), (0, 0))):
        s_x, d_x, to_g = (cx, 0, g_up) if xu else (1, cx + 1, g_dn)
        s_y, d_y, to_p = (PAD + cy - 1, PAD - 1, p_up) if yu else (PAD, PAD + cy, p_dn)
        c = remote(win.at[pl.ds(6, 4), s_x, pl.ds(s_y, 1)], win.at[pl.ds(6, 4), d_x, pl.ds(d_y, 1)],
                   ds.at[i], dr.at[i], (to_g, to_p))
        to = (has_xu if xu else has_xd) & (has_yu if yu else has_yd)
        come = (has_xd if xu else has_xu) & (has_yd if yu else has_yu)
        diag.append((c, to, come))
    ion = [
        (lax.rem(b + 1, n), 0),
        (lax.rem(b + n - 1, n), 2),
        (lax.rem(b + half + 1, n), 3),
        (lax.rem(b + half, n), 4),
        (lax.rem(b + half + n - 1, n), 5),
    ]
    cond_copies = [
        remote(cwin.at[1, pl.ds(0, 3 if slot < 3 else 2)], cwin.at[slot, pl.ds(0, 3 if slot < 3 else 2)],
               cs.at[slot], cr.at[slot], dev(flat)) for flat, slot in ion]

    each(has_yu, yc[:1], "start")
    each(has_yd, yc[1:], "start")
    for c, to, _ in diag:
        each(to, [c], "start")
    each(has_xu, xc[:1], "start")
    each(has_xd, xc[1:], "start")
    for c in cond_copies[:2]:
        c.start()

    each(has_yd, yc[:1], "wait_recv")
    each(has_yu, yc[1:], "wait_recv")

    @pl.when(p == 0)
    def _():
        for v in range(8):
            win[v, 1:1 + cx, PAD - 1:PAD, :] = win[v, 1:1 + cx, PAD:PAD + 1, :]

    @pl.when(p == ny - 1)
    def _():
        for v in range(8):
            win[v, 1:1 + cx, PAD + cy:PAD + cy + 1, :] = win[v, 1:1 + cx, PAD + cy - 1:PAD + cy, :]

    def x_inner(values, u, f):
        if cx == 1:
            return values
        speed = win[SPEED, 1:1 + cx, PAD:PAD + cy, :]
        lows = face(None if f is None else f[:-1], None if f is None else f[1:], u[:-1], u[1:],
                    jnp.maximum(speed[:-1], speed[1:]))
        none = jnp.zeros_like(lows[:1])
        return values - COURANT * (jnp.concatenate([lows, none], 0) - jnp.concatenate([none, lows], 0))

    prim = [win[v, 1:1 + cx] for v in ORDER]
    terms = cell_terms(prim)
    flux, speed = flux_of(prim, terms, 1), speed_of(prim, terms, 1)
    largest = jnp.maximum(speed, roll(speed, 1, 1))

    def y_change(v):
        u, f = terms[0][v], flux[v]
        low = face(None if f is None else roll(f, 1, 1), f, roll(u, 1, 1), u, largest)
        return roll(low, -1, 1) - low

    def ends(a):
        return jnp.concatenate([a[:, :PAD], a[:, PAD + cy:]], axis=1)

    side = {}
    for v in (5, 6, 4):
        diff = y_change(v)
        if v != 5:
            side[v] = ends(diff)
        u = win[FIELD[v], 1:1 + cx, PAD:PAD + cy, :]
        f = None if v == 4 else win[FLUX[v], 1:1 + cx, PAD:PAD + cy, :]
        done = x_inner(out[v] - COURANT * diff[:, PAD:PAD + cy, :], u, f)
        if v == 4:
            out[v] = done
        else:
            pstage[v - 5] = done
        if v == 6:
            pc = [
                remote(pstage.at[:, s], pin.at[way], ps.at[way], pr.at[way], (where, p))
                for way, (s, where) in enumerate(((cx - 1, g_up), (0, g_dn)))]
            each(has_xu, pc[:1], "start")
            each(has_xd, pc[1:], "start")
            for at, r in enumerate(doubling[:-1]):
                hear(r)
                pass_on(doubling[at + 1])
    for v in (0, 1, 2, 3, 7):
        out[v] = out[v] - COURANT * y_change(v)[:, PAD:PAD + cy, :]

    for c, _, come in diag:
        each(come, [c], "wait_recv")

    def edge_planes(which, at, count):
        at = pl.ds(at, count)

        @pl.when(g == 0)
        def _():
            for v in which:
                win[v, 0, at, :] = win[v, 1, at, :]

        @pl.when(g == nx - 1)
        def _():
            for v in which:
                win[v, cx + 1, at, :] = win[v, cx, at, :]

    def tiles(v, at):
        return jnp.concatenate([win[v, at, :PAD, :], win[v, at, PAD + cy:, :]], axis=1)

    own = [tiles(v, slice(1, 1 + cx)) for v in ORDER]
    terms = cell_terms(own)
    for v, value in ((SPEED, speed_of(own, terms, 0)), (FLUX[6], own[6] * own[1] - own[4] * own[3])):
        win[v, 1:1 + cx, :PAD, :] = value[:, :PAD]
        win[v, 1:1 + cx, PAD + cy:, :] = value[:, PAD:]
    edge_planes(range(6, 10), 0, PAD)
    edge_planes(range(6, 10), PAD + cy, PAD)
    speed_z = speed_of(own, terms, 2)
    largest_z = jnp.maximum(speed_z, z_dn(speed_z))
    around = slice(0, cx + 2)
    speed_x = tiles(SPEED, around)
    largest_x = jnp.maximum(speed_x[:-1], speed_x[1:])
    for v in (4, 6):
        u = tiles(FIELD[v], around)
        fz = None if v == 6 else own[v] * own[3] - own[6] * own[v - 3]
        fx = None if v == 4 else tiles(FLUX[v], around)
        lows = face(None if fx is None else fx[:-1], None if fx is None else fx[1:], u[:-1], u[1:], largest_x)
        new = own[v] - COURANT * (z_change(own[v], fz, largest_z) + side[v] + (lows[1:] - lows[:-1]))
        fwin[v // 6, :, 0:PAD, :] = new[:, :PAD]
        fwin[v // 6, :, PAD + cy:, :] = new[:, PAD:]

    key = own_v[0] * ri + row_v[...]
    at = lax.broadcasted_iota(jnp.int32, (nx * ri, cx * cy), 0)
    pair, rest = at // (2 * ri), at % (2 * ri)
    hot = (key == (pair + (rest // ri) * pairs) * ri + rest % ri).astype(BF16)
    hot = jnp.concatenate([hot, hot, hot], axis=1)

    for r in doubling[-1:]:
        hear(r)
    for c in cond_copies[2:]:
        c.start()
    each(has_xd, xc[:1], "wait_recv")
    each(has_xu, xc[1:], "wait_recv")
    edge_planes(range(5, 11), PAD, cy)

    def outer_faces(v, f_of):
        faces = []
        for lo in (0, cx):
            u = [win[FIELD[v], lo + i, PAD:PAD + cy, :] for i in range(2)]
            f = [f_of(v, lo + i) for i in range(2)]
            most = jnp.maximum(win[SPEED, lo, PAD:PAD + cy, :], win[SPEED, lo + 1, PAD:PAD + cy, :])
            faces.append(COURANT * face(f[0], f[1], u[0], u[1], most))
        return faces

    def b_flux(v, at):
        return None if v == 4 else win[FLUX[v], at, PAD:PAD + cy, :]

    def close(values, faces):
        planes = [values[i] for i in range(cx)]
        planes[0] = planes[0] + faces[0]
        planes[-1] = planes[-1] - faces[1]
        return planes

    field, outer = {}, {}
    for v in (4, 6, 5):
        outer[v] = outer_faces(v, b_flux)
        field[v] = close(out[v] if v == 4 else pstage[v - 5], outer[v])
        for i in range(cx):
            out[v, i] = field[v][i]
            if v != 5:
                fwin[v // 6, i, PAD:PAD + cy, :] = field[v][i]

    @pl.when(p == 0)
    def _():
        fwin[:, :, PAD - 1:PAD, :] = fwin[:, :, PAD:PAD + 1, :]

    @pl.when(p == ny - 1)
    def _():
        fwin[:, :, PAD + cy:PAD + cy + 1, :] = fwin[:, :, PAD + cy - 1:PAD + cy, :]

    def d_y(v):
        a = fwin[v // 6]
        return 0.5 * (roll(a, -1, 1) - roll(a, 1, 1))[:, PAD:PAD + cy, :]

    def d_z(a):
        return 0.5 * (jnp.where(last, a, roll(a, -1, 2)) - z_dn(a))

    bx, by, bz = [jnp.stack(field[v]) for v in (4, 5, 6)]
    jx = d_y(6) - d_z(by)
    size = jnp.sqrt(bx * bx + by * by + bz * bz)
    dzx, dyx = d_z(bx), d_y(4)

    each(has_xd, pc[:1], "wait_recv")
    each(has_xu, pc[1:], "wait_recv")

    def d_x(v):
        lo = jnp.where(g == 0, field[v][0], pin[0, v - 5] - outer[v][0])
        hi = jnp.where(g == nx - 1, field[v][-1], pin[1, v - 5] + outer[v][1])
        a = jnp.stack([lo] + field[v] + [hi])
        return 0.5 * (a[2:] - a[:-2])

    jy = dzx - d_x(6)
    jz = d_x(5) - dyx
    current = (jx * bx + jy * by + jz * bz) / jnp.maximum(size, 1.0)
    current = current.reshape(cx * cy, nz)

    head = current.astype(BF16)
    tail = current - head.astype(F32)
    body_ = tail.astype(BF16)
    tail = (tail - body_.astype(F32)).astype(BF16)
    sums = jnp.dot(hot, jnp.concatenate([head, body_, tail], axis=0),
                   preferred_element_type=F32)
    part[...] = sums.reshape(pairs, 2, ri, nz)

    odd = lax.rem(p, 2)
    mate = (g, p + 1 - 2 * odd)
    out_g, out_p = jnp.where(odd == 1, beside[1][0], beside[-1][0]), jnp.where(odd == 1, beside[1][1], beside[-1][1])
    step = lax.rem(out_g - g + nx, nx)

    def own_copy(to):
        return remote(part.at[lax.rem(to, pairs)], part_in.at[0, g], as_.at[0], ar.at[0], (to, p))

    def outer_copy(to, first_row):
        some = pl.ds(first_row, ri - 1)
        return remote(part.at[lax.rem(to, pairs), :, some], part_in.at[1, g, :, some], as_.at[1], ar.at[1],
                      (lax.rem(to + step, nx), out_p))

    def send_own(k, carry):
        own_copy(lax.rem(g + k, nx)).start()
        return carry

    def send_outer(first_row):
        def send(k, carry):
            outer_copy(lax.rem(g + k, nx), first_row).start()
            return carry

        lax.fori_loop(0, nx, send, 0, unroll=nx <= 8)

    lax.fori_loop(1, nx, send_own, 0, unroll=nx <= 8)
    pl.when(odd == 1)(lambda: send_outer(1))
    pl.when(odd == 0)(lambda: send_outer(0))

    for c in cond_copies:
        c.wait_recv()
    each(has_xu, xlate[:1], "start")
    each(has_xd, xlate[1:], "start")
    lines = 6 * ri
    row = lax.broadcasted_iota(jnp.int32, (lines, nz), 0)
    row = jnp.where(row >= 3 * ri, row - 3 * ri, row)
    place = lax.rem(b, half)
    low_row = jnp.where(place == half // 2, ri, 0)
    high_row = jnp.where(place == half // 2 - 1, 2 * ri, 3 * ri)
    valid = (row >= low_row) & (row < high_row)
    pw = jnp.where(valid, cwin[:, 0].reshape(lines, nz), 0.0)
    hw = jnp.where(valid, cwin[:, 1].reshape(lines, nz), 0.0)
    own_shift = cwin[0:3, 2].reshape(3 * ri, nz).astype(jnp.int32)
    col = lax.broadcasted_iota(jnp.int32, (3 * ri, nz), 1)
    cols = jnp.concatenate(
        [(col + own_shift) % nz, (col + (nz - own_shift)) % nz], axis=0)
    he, hwst = east(hw), west(hw)
    coef = [
        0.5 * (pw + up(pw)), 0.5 * (pw + down(pw)),
        0.5 * (pw + east(pw)), 0.5 * (pw + west(pw)),
        0.125 * (hw + up(he)), 0.125 * (hw + up(hwst)),
        0.125 * (hw + down(he)), 0.125 * (hw + down(hwst)),
    ]
    center = coef[0]
    for c in coef[1:]:
        center = center + c
    inv = jnp.where(valid, 1.0 / jnp.where(valid, center, 1.0), 0.0)
    pm = swap_by(cols, pw)
    both = jnp.where(valid, pw + pm, 1.0)
    c_up, c_down, c_east, c_west, c_ue, c_uw, c_de, c_dw = [c * inv for c in coef]
    wa, wb = jnp.where(valid, pw / both, 0.0), jnp.where(valid, pm / both, 0.0)
    for i, c in enumerate((
            inv, c_east, c_west, down(c_up), down(c_ue), -down(c_uw), up(c_down), -up(c_de), up(c_dw),
            wa, wb, east(wa), east(wb), west(wa), west(wb))):
        coef_out[i] = c
    for i, c in enumerate((cols, east(cols), west(cols))):
        cols_out[i] = c

    rest = (0, 1, 2, 3, 7)
    prim = [win[v, 1:1 + cx, PAD:PAD + cy, :] for v in ORDER]
    terms = cell_terms(prim)
    flux = flux_of(prim, terms, 0)
    for at, v in enumerate(rest):
        out[v] = x_inner(out[v], terms[0][v], flux[v])
        for side_at, plane in enumerate((0, cx - 1)):
            edge[0, at, side_at] = terms[0][v][plane]
            edge[1, at, side_at] = flux[v][plane]

    each(has_xu, [xc[0], pc[0]], "wait_send")
    each(has_xd, [xc[1], pc[1]], "wait_send")
    each(has_yu, yc[:1], "wait_send")
    each(has_yd, yc[1:], "wait_send")
    for c, to, _ in diag:
        each(to, [c], "wait_send")
    for c in cond_copies:
        c.wait_send()
    def taken(slot, sems):
        some = part_in.at[slot, pl.ds(0, nx - 1 if slot == 0 else nx), :, pl.ds(0, ri if slot == 0 else ri - 1)]
        pltpu.make_async_copy(some, some, sems.at[slot]).wait()

    def total_of(slot):
        def add(at, total):
            return total + part_in[slot, at]
        return lax.fori_loop(1, nx, add, part_in[slot, 0], unroll=nx <= 8)

    taken(0, ar)
    part_in[0, g] = part[lax.rem(g, pairs)]
    shared[0] = total_of(0)
    to_mate = remote(shared.at[0], shared.at[1], hs.at[0], hr.at[0], mate)
    to_mate.start()
    each(has_xd, xlate[:1], "wait_recv")
    each(has_xu, xlate[1:], "wait_recv")

    def ghosts(v):
        return jnp.stack([win[v, at, PAD:PAD + cy, :] for at in (0, cx + 1)])

    prim = [ghosts(v) for v in ORDER]
    terms = cell_terms(prim)
    flux = flux_of(prim, terms, 0)
    speed = jnp.maximum(ghosts(SPEED), jnp.stack([win[SPEED, at, PAD:PAD + cy, :] for at in (1, cx)]))
    for at, v in enumerate(rest):
        u, f = terms[0][v], flux[v]
        own_u, own_f = edge[0, at], edge[1, at]
        low = face(f[0], own_f[0], u[0], own_u[0], speed[0])
        high = face(own_f[1], f[1], own_u[1], u[1], speed[1])
        low = jnp.where(g == 0, own_f[0], low)
        high = jnp.where(g == nx - 1, own_f[1], high)
        out[v, 0] = out[v, 0] + COURANT * low
        out[v, cx - 1] = out[v, cx - 1] - COURANT * high

    each(has_xu, xlate[:1], "wait_send")
    each(has_xd, xlate[1:], "wait_send")
    taken(0, as_)
    taken(1, as_)
    taken(1, ar)
    outer_sum = total_of(1)
    to_mate.wait_recv()

    def place_sums(slot, total, block):
        northern = block < half
        src_out[0, slot] = jnp.where(northern, total[0], total[1])
        src_out[1, slot] = jnp.where(northern, total[1], total[0])

    mate_sum = shared[1]
    place_sums(0, jnp.where(odd == 1, mate_sum, outer_sum), lax.rem(b + n - 1, n))
    place_sums(1, shared[0], b)
    place_sums(2, jnp.where(odd == 1, outer_sum, mate_sum), lax.rem(b + 1, n))

    to_mate.wait_send()


def sweep_kernel(con, src, coef, cols_ref, out, phi_out, phi_v, sems):
    write = pltpu.make_async_copy(con, out, sems.at[0])
    write.start()
    inv, ce, cw, u0, u1, u2, d0, d1, d2, wa, wb, wae, wbe, waw, wbw = [coef[i] for i in range(COEFS)]
    cols, colse, colsw = [cols_ref[i] for i in range(3)]
    ri = phi_v.shape[0]
    source = src[...].reshape(inv.shape) * inv

    def triple(a):
        h = a.shape[0] // 2
        other = jnp.concatenate([a[h:], a[:h]], axis=0)
        take = lambda c: jnp.take_along_axis(other, c, axis=1)
        return wa * a + wb * take(cols), wae * east(a) + wbe * take(colse), waw * west(a) + wbw * take(colsw)

    acc = source
    for _ in range(SWEEPS - 1):
        phi, e, w = triple(acc)
        acc = (source + (ce * e + cw * w)) + (up(u0 * phi + u1 * e + u2 * w) + down(d0 * phi + d1 * e + d2 * w))
    phi = wa * acc + wb * swap_by(cols, acc)
    phi_v[...] = phi[ri:2 * ri]
    last = pltpu.make_async_copy(phi_v, phi_out, sems.at[1])
    last.start()
    write.wait()
    last.wait()


def body(sizes, density, velocity, magnetic, pressure, line_owner, line_row, pedersen, hall, mirror_shift):
    cx, cy, nz = density.shape
    ri = pedersen.shape[0]
    nx = sizes[0]
    any_ = pl.BlockSpec(memory_space=pl.ANY)
    vmem = pl.BlockSpec(memory_space=pltpu.VMEM)
    dma = pltpu.SemaphoreType.DMA
    con, src, coef, cols = pl.pallas_call(
        functools.partial(flux_kernel, sizes),
        out_shape=(
            pltpu.VMEM((8, cx, cy, nz), F32),
            pltpu.VMEM((2, 3, ri, nz), F32),
            pltpu.VMEM((COEFS, 6 * ri, nz), F32),
            pltpu.VMEM((3, 6 * ri, nz), jnp.int32),
        ),
        in_specs=[any_] * 9,
        out_specs=(vmem,) * 4,
        scratch_shapes=[
            pltpu.VMEM((11, cx + 2, cy + 2 * PAD, nz), F32),
            pltpu.VMEM((2, cx, cy + 2 * PAD, nz), F32),
            pltpu.VMEM((2, cx, cy, nz), F32),
            pltpu.VMEM((2, 2, cy, nz), F32),
            pltpu.VMEM((2, 5, 2, cy, nz), F32),
            pltpu.VMEM((nx // 2, 2, ri, nz), F32),
            pltpu.VMEM((2, nx, 2, ri, nz), F32),
            pltpu.VMEM((2, 2, ri, nz), F32),
            pltpu.VMEM((6, 3, ri, nz), F32),
            pltpu.VMEM((1, 1, cx * cy), jnp.int32),
            pltpu.VMEM((1, cx * cy), jnp.int32),
            pltpu.SMEM((ri,), jnp.int32),
            dma((11,)),
            dma((2,)), dma((2,)), dma((2,)), dma((2,)), dma((2,)), dma((2,)),
            dma((4,)), dma((4,)), dma((2,)), dma((2,)), dma((6,)), dma((6,)),
            dma((2,)), dma((2,)), dma((1,)), dma((1,)),
            pltpu.SemaphoreType.REGULAR((8,)),
        ],
        compiler_params=pltpu.CompilerParams(collective_id=0, has_side_effects=True),
        name="flux_and_sources",
    )(density, velocity, magnetic, pressure, line_owner.reshape(1, 1, cx * cy), line_row.reshape(1, cx * cy),
      pedersen, hall, mirror_shift)
    return pl.pallas_call(
        sweep_kernel,
        out_shape=(
            jax.ShapeDtypeStruct((8, cx, cy, nz), F32),
            jax.ShapeDtypeStruct((ri, nz), F32),
        ),
        in_specs=[vmem] * 4,
        out_specs=(any_, any_),
        scratch_shapes=[pltpu.VMEM((ri, nz), F32), dma((2,))],
        name="sweeps",
    )(*[pltpu.with_memory_space_constraint(a, pltpu.VMEM) for a in (con, src, coef, cols)])


def solution(mesh):
    sizes = (mesh.shape["gx"], mesh.shape["pb"])
    in_specs = (
        P("gx", "pb", None),
        P(None, "gx", "pb", None),
        P(None, "gx", "pb", None),
        P("gx", "pb", None),
        P("gx", "pb", None, None),
        P("gx", "pb", None),
        P(("gx", "pb"), None),
        P(("gx", "pb"), None),
        P(("gx", "pb")),
    )
    out_specs = (P(None, "gx", "pb", None), P(("gx", "pb"), None))
    return jax.shard_map(
        functools.partial(body, sizes), mesh=mesh, in_specs=in_specs, out_specs=out_specs,
        check_vma=False)
```

```python
import functools

import jax
import jax.numpy as jnp
from jax import lax
from jax.experimental import pallas as pl
from jax.experimental.pallas import tpu as pltpu
from jax.sharding import PartitionSpec as P

SWEEPS = 8
GAMMA = 5.0 / 3.0
COURANT = 0.08
PAD = 8
COEFS = 15
F32 = jnp.float32
BF16 = jnp.bfloat16
MESH = pl.DeviceIdType.MESH
ORDER = (0, 2, 3, 4, 6, 5, 7, 1)
FIELD = {4: 6, 5: 5, 6: 7}
SPEED = 8
FLUX = {6: 9, 5: 10}


def cell_terms(prim):
    rho, vel, mag, pres = prim[0], prim[1:4], prim[4:7], prim[7]
    field_sq = mag[0] * mag[0] + mag[1] * mag[1] + mag[2] * mag[2]
    vel_sq = vel[0] * vel[0] + vel[1] * vel[1] + vel[2] * vel[2]
    half_sq = 0.5 * field_sq
    energy = pres * (1.0 / (GAMMA - 1.0)) + 0.5 * rho * vel_sq + half_sq
    total_p = pres + half_sq
    v_dot_b = vel[0] * mag[0] + vel[1] * mag[1] + vel[2] * mag[2]
    inv = 1.0 / rho
    sound_sq = GAMMA * pres * inv
    both = sound_sq + field_sq * inv
    momentum = [rho * v for v in vel]
    state = [rho] + momentum + list(mag) + [energy]
    return state, total_p, v_dot_b, sound_sq * inv, both


def flux_of(prim, terms, d):
    state, total_p, v_dot_b = terms[:3]
    vel, mag = prim[1:4], prim[4:7]
    vn, bn = vel[d], mag[d]
    flux = [state[1 + d]]
    for e in range(3):
        m = state[1 + e] * vn - mag[e] * bn
        flux.append(m + total_p if e == d else m)
    for e in range(3):
        flux.append(None if e == d else mag[e] * vn - bn * vel[e])
    flux.append((state[7] + total_p) * vn - bn * v_dot_b)
    return flux


def speed_of(prim, terms, d):
    sound_over, both = terms[3:]
    vn, bn = prim[1 + d], prim[4 + d]
    spread = both * both - 4.0 * sound_over * bn * bn
    fast = jnp.sqrt(0.5 * (both + jnp.sqrt(jnp.maximum(spread, 0.0))))
    return jnp.abs(vn) + fast


def face(f_lo, f_hi, u_lo, u_hi, largest):
    jump = largest * (u_hi - u_lo)
    return -0.5 * jump if f_lo is None else 0.5 * ((f_lo + f_hi) - jump)


def roll(values, shift, axis):
    return pltpu.roll(values, shift % values.shape[axis], axis)


def east(a):
    return roll(a, -1, 1)


def west(a):
    return roll(a, 1, 1)


def up(a):
    return roll(a, 1, 0)


def down(a):
    return roll(a, -1, 0)


def swap_by(cols, a):
    h = a.shape[0] // 2
    other = jnp.concatenate([a[h:], a[:h]], axis=0)
    return jnp.take_along_axis(other, cols, axis=1)


def flux_kernel(sizes, rho, vel, mag, pres, owner, line_row, ped, hall, shift,
                out, src_out, coef_out, cols_out,
                win, fwin, pstage, pin, edge, part, part_in, shared, cwin, own_v, row_v, shift_s,
                loc_sem, xs, xr, ls, lr, ys, yr, ds, dr, ps, pr, cs, cr, as_, ar, hs, hr, far):
    nx, ny = sizes
    cx, cy, nz = rho.shape
    ri = ped.shape[0]
    g, p = lax.axis_index("gx"), lax.axis_index("pb")
    n = nx * ny
    half = n // 2
    pairs = nx // 2
    b = g * ny + p
    wide = cy + 2 * PAD

    def dev(flat):
        return (lax.div(flat, ny), lax.rem(flat, ny))

    beside = {o: dev(lax.rem(b + o + n, n)) for o in (-1, 1)}

    barrier = pltpu.get_barrier_semaphore()

    for dg in (1, -1, 0, 2, -2):
        inside = (g + dg >= 0) & (g + dg < nx)

        @pl.when(inside)
        def _(to=jnp.clip(g + dg, 0, nx - 1), dg=dg):
            for o in (0, 1, -1):
                if (o or dg) and (o == 0 or abs(dg) < 2):
                    pl.semaphore_signal(
                        barrier, inc=1, device_id=(to, beside[o][1] if o else p), device_id_type=MESH)

    at_end = (b == 0) | (b == n - 1)

    @pl.when(at_end)
    def _():
        pl.semaphore_signal(barrier, inc=1, device_id=dev(n - 1 - b), device_id_type=MESH)

    doubling = [1 << i for i in range(1, 32) if 1 << i < nx]

    def pass_on(r):
        for to in (g + r, g - r):
            @pl.when((to >= 0) & (to < nx))
            def _(to=jnp.clip(to, 0, nx - 1), at=doubling.index(r)):
                pl.semaphore_signal(far.at[at], inc=1, device_id=(to, p), device_id_type=MESH)

    def hear(r):
        count = (g + r < nx).astype(jnp.int32) + (g - r >= 0).astype(jnp.int32)
        pl.semaphore_wait(far.at[doubling.index(r)], count)

    rows = pl.ds(PAD, cy)
    mid = pl.ds(1, cx)
    loads = [
        (rho, win.at[0, mid, rows]), (vel, win.at[pl.ds(2, 3), mid, rows]),
        (pres, win.at[1, mid, rows]),
        (ped, cwin.at[1, 0]), (hall, cwin.at[1, 1]), (shift, shift_s),
        (owner, own_v), (line_row, row_v)]
    loads += [(mag.at[v - 4], win.at[FIELD[v], mid, rows]) for v in FIELD]
    loads = [pltpu.make_async_copy(s, d, loc_sem.at[i]) for i, (s, d) in enumerate(loads)]
    for c in loads:
        c.start()
    for c in loads:
        c.wait()

    row8 = lax.broadcasted_iota(jnp.int32, (ri, nz), 0)
    sh = jnp.zeros((ri, nz), F32)
    for i in range(ri):
        sh = jnp.where(row8 == i, shift_s[i].astype(F32), sh)
    cwin[1, 2] = sh

    lane = lax.broadcasted_iota(jnp.int32, (cx, cy, nz), 2)
    first, last = lane == 0, lane == nz - 1

    def z_dn(a):
        return jnp.where(first[:, :a.shape[1]], a, roll(a, 1, 2))

    def z_change(u, f, largest):
        low = face(None if f is None else z_dn(f), f, z_dn(u), u, largest)
        top = jnp.zeros_like(u) if f is None else f
        high = jnp.where(last[:, :u.shape[1]], top, roll(low, -1, 2))
        return high - low

    prim = [win[v, 1:1 + cx, PAD:PAD + cy, :] for v in ORDER]
    terms = cell_terms(prim)
    win[SPEED, 1:1 + cx, PAD:PAD + cy, :] = speed_of(prim, terms, 0)
    for v in FLUX:
        win[FLUX[v], 1:1 + cx, PAD:PAD + cy, :] = prim[v] * prim[1] - prim[4] * prim[v - 3]
    flux, speed = flux_of(prim, terms, 2), speed_of(prim, terms, 2)
    largest = jnp.maximum(speed, z_dn(speed))
    for v in range(8):
        out[v] = terms[0][v] - COURANT * z_change(terms[0][v], flux[v], largest)

    greeted = 3 * (jnp.minimum(g + 1, nx - 1) - jnp.maximum(g - 1, 0) + 1) - 1
    for cond in (g + 2 < nx, g >= 2, at_end):
        greeted = greeted + cond.astype(jnp.int32)
    pl.semaphore_wait(barrier, greeted)
    for r in doubling[:1]:
        pass_on(r)

    def remote(src, dst, send, recv, where):
        return pltpu.make_async_remote_copy(
            src_ref=src, dst_ref=dst, send_sem=send, recv_sem=recv,
            device_id=where, device_id_type=MESH)

    g_up, g_dn = jnp.minimum(g + 1, nx - 1), jnp.maximum(g - 1, 0)
    p_up, p_dn = jnp.minimum(p + 1, ny - 1), jnp.maximum(p - 1, 0)
    has_xu, has_xd, has_yu, has_yd = g < nx - 1, g > 0, p < ny - 1, p > 0

    def each(cond, copies, act):
        @pl.when(cond)
        def _():
            for c in copies:
                getattr(c, act)()

    def x_pair(at, count, send, recv):
        return [
            remote(win.at[pl.ds(at, count), s, rows], win.at[pl.ds(at, count), d, rows],
                   send.at[way], recv.at[way], (where, p))
            for way, (s, d, where) in enumerate(((cx, 0, g_up), (1, cx + 1, g_dn)))]

    xc = x_pair(5, 6, xs, xr)
    xlate = x_pair(0, 5, ls, lr)
    yc = [
        remote(win.at[pl.ds(0, 8), mid, pl.ds(s, 2)], win.at[pl.ds(0, 8), mid, pl.ds(d, 2)],
               ys.at[way], yr.at[way], (g, where))
        for way, (s, d, where) in enumerate(((PAD + cy - 2, PAD - 2, p_up), (PAD, PAD + cy, p_dn)))]
    diag = []
    for i, (xu, yu) in enumerate(((1, 1), (1, 0), (0, 1), (0, 0))):
        s_x, d_x, to_g = (cx, 0, g_up) if xu else (1, cx + 1, g_dn)
        s_y, d_y, to_p = (PAD + cy - 1, PAD - 1, p_up) if yu else (PAD, PAD + cy, p_dn)
        c = remote(win.at[pl.ds(6, 4), s_x, pl.ds(s_y, 1)], win.at[pl.ds(6, 4), d_x, pl.ds(d_y, 1)],
                   ds.at[i], dr.at[i], (to_g, to_p))
        to = (has_xu if xu else has_xd) & (has_yu if yu else has_yd)
        come = (has_xd if xu else has_xu) & (has_yd if yu else has_yu)
        diag.append((c, to, come))
    ion = [
        (lax.rem(b + 1, n), 0),
        (lax.rem(b + n - 1, n), 2),
        (lax.rem(b + half + 1, n), 3),
        (lax.rem(b + half, n), 4),
        (lax.rem(b + half + n - 1, n), 5),
    ]
    cond_copies = [
        remote(cwin.at[1, pl.ds(0, 3 if slot < 3 else 2)], cwin.at[slot, pl.ds(0, 3 if slot < 3 else 2)],
               cs.at[slot], cr.at[slot], dev(flat)) for flat, slot in ion]

    each(has_yu, yc[:1], "start")
    each(has_yd, yc[1:], "start")
    for c, to, _ in diag:
        each(to, [c], "start")
    each(has_xu, xc[:1], "start")
    each(has_xd, xc[1:], "start")

    each(has_yd, yc[:1], "wait_recv")
    each(has_yu, yc[1:], "wait_recv")

    @pl.when(p == 0)
    def _():
        for v in range(8):
            win[v, 1:1 + cx, PAD - 1:PAD, :] = win[v, 1:1 + cx, PAD:PAD + 1, :]

    @pl.when(p == ny - 1)
    def _():
        for v in range(8):
            win[v, 1:1 + cx, PAD + cy:PAD + cy + 1, :] = win[v, 1:1 + cx, PAD + cy - 1:PAD + cy, :]

    def x_inner(values, u, f):
        if cx == 1:
            return values
        speed = win[SPEED, 1:1 + cx, PAD:PAD + cy, :]
        lows = face(None if f is None else f[:-1], None if f is None else f[1:], u[:-1], u[1:],
                    jnp.maximum(speed[:-1], speed[1:]))
        none = jnp.zeros_like(lows[:1])
        return values - COURANT * (jnp.concatenate([lows, none], 0) - jnp.concatenate([none, lows], 0))

    prim = [win[v, 1:1 + cx] for v in ORDER]
    terms = cell_terms(prim)
    flux, speed = flux_of(prim, terms, 1), speed_of(prim, terms, 1)
    largest = jnp.maximum(speed, roll(speed, 1, 1))

    def y_change(v):
        u, f = terms[0][v], flux[v]
        low = face(None if f is None else roll(f, 1, 1), f, roll(u, 1, 1), u, largest)
        return roll(low, -1, 1) - low

    def ends(a):
        return jnp.concatenate([a[:, :PAD], a[:, PAD + cy:]], axis=1)

    side = {}
    for v in (5, 6, 4):
        diff = y_change(v)
        if v != 5:
            side[v] = ends(diff)
        u = win[FIELD[v], 1:1 + cx, PAD:PAD + cy, :]
        f = None if v == 4 else win[FLUX[v], 1:1 + cx, PAD:PAD + cy, :]
        done = x_inner(out[v] - COURANT * diff[:, PAD:PAD + cy, :], u, f)
        if v == 4:
            out[v] = done
        else:
            pstage[v - 5] = done
        if v == 6:
            pc = [
                remote(pstage.at[:, s], pin.at[way], ps.at[way], pr.at[way], (where, p))
                for way, (s, where) in enumerate(((cx - 1, g_up), (0, g_dn)))]
            each(has_xu, pc[:1], "start")
            each(has_xd, pc[1:], "start")
            for at, r in enumerate(doubling[:-1]):
                hear(r)
                pass_on(doubling[at + 1])
    for v in (0, 1, 2, 3, 7):
        out[v] = out[v] - COURANT * y_change(v)[:, PAD:PAD + cy, :]

    for c, _, come in diag:
        each(come, [c], "wait_recv")

    def edge_planes(which, at, count):
        at = pl.ds(at, count)

        @pl.when(g == 0)
        def _():
            for v in which:
                win[v, 0, at, :] = win[v, 1, at, :]

        @pl.when(g == nx - 1)
        def _():
            for v in which:
                win[v, cx + 1, at, :] = win[v, cx, at, :]

    def tiles(v, at):
        return jnp.concatenate([win[v, at, :PAD, :], win[v, at, PAD + cy:, :]], axis=1)

    own = [tiles(v, slice(1, 1 + cx)) for v in ORDER]
    terms = cell_terms(own)
    for v, value in ((SPEED, speed_of(own, terms, 0)), (FLUX[6], own[6] * own[1] - own[4] * own[3])):
        win[v, 1:1 + cx, :PAD, :] = value[:, :PAD]
        win[v, 1:1 + cx, PAD + cy:, :] = value[:, PAD:]
    edge_planes(range(6, 10), 0, PAD)
    edge_planes(range(6, 10), PAD + cy, PAD)
    speed_z = speed_of(own, terms, 2)
    largest_z = jnp.maximum(speed_z, z_dn(speed_z))
    around = slice(0, cx + 2)
    speed_x = tiles(SPEED, around)
    largest_x = jnp.maximum(speed_x[:-1], speed_x[1:])
    for v in (4, 6):
        u = tiles(FIELD[v], around)
        fz = None if v == 6 else own[v] * own[3] - own[6] * own[v - 3]
        fx = None if v == 4 else tiles(FLUX[v], around)
        lows = face(None if fx is None else fx[:-1], None if fx is None else fx[1:], u[:-1], u[1:], largest_x)
        new = own[v] - COURANT * (z_change(own[v], fz, largest_z) + side[v] + (lows[1:] - lows[:-1]))
        fwin[v // 6, :, 0:PAD, :] = new[:, :PAD]
        fwin[v // 6, :, PAD + cy:, :] = new[:, PAD:]

    key = own_v[0] * ri + row_v[...]
    at = lax.broadcasted_iota(jnp.int32, (nx * ri, cx * cy), 0)
    pair, rest = at // (2 * ri), at % (2 * ri)
    hot = (key == (pair + (rest // ri) * pairs) * ri + rest % ri).astype(BF16)
    hot = jnp.concatenate([hot, hot, hot], axis=1)

    for r in doubling[-1:]:
        hear(r)
    for c in cond_copies:
        c.start()
    each(has_xd, xc[:1], "wait_recv")
    each(has_xu, xc[1:], "wait_recv")
    edge_planes(range(5, 11), PAD, cy)

    def outer_faces(v, f_of):
        faces = []
        for lo in (0, cx):
            u = [win[FIELD[v], lo + i, PAD:PAD + cy, :] for i in range(2)]
            f = [f_of(v, lo + i) for i in range(2)]
            most = jnp.maximum(win[SPEED, lo, PAD:PAD + cy, :], win[SPEED, lo + 1, PAD:PAD + cy, :])
            faces.append(COURANT * face(f[0], f[1], u[0], u[1], most))
        return faces

    def b_flux(v, at):
        return None if v == 4 else win[FLUX[v], at, PAD:PAD + cy, :]

    def close(values, faces):
        planes = [values[i] for i in range(cx)]
        planes[0] = planes[0] + faces[0]
        planes[-1] = planes[-1] - faces[1]
        return planes

    field, outer = {}, {}
    for v in (4, 6, 5):
        outer[v] = outer_faces(v, b_flux)
        field[v] = close(out[v] if v == 4 else pstage[v - 5], outer[v])
        for i in range(cx):
            out[v, i] = field[v][i]
            if v != 5:
                fwin[v // 6, i, PAD:PAD + cy, :] = field[v][i]

    @pl.when(p == 0)
    def _():
        fwin[:, :, PAD - 1:PAD, :] = fwin[:, :, PAD:PAD + 1, :]

    @pl.when(p == ny - 1)
    def _():
        fwin[:, :, PAD + cy:PAD + cy + 1, :] = fwin[:, :, PAD + cy - 1:PAD + cy, :]

    def d_y(v):
        a = fwin[v // 6]
        return 0.5 * (roll(a, -1, 1) - roll(a, 1, 1))[:, PAD:PAD + cy, :]

    def d_z(a):
        return 0.5 * (jnp.where(last, a, roll(a, -1, 2)) - z_dn(a))

    bx, by, bz = [jnp.stack(field[v]) for v in (4, 5, 6)]
    jx = d_y(6) - d_z(by)
    size = jnp.sqrt(bx * bx + by * by + bz * bz)
    dzx, dyx = d_z(bx), d_y(4)

    each(has_xd, pc[:1], "wait_recv")
    each(has_xu, pc[1:], "wait_recv")

    def d_x(v):
        lo = jnp.where(g == 0, field[v][0], pin[0, v - 5] - outer[v][0])
        hi = jnp.where(g == nx - 1, field[v][-1], pin[1, v - 5] + outer[v][1])
        a = jnp.stack([lo] + field[v] + [hi])
        return 0.5 * (a[2:] - a[:-2])

    jy = dzx - d_x(6)
    jz = d_x(5) - dyx
    current = (jx * bx + jy * by + jz * bz) / jnp.maximum(size, 1.0)
    current = current.reshape(cx * cy, nz)

    head = current.astype(BF16)
    tail = current - head.astype(F32)
    body_ = tail.astype(BF16)
    tail = (tail - body_.astype(F32)).astype(BF16)
    sums = jnp.dot(hot, jnp.concatenate([head, body_, tail], axis=0),
                   preferred_element_type=F32)
    part[...] = sums.reshape(pairs, 2, ri, nz)

    odd = lax.rem(p, 2)
    mate = (g, p + 1 - 2 * odd)
    out_g, out_p = jnp.where(odd == 1, beside[1][0], beside[-1][0]), jnp.where(odd == 1, beside[1][1], beside[-1][1])
    step = lax.rem(out_g - g + nx, nx)

    def own_copy(to):
        return remote(part.at[lax.rem(to, pairs)], part_in.at[0, g], as_.at[0], ar.at[0], (to, p))

    def outer_copy(to, first_row):
        some = pl.ds(first_row, ri - 1)
        return remote(part.at[lax.rem(to, pairs), :, some], part_in.at[1, g, :, some], as_.at[1], ar.at[1],
                      (lax.rem(to + step, nx), out_p))

    def send_own(k, carry):
        own_copy(lax.rem(g + k, nx)).start()
        return carry

    def send_outer(first_row):
        def send(k, carry):
            outer_copy(lax.rem(g + k, nx), first_row).start()
            return carry

        lax.fori_loop(0, nx, send, 0, unroll=nx <= 8)

    lax.fori_loop(1, nx, send_own, 0, unroll=nx <= 8)
    pl.when(odd == 1)(lambda: send_outer(1))
    pl.when(odd == 0)(lambda: send_outer(0))

    for c in cond_copies:
        c.wait_recv()
    each(has_xu, xlate[:1], "start")
    each(has_xd, xlate[1:], "start")
    lines = 6 * ri
    row = lax.broadcasted_iota(jnp.int32, (lines, nz), 0)
    row = jnp.where(row >= 3 * ri, row - 3 * ri, row)
    place = lax.rem(b, half)
    low_row = jnp.where(place == half // 2, ri, 0)
    high_row = jnp.where(place == half // 2 - 1, 2 * ri, 3 * ri)
    valid = (row >= low_row) & (row < high_row)
    pw = jnp.where(valid, cwin[:, 0].reshape(lines, nz), 0.0)
    hw = jnp.where(valid, cwin[:, 1].reshape(lines, nz), 0.0)
    own_shift = cwin[0:3, 2].reshape(3 * ri, nz).astype(jnp.int32)
    col = lax.broadcasted_iota(jnp.int32, (3 * ri, nz), 1)
    cols = jnp.concatenate(
        [(col + own_shift) % nz, (col + (nz - own_shift)) % nz], axis=0)
    he, hwst = east(hw), west(hw)
    coef = [
        0.5 * (pw + up(pw)), 0.5 * (pw + down(pw)),
        0.5 * (pw + east(pw)), 0.5 * (pw + west(pw)),
        0.125 * (hw + up(he)), 0.125 * (hw + up(hwst)),
        0.125 * (hw + down(he)), 0.125 * (hw + down(hwst)),
    ]
    center = coef[0]
    for c in coef[1:]:
        center = center + c
    inv = jnp.where(valid, 1.0 / jnp.where(valid, center, 1.0), 0.0)
    pm = swap_by(cols, pw)
    both = jnp.where(valid, pw + pm, 1.0)
    c_up, c_down, c_east, c_west, c_ue, c_uw, c_de, c_dw = [c * inv for c in coef]
    wa, wb = jnp.where(valid, pw / both, 0.0), jnp.where(valid, pm / both, 0.0)
    for i, c in enumerate((
            inv, c_east, c_west, down(c_up), down(c_ue), -down(c_uw), up(c_down), -up(c_de), up(c_dw),
            wa, wb, east(wa), east(wb), west(wa), west(wb))):
        coef_out[i] = c
    for i, c in enumerate((cols, east(cols), west(cols))):
        cols_out[i] = c

    rest = (0, 1, 2, 3, 7)
    prim = [win[v, 1:1 + cx, PAD:PAD + cy, :] for v in ORDER]
    terms = cell_terms(prim)
    flux = flux_of(prim, terms, 0)
    for at, v in enumerate(rest):
        out[v] = x_inner(out[v], terms[0][v], flux[v])
        for side_at, plane in enumerate((0, cx - 1)):
            edge[0, at, side_at] = terms[0][v][plane]
            edge[1, at, side_at] = flux[v][plane]

    each(has_xu, [xc[0], pc[0]], "wait_send")
    each(has_xd, [xc[1], pc[1]], "wait_send")
    each(has_yu, yc[:1], "wait_send")
    each(has_yd, yc[1:], "wait_send")
    for c, to, _ in diag:
        each(to, [c], "wait_send")
    for c in cond_copies:
        c.wait_send()
    def taken(slot, sems):
        some = part_in.at[slot, pl.ds(0, nx - 1 if slot == 0 else nx), :, pl.ds(0, ri if slot == 0 else ri - 1)]
        pltpu.make_async_copy(some, some, sems.at[slot]).wait()

    def total_of(slot):
        def add(at, total):
            return total + part_in[slot, at]
        return lax.fori_loop(1, nx, add, part_in[slot, 0], unroll=nx <= 8)

    taken(0, ar)
    part_in[0, g] = part[lax.rem(g, pairs)]
    shared[0] = total_of(0)
    to_mate = remote(shared.at[0], shared.at[1], hs.at[0], hr.at[0], mate)
    to_mate.start()
    each(has_xd, xlate[:1], "wait_recv")
    each(has_xu, xlate[1:], "wait_recv")

    def ghosts(v):
        return jnp.stack([win[v, at, PAD:PAD + cy, :] for at in (0, cx + 1)])

    prim = [ghosts(v) for v in ORDER]
    terms = cell_terms(prim)
    flux = flux_of(prim, terms, 0)
    speed = jnp.maximum(ghosts(SPEED), jnp.stack([win[SPEED, at, PAD:PAD + cy, :] for at in (1, cx)]))
    for at, v in enumerate(rest):
        u, f = terms[0][v], flux[v]
        own_u, own_f = edge[0, at], edge[1, at]
        low = face(f[0], own_f[0], u[0], own_u[0], speed[0])
        high = face(own_f[1], f[1], own_u[1], u[1], speed[1])
        low = jnp.where(g == 0, own_f[0], low)
        high = jnp.where(g == nx - 1, own_f[1], high)
        out[v, 0] = out[v, 0] + COURANT * low
        out[v, cx - 1] = out[v, cx - 1] - COURANT * high

    each(has_xu, xlate[:1], "wait_send")
    each(has_xd, xlate[1:], "wait_send")
    taken(0, as_)
    taken(1, as_)
    taken(1, ar)
    outer_sum = total_of(1)
    to_mate.wait_recv()

    def place_sums(slot, total, block):
        northern = block < half
        src_out[0, slot] = jnp.where(northern, total[0], total[1])
        src_out[1, slot] = jnp.where(northern, total[1], total[0])

    mate_sum = shared[1]
    place_sums(0, jnp.where(odd == 1, mate_sum, outer_sum), lax.rem(b + n - 1, n))
    place_sums(1, shared[0], b)
    place_sums(2, jnp.where(odd == 1, outer_sum, mate_sum), lax.rem(b + 1, n))

    to_mate.wait_send()


def sweep_kernel(con, src, coef, cols_ref, out, phi_out, phi_v, sems):
    write = pltpu.make_async_copy(con, out, sems.at[0])
    write.start()
    inv, ce, cw, u0, u1, u2, d0, d1, d2, wa, wb, wae, wbe, waw, wbw = [coef[i] for i in range(COEFS)]
    cols, colse, colsw = [cols_ref[i] for i in range(3)]
    ri = phi_v.shape[0]
    source = src[...].reshape(inv.shape) * inv

    def triple(a):
        h = a.shape[0] // 2
        other = jnp.concatenate([a[h:], a[:h]], axis=0)
        take = lambda c: jnp.take_along_axis(other, c, axis=1)
        return wa * a + wb * take(cols), wae * east(a) + wbe * take(colse), waw * west(a) + wbw * take(colsw)

    acc = source
    for _ in range(SWEEPS - 1):
        phi, e, w = triple(acc)
        acc = (source + (ce * e + cw * w)) + (up(u0 * phi + u1 * e + u2 * w) + down(d0 * phi + d1 * e + d2 * w))
    phi = wa * acc + wb * swap_by(cols, acc)
    phi_v[...] = phi[ri:2 * ri]
    last = pltpu.make_async_copy(phi_v, phi_out, sems.at[1])
    last.start()
    write.wait()
    last.wait()


def body(sizes, density, velocity, magnetic, pressure, line_owner, line_row, pedersen, hall, mirror_shift):
    cx, cy, nz = density.shape
    ri = pedersen.shape[0]
    nx = sizes[0]
    any_ = pl.BlockSpec(memory_space=pl.ANY)
    vmem = pl.BlockSpec(memory_space=pltpu.VMEM)
    dma = pltpu.SemaphoreType.DMA
    con, src, coef, cols = pl.pallas_call(
        functools.partial(flux_kernel, sizes),
        out_shape=(
            pltpu.VMEM((8, cx, cy, nz), F32),
            pltpu.VMEM((2, 3, ri, nz), F32),
            pltpu.VMEM((COEFS, 6 * ri, nz), F32),
            pltpu.VMEM((3, 6 * ri, nz), jnp.int32),
        ),
        in_specs=[any_] * 9,
        out_specs=(vmem,) * 4,
        scratch_shapes=[
            pltpu.VMEM((11, cx + 2, cy + 2 * PAD, nz), F32),
            pltpu.VMEM((2, cx, cy + 2 * PAD, nz), F32),
            pltpu.VMEM((2, cx, cy, nz), F32),
            pltpu.VMEM((2, 2, cy, nz), F32),
            pltpu.VMEM((2, 5, 2, cy, nz), F32),
            pltpu.VMEM((nx // 2, 2, ri, nz), F32),
            pltpu.VMEM((2, nx, 2, ri, nz), F32),
            pltpu.VMEM((2, 2, ri, nz), F32),
            pltpu.VMEM((6, 3, ri, nz), F32),
            pltpu.VMEM((1, 1, cx * cy), jnp.int32),
            pltpu.VMEM((1, cx * cy), jnp.int32),
            pltpu.SMEM((ri,), jnp.int32),
            dma((11,)),
            dma((2,)), dma((2,)), dma((2,)), dma((2,)), dma((2,)), dma((2,)),
            dma((4,)), dma((4,)), dma((2,)), dma((2,)), dma((6,)), dma((6,)),
            dma((2,)), dma((2,)), dma((1,)), dma((1,)),
            pltpu.SemaphoreType.REGULAR((8,)),
        ],
        compiler_params=pltpu.CompilerParams(collective_id=0, has_side_effects=True),
        name="flux_and_sources",
    )(density, velocity, magnetic, pressure, line_owner.reshape(1, 1, cx * cy), line_row.reshape(1, cx * cy),
      pedersen, hall, mirror_shift)
    return pl.pallas_call(
        sweep_kernel,
        out_shape=(
            jax.ShapeDtypeStruct((8, cx, cy, nz), F32),
            jax.ShapeDtypeStruct((ri, nz), F32),
        ),
        in_specs=[vmem] * 4,
        out_specs=(any_, any_),
        scratch_shapes=[pltpu.VMEM((ri, nz), F32), dma((2,))],
        name="sweeps",
    )(*[pltpu.with_memory_space_constraint(a, pltpu.VMEM) for a in (con, src, coef, cols)])


def solution(mesh):
    sizes = (mesh.shape["gx"], mesh.shape["pb"])
    in_specs = (
        P("gx", "pb", None),
        P(None, "gx", "pb", None),
        P(None, "gx", "pb", None),
        P("gx", "pb", None),
        P("gx", "pb", None, None),
        P("gx", "pb", None),
        P(("gx", "pb"), None),
        P(("gx", "pb"), None),
        P(("gx", "pb")),
    )
    out_specs = (P(None, "gx", "pb", None), P(("gx", "pb"), None))
    return jax.shard_map(
        functools.partial(body, sizes), mesh=mesh, in_specs=in_specs, out_specs=out_specs,
        check_vma=False)
```

```python
import functools

import jax
import jax.numpy as jnp
from jax import lax
from jax.experimental import pallas as pl
from jax.experimental.pallas import tpu as pltpu
from jax.sharding import PartitionSpec as P

SWEEPS = 8
GAMMA = 5.0 / 3.0
COURANT = 0.08
PAD = 8
COEFS = 15
F32 = jnp.float32
BF16 = jnp.bfloat16
MESH = pl.DeviceIdType.MESH
ORDER = (0, 2, 3, 4, 6, 5, 7, 1)
FIELD = {4: 6, 5: 5, 6: 7}
SPEED = 8
FLUX = {6: 9, 5: 10}


def cell_terms(prim):
    rho, vel, mag, pres = prim[0], prim[1:4], prim[4:7], prim[7]
    field_sq = mag[0] * mag[0] + mag[1] * mag[1] + mag[2] * mag[2]
    vel_sq = vel[0] * vel[0] + vel[1] * vel[1] + vel[2] * vel[2]
    half_sq = 0.5 * field_sq
    energy = pres * (1.0 / (GAMMA - 1.0)) + 0.5 * rho * vel_sq + half_sq
    total_p = pres + half_sq
    v_dot_b = vel[0] * mag[0] + vel[1] * mag[1] + vel[2] * mag[2]
    inv = 1.0 / rho
    sound_sq = GAMMA * pres * inv
    both = sound_sq + field_sq * inv
    momentum = [rho * v for v in vel]
    state = [rho] + momentum + list(mag) + [energy]
    return state, total_p, v_dot_b, sound_sq * inv, both


def flux_of(prim, terms, d):
    state, total_p, v_dot_b = terms[:3]
    vel, mag = prim[1:4], prim[4:7]
    vn, bn = vel[d], mag[d]
    flux = [state[1 + d]]
    for e in range(3):
        m = state[1 + e] * vn - mag[e] * bn
        flux.append(m + total_p if e == d else m)
    for e in range(3):
        flux.append(None if e == d else mag[e] * vn - bn * vel[e])
    flux.append((state[7] + total_p) * vn - bn * v_dot_b)
    return flux


def speed_of(prim, terms, d):
    sound_over, both = terms[3:]
    vn, bn = prim[1 + d], prim[4 + d]
    spread = both * both - 4.0 * sound_over * bn * bn
    fast = jnp.sqrt(0.5 * (both + jnp.sqrt(jnp.maximum(spread, 0.0))))
    return jnp.abs(vn) + fast


def face(f_lo, f_hi, u_lo, u_hi, largest):
    jump = largest * (u_hi - u_lo)
    return -0.5 * jump if f_lo is None else 0.5 * ((f_lo + f_hi) - jump)


def roll(values, shift, axis):
    return pltpu.roll(values, shift % values.shape[axis], axis)


def east(a):
    return roll(a, -1, 1)


def west(a):
    return roll(a, 1, 1)


def up(a):
    return roll(a, 1, 0)


def down(a):
    return roll(a, -1, 0)


def swap_by(cols, a):
    h = a.shape[0] // 2
    other = jnp.concatenate([a[h:], a[:h]], axis=0)
    return jnp.take_along_axis(other, cols, axis=1)


def flux_kernel(sizes, rho, vel, mag, pres, owner, line_row, ped, hall, shift,
                out, src_out, coef_out, cols_out,
                win, fwin, pstage, pin, edge, part, part_in, shared, cwin, own_v, row_v, shift_s,
                loc_sem, xs, xr, ls, lr, ys, yr, ds, dr, ps, pr, cs, cr, as_, ar, hs, hr, far):
    nx, ny = sizes
    cx, cy, nz = rho.shape
    ri = ped.shape[0]
    g, p = lax.axis_index("gx"), lax.axis_index("pb")
    n = nx * ny
    half = n // 2
    pairs = nx // 2
    b = g * ny + p
    wide = cy + 2 * PAD

    def dev(flat):
        return (lax.div(flat, ny), lax.rem(flat, ny))

    beside = {o: dev(lax.rem(b + o + n, n)) for o in (-1, 1)}

    barrier = pltpu.get_barrier_semaphore()

    for dg in (1, -1, 0, 2, -2):
        inside = (g + dg >= 0) & (g + dg < nx)

        @pl.when(inside)
        def _(to=jnp.clip(g + dg, 0, nx - 1), dg=dg):
            for o in (0, 1, -1):
                if (o or dg) and (o == 0 or abs(dg) < 2):
                    pl.semaphore_signal(
                        barrier, inc=1, device_id=(to, beside[o][1] if o else p), device_id_type=MESH)

    at_end = (b == 0) | (b == n - 1)

    @pl.when(at_end)
    def _():
        pl.semaphore_signal(barrier, inc=1, device_id=dev(n - 1 - b), device_id_type=MESH)

    doubling = [1 << i for i in range(1, 32) if 1 << i < nx]

    def pass_on(r):
        for to in (g + r, g - r):
            @pl.when((to >= 0) & (to < nx))
            def _(to=jnp.clip(to, 0, nx - 1), at=doubling.index(r)):
                pl.semaphore_signal(far.at[at], inc=1, device_id=(to, p), device_id_type=MESH)

    def hear(r):
        count = (g + r < nx).astype(jnp.int32) + (g - r >= 0).astype(jnp.int32)
        pl.semaphore_wait(far.at[doubling.index(r)], count)

    rows = pl.ds(PAD, cy)
    mid = pl.ds(1, cx)
    loads = [
        (rho, win.at[0, mid, rows]), (vel, win.at[pl.ds(2, 3), mid, rows]),
        (pres, win.at[1, mid, rows]),
        (ped, cwin.at[1, 0]), (hall, cwin.at[1, 1]), (shift, shift_s),
        (owner, own_v), (line_row, row_v)]
    loads += [(mag.at[v - 4], win.at[FIELD[v], mid, rows]) for v in FIELD]
    loads = [pltpu.make_async_copy(s, d, loc_sem.at[i]) for i, (s, d) in enumerate(loads)]
    for c in loads:
        c.start()
    for c in loads:
        c.wait()

    row8 = lax.broadcasted_iota(jnp.int32, (ri, nz), 0)
    sh = jnp.zeros((ri, nz), F32)
    for i in range(ri):
        sh = jnp.where(row8 == i, shift_s[i].astype(F32), sh)
    cwin[1, 2] = sh

    lane = lax.broadcasted_iota(jnp.int32, (cx, cy, nz), 2)
    first, last = lane == 0, lane == nz - 1

    def z_dn(a):
        return jnp.where(first[:, :a.shape[1]], a, roll(a, 1, 2))

    def z_change(u, f, largest):
        low = face(None if f is None else z_dn(f), f, z_dn(u), u, largest)
        top = jnp.zeros_like(u) if f is None else f
        high = jnp.where(last[:, :u.shape[1]], top, roll(low, -1, 2))
        return high - low

    prim = [win[v, 1:1 + cx, PAD:PAD + cy, :] for v in ORDER]
    terms = cell_terms(prim)
    win[SPEED, 1:1 + cx, PAD:PAD + cy, :] = speed_of(prim, terms, 0)
    for v in FLUX:
        win[FLUX[v], 1:1 + cx, PAD:PAD + cy, :] = prim[v] * prim[1] - prim[4] * prim[v - 3]
    flux, speed = flux_of(prim, terms, 2), speed_of(prim, terms, 2)
    largest = jnp.maximum(speed, z_dn(speed))
    for v in range(8):
        out[v] = terms[0][v] - COURANT * z_change(terms[0][v], flux[v], largest)

    greeted = 3 * (jnp.minimum(g + 1, nx - 1) - jnp.maximum(g - 1, 0) + 1) - 1
    for cond in (g + 2 < nx, g >= 2, at_end):
        greeted = greeted + cond.astype(jnp.int32)
    pl.semaphore_wait(barrier, greeted)
    for r in doubling[:1]:
        pass_on(r)

    def remote(src, dst, send, recv, where):
        return pltpu.make_async_remote_copy(
            src_ref=src, dst_ref=dst, send_sem=send, recv_sem=recv,
            device_id=where, device_id_type=MESH)

    g_up, g_dn = jnp.minimum(g + 1, nx - 1), jnp.maximum(g - 1, 0)
    p_up, p_dn = jnp.minimum(p + 1, ny - 1), jnp.maximum(p - 1, 0)
    has_xu, has_xd, has_yu, has_yd = g < nx - 1, g > 0, p < ny - 1, p > 0

    def each(cond, copies, act):
        @pl.when(cond)
        def _():
            for c in copies:
                getattr(c, act)()

    def x_pair(at, count, send, recv):
        return [
            remote(win.at[pl.ds(at, count), s, rows], win.at[pl.ds(at, count), d, rows],
                   send.at[way], recv.at[way], (where, p))
            for way, (s, d, where) in enumerate(((cx, 0, g_up), (1, cx + 1, g_dn)))]

    xc = x_pair(5, 6, xs, xr)
    xlate = x_pair(0, 5, ls, lr)
    yc = [
        remote(win.at[pl.ds(0, 8), mid, pl.ds(s, PAD)], win.at[pl.ds(0, 8), mid, pl.ds(d, PAD)],
               ys.at[way], yr.at[way], (g, where))
        for way, (s, d, where) in enumerate(((cy, 0, p_up), (PAD, PAD + cy, p_dn)))]
    diag = []
    for i, (xu, yu) in enumerate(((1, 1), (1, 0), (0, 1), (0, 0))):
        s_x, d_x, to_g = (cx, 0, g_up) if xu else (1, cx + 1, g_dn)
        s_y, d_y, to_p = (PAD + cy - 1, PAD - 1, p_up) if yu else (PAD, PAD + cy, p_dn)
        c = remote(win.at[pl.ds(6, 4), s_x, pl.ds(s_y, 1)], win.at[pl.ds(6, 4), d_x, pl.ds(d_y, 1)],
                   ds.at[i], dr.at[i], (to_g, to_p))
        to = (has_xu if xu else has_xd) & (has_yu if yu else has_yd)
        come = (has_xd if xu else has_xu) & (has_yd if yu else has_yu)
        diag.append((c, to, come))
    ion = [
        (lax.rem(b + 1, n), 0),
        (lax.rem(b + n - 1, n), 2),
        (lax.rem(b + half + 1, n), 3),
        (lax.rem(b + half, n), 4),
        (lax.rem(b + half + n - 1, n), 5),
    ]
    cond_copies = [
        remote(cwin.at[1, pl.ds(0, 3 if slot < 3 else 2)], cwin.at[slot, pl.ds(0, 3 if slot < 3 else 2)],
               cs.at[slot], cr.at[slot], dev(flat)) for flat, slot in ion]

    each(has_yu, yc[:1], "start")
    each(has_yd, yc[1:], "start")
    for c, to, _ in diag:
        each(to, [c], "start")
    each(has_xu, xc[:1], "start")
    each(has_xd, xc[1:], "start")

    each(has_yd, yc[:1], "wait_recv")
    each(has_yu, yc[1:], "wait_recv")

    @pl.when(p == 0)
    def _():
        for v in range(8):
            win[v, 1:1 + cx, PAD - 1:PAD, :] = win[v, 1:1 + cx, PAD:PAD + 1, :]

    @pl.when(p == ny - 1)
    def _():
        for v in range(8):
            win[v, 1:1 + cx, PAD + cy:PAD + cy + 1, :] = win[v, 1:1 + cx, PAD + cy - 1:PAD + cy, :]

    def x_inner(values, u, f):
        if cx == 1:
            return values
        speed = win[SPEED, 1:1 + cx, PAD:PAD + cy, :]
        lows = face(None if f is None else f[:-1], None if f is None else f[1:], u[:-1], u[1:],
                    jnp.maximum(speed[:-1], speed[1:]))
        none = jnp.zeros_like(lows[:1])
        return values - COURANT * (jnp.concatenate([lows, none], 0) - jnp.concatenate([none, lows], 0))

    prim = [win[v, 1:1 + cx] for v in ORDER]
    terms = cell_terms(prim)
    flux, speed = flux_of(prim, terms, 1), speed_of(prim, terms, 1)
    largest = jnp.maximum(speed, roll(speed, 1, 1))

    def y_change(v):
        u, f = terms[0][v], flux[v]
        low = face(None if f is None else roll(f, 1, 1), f, roll(u, 1, 1), u, largest)
        return roll(low, -1, 1) - low

    def ends(a):
        return jnp.concatenate([a[:, :PAD], a[:, PAD + cy:]], axis=1)

    side = {}
    for v in (5, 6, 4):
        diff = y_change(v)
        if v != 5:
            side[v] = ends(diff)
        u = win[FIELD[v], 1:1 + cx, PAD:PAD + cy, :]
        f = None if v == 4 else win[FLUX[v], 1:1 + cx, PAD:PAD + cy, :]
        done = x_inner(out[v] - COURANT * diff[:, PAD:PAD + cy, :], u, f)
        if v == 4:
            out[v] = done
        else:
            pstage[v - 5] = done
        if v == 6:
            pc = [
                remote(pstage.at[:, s], pin.at[way], ps.at[way], pr.at[way], (where, p))
                for way, (s, where) in enumerate(((cx - 1, g_up), (0, g_dn)))]
            each(has_xu, pc[:1], "start")
            each(has_xd, pc[1:], "start")
            for at, r in enumerate(doubling[:-1]):
                hear(r)
                pass_on(doubling[at + 1])
    for v in (0, 1, 2, 3, 7):
        out[v] = out[v] - COURANT * y_change(v)[:, PAD:PAD + cy, :]

    for c, _, come in diag:
        each(come, [c], "wait_recv")

    def edge_planes(which, at, count):
        at = pl.ds(at, count)

        @pl.when(g == 0)
        def _():
            for v in which:
                win[v, 0, at, :] = win[v, 1, at, :]

        @pl.when(g == nx - 1)
        def _():
            for v in which:
                win[v, cx + 1, at, :] = win[v, cx, at, :]

    def tiles(v, at):
        return jnp.concatenate([win[v, at, :PAD, :], win[v, at, PAD + cy:, :]], axis=1)

    own = [tiles(v, slice(1, 1 + cx)) for v in ORDER]
    terms = cell_terms(own)
    for v, value in ((SPEED, speed_of(own, terms, 0)), (FLUX[6], own[6] * own[1] - own[4] * own[3])):
        win[v, 1:1 + cx, :PAD, :] = value[:, :PAD]
        win[v, 1:1 + cx, PAD + cy:, :] = value[:, PAD:]
    edge_planes(range(6, 10), 0, PAD)
    edge_planes(range(6, 10), PAD + cy, PAD)
    speed_z = speed_of(own, terms, 2)
    largest_z = jnp.maximum(speed_z, z_dn(speed_z))
    around = slice(0, cx + 2)
    speed_x = tiles(SPEED, around)
    largest_x = jnp.maximum(speed_x[:-1], speed_x[1:])
    for v in (4, 6):
        u = tiles(FIELD[v], around)
        fz = None if v == 6 else own[v] * own[3] - own[6] * own[v - 3]
        fx = None if v == 4 else tiles(FLUX[v], around)
        lows = face(None if fx is None else fx[:-1], None if fx is None else fx[1:], u[:-1], u[1:], largest_x)
        new = own[v] - COURANT * (z_change(own[v], fz, largest_z) + side[v] + (lows[1:] - lows[:-1]))
        fwin[v // 6, :, 0:PAD, :] = new[:, :PAD]
        fwin[v // 6, :, PAD + cy:, :] = new[:, PAD:]

    key = own_v[0] * ri + row_v[...]
    at = lax.broadcasted_iota(jnp.int32, (nx * ri, cx * cy), 0)
    pair, rest = at // (2 * ri), at % (2 * ri)
    hot = (key == (pair + (rest // ri) * pairs) * ri + rest % ri).astype(BF16)
    hot = jnp.concatenate([hot, hot, hot], axis=1)

    for r in doubling[-1:]:
        hear(r)
    for c in cond_copies:
        c.start()
    each(has_xd, xc[:1], "wait_recv")
    each(has_xu, xc[1:], "wait_recv")
    edge_planes(range(5, 11), PAD, cy)

    def outer_faces(v, f_of):
        faces = []
        for lo in (0, cx):
            u = [win[FIELD[v], lo + i, PAD:PAD + cy, :] for i in range(2)]
            f = [f_of(v, lo + i) for i in range(2)]
            most = jnp.maximum(win[SPEED, lo, PAD:PAD + cy, :], win[SPEED, lo + 1, PAD:PAD + cy, :])
            faces.append(COURANT * face(f[0], f[1], u[0], u[1], most))
        return faces

    def b_flux(v, at):
        return None if v == 4 else win[FLUX[v], at, PAD:PAD + cy, :]

    def close(values, faces):
        planes = [values[i] for i in range(cx)]
        planes[0] = planes[0] + faces[0]
        planes[-1] = planes[-1] - faces[1]
        return planes

    field, outer = {}, {}
    for v in (4, 6, 5):
        outer[v] = outer_faces(v, b_flux)
        field[v] = close(out[v] if v == 4 else pstage[v - 5], outer[v])
        for i in range(cx):
            out[v, i] = field[v][i]
            if v != 5:
                fwin[v // 6, i, PAD:PAD + cy, :] = field[v][i]

    @pl.when(p == 0)
    def _():
        fwin[:, :, PAD - 1:PAD, :] = fwin[:, :, PAD:PAD + 1, :]

    @pl.when(p == ny - 1)
    def _():
        fwin[:, :, PAD + cy:PAD + cy + 1, :] = fwin[:, :, PAD + cy - 1:PAD + cy, :]

    def d_y(v):
        a = fwin[v // 6]
        return 0.5 * (roll(a, -1, 1) - roll(a, 1, 1))[:, PAD:PAD + cy, :]

    def d_z(a):
        return 0.5 * (jnp.where(last, a, roll(a, -1, 2)) - z_dn(a))

    bx, by, bz = [jnp.stack(field[v]) for v in (4, 5, 6)]
    jx = d_y(6) - d_z(by)
    size = jnp.sqrt(bx * bx + by * by + bz * bz)
    dzx, dyx = d_z(bx), d_y(4)

    each(has_xd, pc[:1], "wait_recv")
    each(has_xu, pc[1:], "wait_recv")

    def d_x(v):
        lo = jnp.where(g == 0, field[v][0], pin[0, v - 5] - outer[v][0])
        hi = jnp.where(g == nx - 1, field[v][-1], pin[1, v - 5] + outer[v][1])
        a = jnp.stack([lo] + field[v] + [hi])
        return 0.5 * (a[2:] - a[:-2])

    jy = dzx - d_x(6)
    jz = d_x(5) - dyx
    current = (jx * bx + jy * by + jz * bz) / jnp.maximum(size, 1.0)
    current = current.reshape(cx * cy, nz)

    head = current.astype(BF16)
    tail = current - head.astype(F32)
    body_ = tail.astype(BF16)
    tail = (tail - body_.astype(F32)).astype(BF16)
    sums = jnp.dot(hot, jnp.concatenate([head, body_, tail], axis=0),
                   preferred_element_type=F32)
    part[...] = sums.reshape(pairs, 2, ri, nz)

    odd = lax.rem(p, 2)
    mate = (g, p + 1 - 2 * odd)
    out_g, out_p = jnp.where(odd == 1, beside[1][0], beside[-1][0]), jnp.where(odd == 1, beside[1][1], beside[-1][1])
    step = lax.rem(out_g - g + nx, nx)

    def own_copy(to):
        return remote(part.at[lax.rem(to, pairs)], part_in.at[0, g], as_.at[0], ar.at[0], (to, p))

    def outer_copy(to, first_row):
        some = pl.ds(first_row, ri - 1)
        return remote(part.at[lax.rem(to, pairs), :, some], part_in.at[1, g, :, some], as_.at[1], ar.at[1],
                      (lax.rem(to + step, nx), out_p))

    def send_own(k, carry):
        own_copy(lax.rem(g + k, nx)).start()
        return carry

    def send_outer(first_row):
        def send(k, carry):
            outer_copy(lax.rem(g + k, nx), first_row).start()
            return carry

        lax.fori_loop(0, nx, send, 0, unroll=nx <= 8)

    lax.fori_loop(1, nx, send_own, 0, unroll=nx <= 8)
    pl.when(odd == 1)(lambda: send_outer(1))
    pl.when(odd == 0)(lambda: send_outer(0))

    for c in cond_copies:
        c.wait_recv()
    each(has_xu, xlate[:1], "start")
    each(has_xd, xlate[1:], "start")
    lines = 6 * ri
    row = lax.broadcasted_iota(jnp.int32, (lines, nz), 0)
    row = jnp.where(row >= 3 * ri, row - 3 * ri, row)
    place = lax.rem(b, half)
    low_row = jnp.where(place == half // 2, ri, 0)
    high_row = jnp.where(place == half // 2 - 1, 2 * ri, 3 * ri)
    valid = (row >= low_row) & (row < high_row)
    pw = jnp.where(valid, cwin[:, 0].reshape(lines, nz), 0.0)
    hw = jnp.where(valid, cwin[:, 1].reshape(lines, nz), 0.0)
    own_shift = cwin[0:3, 2].reshape(3 * ri, nz).astype(jnp.int32)
    col = lax.broadcasted_iota(jnp.int32, (3 * ri, nz), 1)
    cols = jnp.concatenate(
        [(col + own_shift) % nz, (col + (nz - own_shift)) % nz], axis=0)
    he, hwst = east(hw), west(hw)
    coef = [
        0.5 * (pw + up(pw)), 0.5 * (pw + down(pw)),
        0.5 * (pw + east(pw)), 0.5 * (pw + west(pw)),
        0.125 * (hw + up(he)), 0.125 * (hw + up(hwst)),
        0.125 * (hw + down(he)), 0.125 * (hw + down(hwst)),
    ]
    center = coef[0]
    for c in coef[1:]:
        center = center + c
    inv = jnp.where(valid, 1.0 / jnp.where(valid, center, 1.0), 0.0)
    pm = swap_by(cols, pw)
    both = jnp.where(valid, pw + pm, 1.0)
    c_up, c_down, c_east, c_west, c_ue, c_uw, c_de, c_dw = [c * inv for c in coef]
    wa, wb = jnp.where(valid, pw / both, 0.0), jnp.where(valid, pm / both, 0.0)
    for i, c in enumerate((
            inv, c_east, c_west, down(c_up), down(c_ue), -down(c_uw), up(c_down), -up(c_de), up(c_dw),
            wa, wb, east(wa), east(wb), west(wa), west(wb))):
        coef_out[i] = c
    for i, c in enumerate((cols, east(cols), west(cols))):
        cols_out[i] = c

    rest = (0, 1, 2, 3, 7)
    prim = [win[v, 1:1 + cx, PAD:PAD + cy, :] for v in ORDER]
    terms = cell_terms(prim)
    flux = flux_of(prim, terms, 0)
    for at, v in enumerate(rest):
        out[v] = x_inner(out[v], terms[0][v], flux[v])
        for side_at, plane in enumerate((0, cx - 1)):
            edge[0, at, side_at] = terms[0][v][plane]
            edge[1, at, side_at] = flux[v][plane]

    each(has_xu, [xc[0], pc[0]], "wait_send")
    each(has_xd, [xc[1], pc[1]], "wait_send")
    each(has_yu, yc[:1], "wait_send")
    each(has_yd, yc[1:], "wait_send")
    for c, to, _ in diag:
        each(to, [c], "wait_send")
    for c in cond_copies:
        c.wait_send()
    def taken(slot, sems):
        some = part_in.at[slot, pl.ds(0, nx - 1 if slot == 0 else nx), :, pl.ds(0, ri if slot == 0 else ri - 1)]
        pltpu.make_async_copy(some, some, sems.at[slot]).wait()

    def total_of(slot):
        def add(at, total):
            return total + part_in[slot, at]
        return lax.fori_loop(1, nx, add, part_in[slot, 0], unroll=nx <= 8)

    taken(0, ar)
    part_in[0, g] = part[lax.rem(g, pairs)]
    shared[0] = total_of(0)
    to_mate = remote(shared.at[0], shared.at[1], hs.at[0], hr.at[0], mate)
    to_mate.start()
    each(has_xd, xlate[:1], "wait_recv")
    each(has_xu, xlate[1:], "wait_recv")

    def ghosts(v):
        return jnp.stack([win[v, at, PAD:PAD + cy, :] for at in (0, cx + 1)])

    prim = [ghosts(v) for v in ORDER]
    terms = cell_terms(prim)
    flux = flux_of(prim, terms, 0)
    speed = jnp.maximum(ghosts(SPEED), jnp.stack([win[SPEED, at, PAD:PAD + cy, :] for at in (1, cx)]))
    for at, v in enumerate(rest):
        u, f = terms[0][v], flux[v]
        own_u, own_f = edge[0, at], edge[1, at]
        low = face(f[0], own_f[0], u[0], own_u[0], speed[0])
        high = face(own_f[1], f[1], own_u[1], u[1], speed[1])
        low = jnp.where(g == 0, own_f[0], low)
        high = jnp.where(g == nx - 1, own_f[1], high)
        out[v, 0] = out[v, 0] + COURANT * low
        out[v, cx - 1] = out[v, cx - 1] - COURANT * high

    each(has_xu, xlate[:1], "wait_send")
    each(has_xd, xlate[1:], "wait_send")
    taken(0, as_)
    taken(1, as_)
    taken(1, ar)
    outer_sum = total_of(1)
    to_mate.wait_recv()

    def place_sums(slot, total, block):
        northern = block < half
        src_out[0, slot] = jnp.where(northern, total[0], total[1])
        src_out[1, slot] = jnp.where(northern, total[1], total[0])

    mate_sum = shared[1]
    place_sums(0, jnp.where(odd == 1, mate_sum, outer_sum), lax.rem(b + n - 1, n))
    place_sums(1, shared[0], b)
    place_sums(2, jnp.where(odd == 1, outer_sum, mate_sum), lax.rem(b + 1, n))

    to_mate.wait_send()


def sweep_kernel(con, src, coef, cols_ref, out, phi_out, phi_v, sems):
    write = pltpu.make_async_copy(con, out, sems.at[0])
    write.start()
    inv, ce, cw, u0, u1, u2, d0, d1, d2, wa, wb, wae, wbe, waw, wbw = [coef[i] for i in range(COEFS)]
    cols, colse, colsw = [cols_ref[i] for i in range(3)]
    ri = phi_v.shape[0]
    source = src[...].reshape(inv.shape) * inv

    def triple(a):
        h = a.shape[0] // 2
        other = jnp.concatenate([a[h:], a[:h]], axis=0)
        take = lambda c: jnp.take_along_axis(other, c, axis=1)
        return wa * a + wb * take(cols), wae * east(a) + wbe * take(colse), waw * west(a) + wbw * take(colsw)

    acc = source
    for _ in range(SWEEPS - 1):
        phi, e, w = triple(acc)
        acc = (source + (ce * e + cw * w)) + (up(u0 * phi + u1 * e + u2 * w) + down(d0 * phi + d1 * e + d2 * w))
    phi = wa * acc + wb * swap_by(cols, acc)
    phi_v[...] = phi[ri:2 * ri]
    last = pltpu.make_async_copy(phi_v, phi_out, sems.at[1])
    last.start()
    write.wait()
    last.wait()


def body(sizes, density, velocity, magnetic, pressure, line_owner, line_row, pedersen, hall, mirror_shift):
    cx, cy, nz = density.shape
    ri = pedersen.shape[0]
    nx = sizes[0]
    any_ = pl.BlockSpec(memory_space=pl.ANY)
    vmem = pl.BlockSpec(memory_space=pltpu.VMEM)
    dma = pltpu.SemaphoreType.DMA
    con, src, coef, cols = pl.pallas_call(
        functools.partial(flux_kernel, sizes),
        out_shape=(
            pltpu.VMEM((8, cx, cy, nz), F32),
            pltpu.VMEM((2, 3, ri, nz), F32),
            pltpu.VMEM((COEFS, 6 * ri, nz), F32),
            pltpu.VMEM((3, 6 * ri, nz), jnp.int32),
        ),
        in_specs=[any_] * 9,
        out_specs=(vmem,) * 4,
        scratch_shapes=[
            pltpu.VMEM((11, cx + 2, cy + 2 * PAD, nz), F32),
            pltpu.VMEM((2, cx, cy + 2 * PAD, nz), F32),
            pltpu.VMEM((2, cx, cy, nz), F32),
            pltpu.VMEM((2, 2, cy, nz), F32),
            pltpu.VMEM((2, 5, 2, cy, nz), F32),
            pltpu.VMEM((nx // 2, 2, ri, nz), F32),
            pltpu.VMEM((2, nx, 2, ri, nz), F32),
            pltpu.VMEM((2, 2, ri, nz), F32),
            pltpu.VMEM((6, 3, ri, nz), F32),
            pltpu.VMEM((1, 1, cx * cy), jnp.int32),
            pltpu.VMEM((1, cx * cy), jnp.int32),
            pltpu.SMEM((ri,), jnp.int32),
            dma((11,)),
            dma((2,)), dma((2,)), dma((2,)), dma((2,)), dma((2,)), dma((2,)),
            dma((4,)), dma((4,)), dma((2,)), dma((2,)), dma((6,)), dma((6,)),
            dma((2,)), dma((2,)), dma((1,)), dma((1,)),
            pltpu.SemaphoreType.REGULAR((8,)),
        ],
        compiler_params=pltpu.CompilerParams(collective_id=0, has_side_effects=True),
        name="flux_and_sources",
    )(density, velocity, magnetic, pressure, line_owner.reshape(1, 1, cx * cy), line_row.reshape(1, cx * cy),
      pedersen, hall, mirror_shift)
    return pl.pallas_call(
        sweep_kernel,
        out_shape=(
            jax.ShapeDtypeStruct((8, cx, cy, nz), F32),
            jax.ShapeDtypeStruct((ri, nz), F32),
        ),
        in_specs=[vmem] * 4,
        out_specs=(any_, any_),
        scratch_shapes=[pltpu.VMEM((ri, nz), F32), dma((2,))],
        name="sweeps",
    )(*[pltpu.with_memory_space_constraint(a, pltpu.VMEM) for a in (con, src, coef, cols)])


def solution(mesh):
    sizes = (mesh.shape["gx"], mesh.shape["pb"])
    in_specs = (
        P("gx", "pb", None),
        P(None, "gx", "pb", None),
        P(None, "gx", "pb", None),
        P("gx", "pb", None),
        P("gx", "pb", None, None),
        P("gx", "pb", None),
        P(("gx", "pb"), None),
        P(("gx", "pb"), None),
        P(("gx", "pb")),
    )
    out_specs = (P(None, "gx", "pb", None), P(("gx", "pb"), None))
    return jax.shard_map(
        functools.partial(body, sizes), mesh=mesh, in_specs=in_specs, out_specs=out_specs,
        check_vma=False)
```
